32 devices in a mesh: clips: 2 (over y), seq: 4 (over z), tp: 2 (over x), dp: 2 (over core).
Axes of the slice: x: 2, y: 2, z: 4, core: 2. Of those that a mesh axis runs over, the one named last changes fastest.
Arguments:
- video_query: bfloat16 [4, 512, 4096], P(('clips', 'dp'), 'seq', 'tp'), parts along dimension 0, may hold values from -384 to 384
- video_key: bfloat16 [4, 512, 4096], P(('clips', 'dp'), 'seq', 'tp'), parts along dimension 0, may hold values from -384 to 384
- video_value: bfloat16 [4, 512, 4096], P(('clips', 'dp'), 'seq', 'tp'), parts along dimension 0, may hold values from -6 to 6
- cross_query: bfloat16 [4, 512, 2048], P(('clips', 'dp'), 'seq', 'tp'), parts along dimension 0, may hold values from -384 to 384
- audio_key: bfloat16 [4, 32, 2048], P(('clips', 'dp'), 'seq', 'tp'), parts along dimension 0, may hold values from -384 to 384
- audio_value: bfloat16 [4, 32, 2048], P(('clips', 'dp'), 'seq', 'tp'), parts along dimension 0, may hold values from -6 to 6
- audio_query: bfloat16 [4, 32, 2048], P(('clips', 'dp'), 'seq', 'tp'), parts along dimension 0, may hold values from -384 to 384
- cross_key: bfloat16 [4, 512, 2048], P(('clips', 'dp'), 'seq', 'tp'), parts along dimension 0, may hold values from -384 to 384
- cross_value: bfloat16 [4, 512, 2048], P(('clips', 'dp'), 'seq', 'tp'), parts along dimension 0, may hold values from -6 to 6
- audio_input: bfloat16 [4, 32, 2048], P(('clips', 'dp'), 'seq'), parts along dimension 0, may hold values from -0.29882812 to 0.29882812
- norm_gain: float32 [2048], replicated, may hold values from 0.1 to 1.9
- up_weight: bfloat16 [2048, 8192], P('tp', 'seq'), may hold values from -0.125 to 0.125
- down_weight: bfloat16 [8192, 2048], P('seq', 'tp'), may hold values from -0.0625 to 0.0625
Outputs:
- video_mixed: bfloat16 [4, 512, 4096], P(('clips', 'dp'), 'seq', 'tp'), parts along dimension 0
- video_heard: bfloat16 [4, 512, 2048], P(('clips', 'dp'), 'seq', 'tp'), parts along dimension 0
- audio_seen: bfloat16 [4, 32, 2048], P(('clips', 'dp'), 'seq', 'tp'), parts along dimension 0
- audio_mlp: bfloat16 [4, 32, 2048], P(('clips', 'dp'), 'seq', 'tp'), parts along dimension 0
The draws below stay inside these ranges and needn't reach their ends.
There are 2 independent parts, one for each index of `clips`. The reference program is written for one: setup_inputs(seed, part) draws one part's arguments, and reference() takes and returns one part's arrays. A program takes and returns all parts, laid end to end along the dimension named above; an argument that names none is the same for every part. Nothing has to cross between parts.
All inputs are finite; a program needn't handle non-finite values.
Results may differ from the reference program's by a relative error of at most 0.013.
Values may be sent and summed in bfloat16 or wider, within the bound.
A program may use at most 64 MiB of HBM per device.

```python
import math
import jax
import jax.numpy as jnp
from jax import lax

VHEADS = 32
VHEAD = 128
CHEADS = 32
CHEAD = 64
FFA = 8192
BATCH = 2
VWIDTH = 4096
AUDIO_D = 2048
VIDEO_LEN = 512
AUDIO_LEN = 32


def make_pair(base_key, query_rows, key_rows, head_count, head_size):
    key_query, key_keys = jax.random.split(base_key, 2)
    queries = jnp.clip(jax.random.normal(key_query, (BATCH, query_rows, head_count, head_size), jnp.float32), -4.0, 4.0)
    keys_out = 2.0 * jnp.clip(jax.random.normal(key_keys, (BATCH, key_rows, head_count, head_size), jnp.float32), -4.0, 4.0)
    return (queries.reshape(BATCH, query_rows, head_count * head_size), keys_out.reshape(BATCH, key_rows, head_count * head_size))


def draw_video_query(key, part):
    return make_pair(jax.random.fold_in(key, 11), VIDEO_LEN, VIDEO_LEN, VHEADS, VHEAD)[0].astype(jnp.bfloat16)


def draw_video_key(key, part):
    return make_pair(jax.random.fold_in(key, 11), VIDEO_LEN, VIDEO_LEN, VHEADS, VHEAD)[1].astype(jnp.bfloat16)


def draw_cross_query(key, part):
    return make_pair(jax.random.fold_in(key, 12), VIDEO_LEN, AUDIO_LEN, CHEADS, CHEAD)[0].astype(jnp.bfloat16)


def draw_audio_key(key, part):
    return make_pair(jax.random.fold_in(key, 12), VIDEO_LEN, AUDIO_LEN, CHEADS, CHEAD)[1].astype(jnp.bfloat16)


def draw_audio_query(key, part):
    return make_pair(jax.random.fold_in(key, 13), AUDIO_LEN, VIDEO_LEN, CHEADS, CHEAD)[0].astype(jnp.bfloat16)


def draw_cross_key(key, part):
    return make_pair(jax.random.fold_in(key, 13), AUDIO_LEN, VIDEO_LEN, CHEADS, CHEAD)[1].astype(jnp.bfloat16)


def steps_of(key, shape, shards, least, largest):
    factor_of = 1.0
    for axis_at, shards_of in shards:
        steps = jax.random.uniform(jax.random.fold_in(jax.random.fold_in(key, 6), axis_at), (shards_of,), jnp.float32, least / len(shards), largest / len(shards))
        factor_of = factor_of * jnp.repeat(jnp.exp(steps), shape[axis_at] // shards_of).reshape((-1,) + (1,) * (len(shape) - 1 - axis_at))
    return factor_of


def bell_draw(rng, shape, spread, limit, shards=(), kind=jnp.bfloat16):
    factor_of = steps_of(rng, shape, shards, -0.22, 0.18) if shards else 1.0
    values = jax.random.normal(rng, shape, jnp.float32) * spread * factor_of
    return jnp.minimum(jnp.maximum(values, -limit), limit).astype(kind)


def setup_inputs(seed: int = 0, part: int = 0) -> dict:
    arg_keys = jax.random.split(jax.random.key(seed), 14)
    part_splits = jax.random.split(jax.random.fold_in(arg_keys[13], part), 14)
    video_query = draw_video_query(jax.random.fold_in(jax.random.fold_in(arg_keys[13], part), 71), part)
    video_key = draw_video_key(jax.random.fold_in(jax.random.fold_in(arg_keys[13], part), 71), part)
    video_value = bell_draw(part_splits[2], (BATCH, VIDEO_LEN, VWIDTH), 1.0, 6.0, ((0, 2), (1, 4), (2, 2)))
    cross_query = draw_cross_query(jax.random.fold_in(jax.random.fold_in(arg_keys[13], part), 71), part)
    audio_key = draw_audio_key(jax.random.fold_in(jax.random.fold_in(arg_keys[13], part), 71), part)
    audio_value = bell_draw(part_splits[5], (BATCH, AUDIO_LEN, AUDIO_D), 1.0, 6.0, ((0, 2), (1, 4), (2, 2)))
    audio_query = draw_audio_query(jax.random.fold_in(jax.random.fold_in(arg_keys[13], part), 71), part)
    cross_key = draw_cross_key(jax.random.fold_in(jax.random.fold_in(arg_keys[13], part), 71), part)
    cross_value = bell_draw(part_splits[8], (BATCH, VIDEO_LEN, AUDIO_D), 1.0, 6.0, ((0, 2), (1, 4), (2, 2)))
    audio_input = jnp.clip(jax.random.uniform(part_splits[9], (BATCH, AUDIO_LEN, AUDIO_D), jnp.float32, -0.29882812, 0.29882812) * steps_of(part_splits[9], (BATCH, AUDIO_LEN, AUDIO_D), ((0, 2), (1, 4)), -0.4, 0.0), -0.29882812, 0.29882812).astype(jnp.bfloat16)
    norm_gain = jnp.clip(1.0 + 0.18 * jax.random.normal(arg_keys[10], (AUDIO_D,), jnp.float32), 0.1, 1.9)
    up_weight = bell_draw(arg_keys[11], (AUDIO_D, FFA), AUDIO_D ** -0.5, 0.125, ((0, 2), (1, 4)))
    down_weight = bell_draw(arg_keys[12], (FFA, AUDIO_D), FFA ** -0.5, 0.0625, ((0, 4), (1, 2)))
    return dict(video_query=video_query, video_key=video_key, video_value=video_value, cross_query=cross_query, audio_key=audio_key, audio_value=audio_value, audio_query=audio_query, cross_key=cross_key, cross_value=cross_value, audio_input=audio_input, norm_gain=norm_gain, up_weight=up_weight, down_weight=down_weight)


def attend_rows(queries, keys_in, values_in, head_count):
    head_size = queries.shape[1] // head_count
    query_heads = queries.reshape(queries.shape[0], head_count, head_size).astype(jnp.float32)
    key_heads = keys_in.reshape(keys_in.shape[0], head_count, head_size).astype(jnp.float32)
    value_heads = values_in.reshape(values_in.shape[0], head_count, head_size).astype(jnp.float32)
    scores = jnp.einsum('qhd,khd->qhk', query_heads, key_heads) / math.sqrt(head_size)
    peak_value = lax.optimization_barrier(jnp.max(scores, axis=2, keepdims=True))
    weights = jnp.exp(scores - peak_value)
    totals = lax.optimization_barrier(jnp.sum(weights, axis=2))
    rounded = lax.optimization_barrier(weights.astype(jnp.bfloat16)).astype(jnp.float32)
    weighted = jnp.einsum('qhk,khd->qhd', rounded, value_heads)
    result = weighted / totals[:, :, None]
    return result.reshape(queries.shape[0], head_count * head_size).astype(jnp.bfloat16)

def attend(queries, keys_in, values_in, head_count):
    row_total = queries.shape[0]
    block_rows = 512 if row_total % 512 == 0 else row_total
    pieces = queries.reshape(row_total // block_rows, block_rows, queries.shape[1])
    result = lax.map(lambda row_piece: attend_rows(row_piece, keys_in, values_in, head_count), pieces)
    return result.reshape(row_total, queries.shape[1])

def reference(video_query, video_key, video_value, cross_query, audio_key, audio_value, audio_query, cross_key, cross_value, audio_input, norm_gain, up_weight, down_weight):
    mixed_list, heard_list, seen_list, output_list = ([], [], [], [])
    for sample in range(BATCH):
        mixed_list.append(attend(video_query[sample], video_key[sample], video_value[sample], VHEADS))
        heard_list.append(attend(cross_query[sample], audio_key[sample], audio_value[sample], CHEADS))
        audio_seen = attend(audio_query[sample], cross_key[sample], cross_value[sample], CHEADS)
        seen_list.append(audio_seen)
        residual = audio_input[sample].astype(jnp.float32) + audio_seen.astype(jnp.float32)
        scale_factor = lax.rsqrt(lax.optimization_barrier(jnp.mean(residual * residual, axis=1, keepdims=True)) + 1e-06)
        normed = (residual * scale_factor * norm_gain.astype(jnp.float32)).astype(jnp.bfloat16)
        hidden = jax.nn.gelu(jnp.dot(normed, up_weight, preferred_element_type=jnp.float32)).astype(jnp.bfloat16)
        output_list.append(jnp.dot(hidden, down_weight, preferred_element_type=jnp.float32).astype(jnp.bfloat16))
    return (jnp.stack(mixed_list), jnp.stack(heard_list), jnp.stack(seen_list), jnp.stack(output_list))
```

```python
import functools
import math

import jax
import jax.numpy as jnp
from jax import lax
from jax.experimental import pallas as pl
from jax.experimental.pallas import tpu as pltpu
from jax.sharding import PartitionSpec as P

VHEAD = 128
CHEAD = 64
MESH = pl.DeviceIdType.MESH
LOG2E = math.log2(math.e)
CHUNKS = 4
PACE = (2, 2, 2, 2, 2, 2, 0, 0)


def dot_t(a, b):
    return lax.dot_general(a, b, (((1,), (1,)), ((), ())), preferred_element_type=jnp.float32)


def softmax_parts(q, k, scale):
    s = dot_t(q, k)
    peak = jnp.max(s, axis=1, keepdims=True)
    p = jnp.exp2((s - peak) * (scale * LOG2E))
    return p, peak * scale, jnp.sum(p, axis=1, keepdims=True)


def pair_attend(q, k, v, scale):
    low = lax.broadcasted_iota(jnp.int32, q.shape, 1) < CHEAD
    zero = jnp.zeros_like(q)
    both = jnp.concatenate([jnp.where(low, q, zero), jnp.where(low, zero, q)], axis=0)
    p, peak, total = softmax_parts(both, k, scale)
    o = jnp.dot(p.astype(jnp.bfloat16), v, preferred_element_type=jnp.float32)
    return o, peak, total


def partners(me, n):
    if n & (n - 1):
        return [lax.rem(me + d, n) for d in range(1, n)]
    found = []
    for flip in range(n - 1, 0, -1):
        place, bit = me * 0, 1
        while bit < n:
            digit = lax.rem(lax.div(me, bit), 2)
            place = place + bit * ((1 - digit) if flip & bit else digit)
            bit *= 2
        found.append(place)
    return found


def fused_kernel(
    n, tp,
    vq, vk, vv, cq, ak, av, aq, ck, cv, ai, gain, up, down,
    mixed, heard, seen, mlp,
    qbuf, kbuf, vbuf, obuf, abuf, cqv, ckv, cvv, upv, downv, aiv, gainv, xown, xsend, xrecv, tsend, trecv, ssbuf, nbuf, pbuf, ubuf, racc, rsend, rrecv,
    v_send, v_recv, o_send, o_recv, a_send, a_recv, x_send, x_recv, t_send, t_recv, s_send, s_recv,
    n_send, n_recv, p_send, p_recv, r_send, r_recv, own_sem, oown_sem, load_sem,
):
    me = lax.axis_index("seq")
    col = lax.axis_index("tp")
    tokens = vq.shape[0]
    hd = vq.shape[1] // VHEAD // n
    rows, width = aq.shape
    pairs = width // 128
    units = up.shape[1]
    step = units // CHUNKS
    f32, bf16 = jnp.float32, jnp.bfloat16
    peers = partners(me, n)
    tp_peers = [lax.rem(col + d, tp) for d in range(1, tp)]

    def remote(src, dst, ss, rs, where):
        copy = pltpu.make_async_remote_copy(
            src_ref=src, dst_ref=dst, send_sem=ss, recv_sem=rs, device_id=where, device_id_type=MESH
        )
        copy.start()
        return copy

    barrier = pltpu.get_barrier_semaphore()
    for p in peers:
        pl.semaphore_signal(barrier, inc=1, device_id={"seq": p}, device_id_type=MESH)
    for t in tp_peers:
        pl.semaphore_signal(barrier, inc=1, device_id={"tp": t}, device_id_type=MESH)

    loads = []
    stays = ((ck, ckv), (cv, cvv), (cq, cqv), (up, upv), (down, downv), (ai, aiv), (gain, gainv))
    stays += tuple((src, abuf.at[i, me]) for i, src in enumerate((aq, ak, av)))
    for i, (src, dst) in enumerate(stays):
        loads.append(pltpu.make_async_copy(src, dst, load_sem.at[i]))
        loads[-1].start()
    owns = []
    for h in range(hd):
        cols = pl.ds(pl.multiple_of((me * hd + h) * VHEAD, VHEAD), VHEAD)
        owns.append([])
        for i, (src, buf) in enumerate(((vq, qbuf), (vk, kbuf), (vv, vbuf))):
            copy = pltpu.make_async_copy(src.at[:, cols], buf.at[h, me], own_sem.at[h, i])
            copy.start()
            owns[-1].append(copy)

    pl.semaphore_wait(barrier, n - 1 + tp - 1)

    sent = []
    order = (2, 0, 1) if n == 4 else tuple(range(n - 1))
    back = (1, 0, 2) if n == 4 else tuple(range(n - 1))
    units = [(h, i) for h in range(hd) for i in (1, 2, 0)]
    video = [[] for _ in range(hd)]

    def pump(count):
        for h, i in units[:count]:
            src, buf = ((vq, qbuf), (vk, kbuf), (vv, vbuf))[i]
            for d in order:
                p = peers[d]
                cols = pl.ds(pl.multiple_of((p * hd + h) * VHEAD, VHEAD), VHEAD)
                video[h].append(
                    remote(src.at[:, cols], buf.at[h, me], v_send.at[h, d, i], v_recv.at[h, d, i], {"seq": p})
                )
            sent.extend(video[h][1 - n :])
        del units[:count]

    def attend_video(h, copies):
        for copy in owns[h]:
            copy.wait()
        for copy in copies:
            copy.wait_recv()
        k = kbuf[h].reshape(n * tokens, VHEAD)
        v = vbuf[h].reshape(n * tokens, VHEAD)
        cols = pl.ds(pl.multiple_of((me * hd + h) * VHEAD, VHEAD), VHEAD)
        out = []
        for d in back + (n - 1,):
            p = (peers + [me])[d]
            w, _, total = softmax_parts(qbuf[h, p], k, 1.0 / math.sqrt(VHEAD))
            o = jnp.dot(w.astype(bf16), v, preferred_element_type=f32) / total
            obuf[h, p] = o.astype(bf16)
            if d < n - 1:
                out.append(remote(obuf.at[h, p], mixed.at[:, cols], o_send.at[h, d], o_recv.at[h, d], {"seq": p}))
        own = pltpu.make_async_copy(obuf.at[h, me], mixed.at[:, cols], oown_sem.at[h])
        own.start()
        return out, own

    far, over, side = peers

    def spread(src, slots, ss, rs):
        copies = [remote(src, slots.at[me], ss.at[d], rs.at[d], {"seq": peers[d]}) for d in (2, 1)]
        sent.extend(copies)
        return copies

    def hand_on(copies, slots, ss, rs):
        copies[1].wait_recv()
        copy = remote(slots.at[over], slots.at[over], ss.at[0], rs.at[0], {"seq": side})
        sent.append(copy)
        return [copies[0], copy]

    asked = spread(aq, abuf.at[0], a_send.at[0], a_recv.at[0])
    pump(PACE[0])
    asked = hand_on(asked, abuf.at[0], a_send.at[0], a_recv.at[0])
    pump(PACE[1])

    for copy in loads[:2] + loads[5:]:
        copy.wait()
    for copy in asked:
        copy.wait_recv()

    def whole(i):
        return jnp.concatenate([abuf[i, s].astype(f32) for s in range(n)], axis=0).astype(bf16)

    scale = 1.0 / math.sqrt(CHEAD)
    total_rows = n * rows
    q_all = whole(0)
    lane = lax.broadcasted_iota(jnp.int32, (total_rows, 128), 1)
    stats = jnp.ones((total_rows, 128), f32)
    for j in range(pairs):
        at = slice(j * 128, (j + 1) * 128)
        o, peak, total = pair_attend(q_all[:, at], ckv[:, at], cvv[:, at], scale)
        picked = jnp.where(lane < CHEAD, o[:total_rows], o[total_rows:])
        xown[:, :, at] = picked.reshape(n, rows, 128)
        for half in range(2):
            part = slice(half * total_rows, (half + 1) * total_rows)
            stats = jnp.where(lane == 2 * j + half, peak[part], stats)
            stats = jnp.where(lane == 64 + 2 * j + half, total[part], stats)
    tsend[...] = stats.reshape(n, rows, 128)

    def send_part(d, slot, k):
        p = peers[d]
        copies = [
            remote(tsend.at[slot], trecv.at[k], t_send.at[k], t_recv.at[k], {"seq": p}),
            remote(xsend.at[k], xrecv.at[k], x_send.at[k], x_recv.at[k], {"seq": p}),
        ]
        sent.extend(copies)
        return copies

    xsend[0] = xown[far].astype(bf16)
    crossing = send_part(2, far, 0)
    xsend[1] = xown[side].astype(bf16)
    near = send_part(2, side, 1)
    place = lax.broadcasted_iota(jnp.int32, (rows, 128), 1)

    def weigh(stats):
        peak = functools.reduce(jnp.maximum, stats)
        factors = [jnp.exp(t - peak) for t in stats]
        return peak, factors, sum(f * pltpu.roll(t, 64, 1) for f, t in zip(factors, stats))

    def blend(factors, blocks):
        pieces = []
        for j in range(pairs):
            at = slice(j * 128, (j + 1) * 128)
            terms = [
                jnp.where(place < CHEAD, f[:, 2 * j : 2 * j + 1], f[:, 2 * j + 1 : 2 * j + 2]) * b[:, at].astype(f32)
                for f, b in zip(factors, blocks)
            ]
            pieces.append(sum(terms[1:], terms[0]))
        return jnp.concatenate(pieces, axis=1).astype(bf16)

    pump(PACE[2])

    for copy in crossing:
        copy.wait_recv()
    peak, factors, total = weigh([tsend[over], trecv[0]])
    xsend[2] = blend(factors, [xown[over], xrecv[0]])
    tsend[over] = jnp.where(place < 64, peak, pltpu.roll(total, 64, 1))
    joined = send_part(1, over, 2)
    audio = [None, None]

    def send_audio():
        for i, src in enumerate((ak, av)):
            audio[i] = spread(src, abuf.at[i + 1], a_send.at[i + 1], a_recv.at[i + 1])

    def pass_audio():
        for i in range(2):
            audio[i] = hand_on(audio[i], abuf.at[i + 1], a_send.at[i + 1], a_recv.at[i + 1])

    pump(PACE[3])

    for copy in near + joined:
        copy.wait_recv()
    _, factors, total = weigh([tsend[me], trecv[1], trecv[2]])
    seen_bf = blend([f / total for f in factors], [xown[me], xrecv[1], xrecv[2]])
    seen[...] = seen_bf

    mine = pl.ds(pl.multiple_of(col * width, 128), width)
    residual = aiv[:, mine].astype(f32) + seen_bf.astype(f32)
    square = jnp.sum(residual * residual, axis=1, keepdims=True)
    first = square.astype(bf16).astype(f32)
    second = (square - first).astype(bf16).astype(f32)
    third = square - first - second
    split = jnp.where(place == 0, first, jnp.where(place == 1, second, jnp.where(place == 2, third, 0.0)))
    nbuf[me, :, :width] = (residual * gainv[:, mine]).astype(bf16)
    nbuf[me, :, width:] = split.astype(bf16)
    normed = spread(nbuf.at[me], nbuf, n_send, n_recv)
    send_audio()
    pump(PACE[4])
    normed = hand_on(normed, nbuf, n_send, n_recv)
    pump(PACE[5])

    loads[3].wait()
    for copy in normed:
        copy.wait_recv()
    held = jnp.concatenate([nbuf[s].astype(f32) for s in range(n)], axis=0)
    x = held[:, :width].astype(bf16)
    square = jnp.sum(held[:, width:], axis=1, keepdims=True)
    ssbuf[col] = jnp.broadcast_to(square, (total_rows, 128))
    partials = []
    for d, t in enumerate(tp_peers):
        partials.append(remote(ssbuf.at[col], ssbuf.at[col], s_send.at[d], s_recv.at[d], {"tp": t}))
    for c in range(CHUNKS):
        ubuf[c] = jnp.dot(x, upv[:, c * step : (c + 1) * step], preferred_element_type=f32)
        pbuf[col, c] = ubuf[c].astype(bf16)
        for d, t in enumerate(tp_peers):
            partials.append(
                remote(pbuf.at[col, c], pbuf.at[col, c], p_send.at[c, d], p_recv.at[c, d], {"tp": t})
            )
    sent.extend(partials)
    pass_audio()
    pump(PACE[6])

    loads[4].wait()
    for copy in partials:
        copy.wait_recv()
    square = sum(ssbuf[t] for t in range(tp))[:, 0:1]
    factor = lax.rsqrt(square / (width * tp) + 1e-6)
    acc = jnp.zeros((total_rows, width), f32)
    for c in range(CHUNKS):
        up_sum = (ubuf[c] + sum(pbuf[t, c].astype(f32) for t in tp_peers)) * factor
        hidden = jax.nn.gelu(up_sum, approximate=True).astype(bf16)
        acc += jnp.dot(hidden, downv[c * step : (c + 1) * step, :], preferred_element_type=f32)
    racc[...] = acc.reshape(n, rows, width)

    def send_sum(d, k):
        copy = remote(rsend.at[k], rrecv.at[k], r_send.at[k], r_recv.at[k], {"seq": peers[d]})
        sent.append(copy)
        return copy

    rsend[0] = racc[far].astype(bf16)
    crossing = send_sum(2, 0)
    rsend[1] = racc[side].astype(bf16)
    near = send_sum(2, 1)
    pump(PACE[7])

    def join_sums():
        crossing.wait_recv()
        rsend[2] = (racc[over] + rrecv[0].astype(f32)).astype(bf16)
        return send_sum(1, 2)

    outs = [attend_video(0, video[0])]
    joined = join_sums()
    pump(len(units))

    loads[2].wait()
    for copy in audio[0] + audio[1]:
        copy.wait_recv()
    k_all, v_all = whole(1), whole(2)
    wide = lax.broadcasted_iota(jnp.int32, (tokens, 128), 1)
    for j in range(pairs):
        at = slice(j * 128, (j + 1) * 128)
        o, _, total = pair_attend(cqv[:, at], k_all[:, at], v_all[:, at], scale)
        o = o / total
        heard[:, at] = jnp.where(wide < CHEAD, o[:tokens], o[tokens:]).astype(bf16)

    for h in range(1, hd - 1):
        outs.append(attend_video(h, video[h]))

    near.wait_recv()
    joined.wait_recv()
    mlp[...] = (racc[me] + rrecv[1].astype(f32) + rrecv[2].astype(f32)).astype(bf16)

    if hd > 1:
        outs.append(attend_video(hd - 1, video[hd - 1]))

    for copy in sent:
        copy.wait_send()
    for out, own in outs:
        for copy in out:
            copy.wait()
        own.wait()


def fused(n, tp, args):
    vq, vk, vv, cq, ak, av, aq, ck, cv, ai, gain, up, down = args
    tokens, vwidth = vq.shape
    hd = vwidth // VHEAD // n
    rows, width = aq.shape
    units = up.shape[1]
    bf16, f32 = jnp.bfloat16, jnp.float32
    anywhere = pl.BlockSpec(memory_space=pl.ANY)
    dma = pltpu.SemaphoreType.DMA
    head = pltpu.VMEM((hd, n, tokens, VHEAD), bf16)
    cross = pltpu.VMEM((tokens, width), bf16)
    z, t = max(n - 1, 1), max(tp - 1, 1)
    return pl.pallas_call(
        functools.partial(fused_kernel, n, tp),
        out_shape=(
            pltpu.VMEM((tokens, vwidth), bf16),
            pltpu.VMEM((tokens, width), bf16),
            pltpu.VMEM((rows, width), bf16),
            pltpu.VMEM((rows, width), bf16),
        ),
        in_specs=[anywhere] * 13,
        out_specs=(pl.BlockSpec(memory_space=pltpu.VMEM),) * 4,
        scratch_shapes=[
            head, head, head, head,
            pltpu.VMEM((3, n, rows, width), bf16),
            cross, cross, cross,
            pltpu.VMEM(up.shape, bf16),
            pltpu.VMEM(down.shape, bf16),
            pltpu.VMEM(ai.shape, bf16),
            pltpu.VMEM((1, gain.shape[0]), f32),
            pltpu.VMEM((n, rows, width), f32),
            pltpu.VMEM((3, rows, width), bf16),
            pltpu.VMEM((3, rows, width), bf16),
            pltpu.VMEM((n, rows, 128), f32),
            pltpu.VMEM((3, rows, 128), f32),
            pltpu.VMEM((tp, n * rows, 128), f32),
            pltpu.VMEM((n, rows, width + 128), bf16),
            pltpu.VMEM((tp, CHUNKS, n * rows, units // CHUNKS), bf16),
            pltpu.VMEM((CHUNKS, n * rows, units // CHUNKS), f32),
            pltpu.VMEM((n, rows, width), f32),
            pltpu.VMEM((3, rows, width), bf16),
            pltpu.VMEM((3, rows, width), bf16),
            dma((hd, z, 3)), dma((hd, z, 3)), dma((hd, z)), dma((hd, z)),
            dma((3, z)), dma((3, z)), dma((z,)), dma((z,)), dma((z,)), dma((z,)), dma((t,)), dma((t,)),
            dma((z,)), dma((z,)), dma((CHUNKS, t)), dma((CHUNKS, t)), dma((z,)), dma((z,)),
            dma((hd, 3)), dma((hd,)), dma((13,)),
        ],
        compiler_params=pltpu.CompilerParams(collective_id=0, has_side_effects=True),
    )(vq, vk, vv, cq, ak, av, aq, ck, cv, ai, gain.reshape(1, -1), up, down)


def hand_over(*refs):
    count = (len(refs) - 1) // 2
    copies = [pltpu.make_async_copy(refs[i], refs[count + i], refs[-1].at[i]) for i in range(count)]
    for copy in copies:
        copy.start()
    for copy in copies:
        copy.wait()


def deliver(arrays):
    arrays = [pltpu.with_memory_space_constraint(a, pltpu.VMEM) for a in arrays]
    return pl.pallas_call(
        hand_over,
        out_shape=tuple(jax.ShapeDtypeStruct(a.shape, a.dtype) for a in arrays),
        in_specs=[pl.BlockSpec(memory_space=pltpu.VMEM)] * len(arrays),
        out_specs=(pl.BlockSpec(memory_space=pl.ANY),) * len(arrays),
        scratch_shapes=[pltpu.SemaphoreType.DMA((len(arrays),))],
    )(*arrays)


def fits(n, vq, aq, up):
    heads = vq.shape[2] // VHEAD
    return (
        n == 4
        and heads % n == 0
        and vq.shape[1] % 16 == 0
        and aq.shape[1] % 8 == 0
        and aq.shape[2] % 128 == 0
        and aq.shape[2] // CHEAD <= 64
        and up.shape[0] == aq.shape[2]
        and up.shape[1] % (128 * CHUNKS) == 0
    )


def attend_rows(queries, keys_in, values_in, head_count):
    head_size = queries.shape[1] // head_count
    query_heads = queries.reshape(queries.shape[0], head_count, head_size)
    key_heads = keys_in.reshape(keys_in.shape[0], head_count, head_size)
    value_heads = values_in.reshape(values_in.shape[0], head_count, head_size)
    scores = jnp.einsum(
        "qhd,khd->qhk", query_heads, key_heads, preferred_element_type=jnp.float32
    ) / math.sqrt(head_size)
    peak_value = jnp.max(scores, axis=2, keepdims=True)
    weights = jnp.exp(scores - peak_value)
    totals = jnp.sum(weights, axis=2)
    weighted = jnp.einsum(
        "qhk,khd->qhd",
        weights.astype(jnp.bfloat16),
        value_heads,
        preferred_element_type=jnp.float32,
    )
    result = weighted / totals[:, :, None]
    return result.reshape(queries.shape[0], head_count * head_size).astype(jnp.bfloat16)


def attend(queries, keys_in, values_in, head_count):
    row_total = queries.shape[0]
    block_rows = 512 if row_total % 512 == 0 else row_total
    pieces = queries.reshape(row_total // block_rows, block_rows, queries.shape[1])
    result = lax.map(
        lambda row_piece: attend_rows(row_piece, keys_in, values_in, head_count), pieces
    )
    return result.reshape(row_total, queries.shape[1])


def video_self(queries, keys_in, values_in):
    seq_count = lax.axis_size("seq")
    local_heads = queries.shape[1] // VHEAD
    dest_heads = max(local_heads // seq_count, 1)
    blocks = seq_count * dest_heads // local_heads
    groups = local_heads // dest_heads
    group_width = dest_heads * VHEAD
    token_count = queries.shape[0]
    block_tokens = token_count // blocks

    def spread(tensor):
        shaped = tensor.reshape(token_count, groups, group_width).transpose(1, 0, 2)
        shaped = jnp.broadcast_to(shaped[:, None], (groups, blocks, token_count, group_width))
        return shaped.reshape(seq_count, token_count, group_width)

    shaped = queries.reshape(blocks, block_tokens, groups, group_width).transpose(2, 0, 1, 3)
    own_queries = lax.all_to_all(
        shaped.reshape(seq_count, block_tokens, group_width),
        "seq",
        split_axis=0,
        concat_axis=0,
        tiled=True,
    )
    keys_all = lax.all_to_all(spread(keys_in), "seq", split_axis=0, concat_axis=0, tiled=True)
    values_all = lax.all_to_all(spread(values_in), "seq", split_axis=0, concat_axis=0, tiled=True)
    keys_all = keys_all.reshape(-1, group_width)
    values_all = values_all.reshape(-1, group_width)
    own_queries = own_queries.reshape(-1, group_width)
    attended = attend(own_queries, keys_all, values_all, dest_heads)
    returned = lax.all_to_all(
        attended.reshape(seq_count, block_tokens, group_width),
        "seq",
        split_axis=0,
        concat_axis=0,
        tiled=True,
    )
    returned = returned.reshape(groups, blocks, block_tokens, group_width).transpose(1, 2, 0, 3)
    return returned.reshape(token_count, groups * group_width)


def audio_listen(queries, keys_in, values_in, head_count):
    head_size = queries.shape[1] // head_count
    query_heads = queries.reshape(queries.shape[0], head_count, head_size)
    key_heads = keys_in.reshape(keys_in.shape[0], head_count, head_size)
    value_heads = values_in.reshape(values_in.shape[0], head_count, head_size)
    scores = jnp.einsum(
        "qhd,khd->qhk", query_heads, key_heads, preferred_element_type=jnp.float32
    ) / math.sqrt(head_size)
    local_peak = jnp.max(scores, axis=2)
    peak_value = lax.pmax(local_peak, "seq")
    weights = jnp.exp(scores - peak_value[:, :, None])
    totals = jnp.sum(weights, axis=2)
    weighted = jnp.einsum(
        "qhk,khd->qhd",
        weights.astype(jnp.bfloat16),
        value_heads,
        preferred_element_type=jnp.float32,
    )
    totals, weighted = (totals, weighted.reshape(queries.shape[0], head_count * head_size))
    totals, weighted = (
        lax.psum_scatter(totals, "seq", scatter_dimension=0, tiled=True),
        lax.psum_scatter(weighted, "seq", scatter_dimension=0, tiled=True),
    )
    return (weighted / jnp.repeat(totals, head_size, axis=1)).astype(jnp.bfloat16)


def audio_block(audio_rows, audio_seen, norm_gain, up_weight, down_weight):
    features = lax.all_gather(audio_seen, "tp", axis=1, tiled=True)
    residual = audio_rows.astype(jnp.float32) + features.astype(jnp.float32)
    scale_factor = lax.rsqrt(jnp.mean(residual * residual, axis=1, keepdims=True) + 1e-06)
    normed = (residual * scale_factor * norm_gain).astype(jnp.bfloat16)
    slice_width = up_weight.shape[0]
    own_features = lax.dynamic_slice_in_dim(
        normed, lax.axis_index("tp") * slice_width, slice_width, 1
    )
    partial_sum = jnp.dot(
        lax.all_gather(own_features, "seq", axis=0, tiled=True),
        up_weight,
        preferred_element_type=jnp.float32,
    )
    hidden = jax.nn.gelu(lax.psum(partial_sum, "tp")).astype(jnp.bfloat16)
    return lax.psum_scatter(
        jnp.dot(hidden, down_weight, preferred_element_type=jnp.float32),
        "seq",
        scatter_dimension=0,
        tiled=True,
    ).astype(jnp.bfloat16)


def body(
    video_query,
    video_key,
    video_value,
    cross_query,
    audio_key,
    audio_value,
    audio_query,
    cross_key,
    cross_value,
    audio_input,
    norm_gain,
    up_weight,
    down_weight,
):
    if fits(lax.axis_size("seq"), video_query, audio_query, up_weight):
        args = (video_query, video_key, video_value, cross_query, audio_key, audio_value)
        args += (audio_query, cross_key, cross_value, audio_input)
        args = tuple(a[0] for a in args) + (norm_gain, up_weight, down_weight)
        outs = deliver(fused(lax.axis_size("seq"), lax.axis_size("tp"), args))
        return tuple(out[None] for out in outs)
    mixed_list, heard_list, seen_list, output_list = ([], [], [], [])
    cross_heads = cross_query.shape[2] // CHEAD
    mixed_list.append(video_self(video_query[0], video_key[0], video_value[0]))
    gathered_query = lax.all_gather(audio_query[0], "seq", axis=0, tiled=True)
    gathered_key = lax.all_gather(audio_key[0], "seq", axis=0, tiled=True)
    gathered_value = lax.all_gather(audio_value[0], "seq", axis=0, tiled=True)
    heard_list.append(attend(cross_query[0], gathered_key, gathered_value, cross_heads))
    audio_seen = audio_listen(gathered_query, cross_key[0], cross_value[0], cross_heads)
    seen_list.append(audio_seen)
    output_list.append(audio_block(audio_input[0], audio_seen, norm_gain, up_weight, down_weight))
    return (
        jnp.stack(mixed_list),
        jnp.stack(heard_list),
        jnp.stack(seen_list),
        jnp.stack(output_list),
    )


def solution(mesh):
    placed = (
        P(("clips", "dp"), "seq", "tp"),
        P(("clips", "dp"), "seq", "tp"),
        P(("clips", "dp"), "seq", "tp"),
        P(("clips", "dp"), "seq", "tp"),
        P(("clips", "dp"), "seq", "tp"),
        P(("clips", "dp"), "seq", "tp"),
        P(("clips", "dp"), "seq", "tp"),
        P(("clips", "dp"), "seq", "tp"),
        P(("clips", "dp"), "seq", "tp"),
        P(("clips", "dp"), "seq", None),
        P(),
        P("tp", "seq"),
        P("seq", "tp"),
    )
    return jax.shard_map(
        body,
        mesh=mesh,
        in_specs=placed,
        out_specs=(
            P(("clips", "dp"), "seq", "tp"),
            P(("clips", "dp"), "seq", "tp"),
            P(("clips", "dp"), "seq", "tp"),
            P(("clips", "dp"), "seq", "tp"),
        ),
        check_vma=False,
    )
```

```python
import functools
import math

import jax
import jax.numpy as jnp
from jax import lax
from jax.experimental import pallas as pl
from jax.experimental.pallas import tpu as pltpu
from jax.sharding import PartitionSpec as P

VHEAD = 128
CHEAD = 64
MESH = pl.DeviceIdType.MESH
LOG2E = math.log2(math.e)
CHUNKS = 4
EARLY = 3
PACE = ((0, 1, 2, 2, 2, 2, 0, 0), (0, 1, 1, 1, 1, 1, 2, 2))
ORDER = (1, 0, 2)
DIRECT = ((False, False), (False, False))
OUTER_FIRST = True
TURNS = (0, 0, 0, 0, 1, 0)


def dot_t(a, b):
    return lax.dot_general(a, b, (((1,), (1,)), ((), ())), preferred_element_type=jnp.float32)


def softmax_parts(q, k, scale):
    s = dot_t(q, k)
    peak = jnp.max(s, axis=1, keepdims=True)
    p = jnp.exp2((s - peak) * (scale * LOG2E))
    return p, peak * scale, jnp.sum(p, axis=1, keepdims=True)


def pair_attend(q, k, v, scale):
    low = lax.broadcasted_iota(jnp.int32, q.shape, 1) < CHEAD
    zero = jnp.zeros_like(q)
    both = jnp.concatenate([jnp.where(low, q, zero), jnp.where(low, zero, q)], axis=0)
    p, peak, total = softmax_parts(both, k, scale)
    o = jnp.dot(p.astype(jnp.bfloat16), v, preferred_element_type=jnp.float32)
    return o, peak, total


def partners(me, n):
    if n & (n - 1):
        return [lax.rem(me + d, n) for d in range(1, n)]
    found = []
    for flip in range(n - 1, 0, -1):
        place, bit = me * 0, 1
        while bit < n:
            digit = lax.rem(lax.div(me, bit), 2)
            place = place + bit * ((1 - digit) if flip & bit else digit)
            bit *= 2
        found.append(place)
    return found


def fused_kernel(
    n, tp,
    vq, vk, vv, cq, ak, av, aq, ck, cv, ai, gain, up, down,
    mixed, heard, seen, mlp,
    qbuf, kbuf, vbuf, obuf, abuf, cqv, ckv, cvv, upv, downv, aiv, gainv, xown, xsend, xrecv, tsend, trecv, ssbuf, nbuf, pbuf, ubuf, racc, rsend, rrecv,
    v_send, v_recv, o_send, o_recv, a_send, a_recv, x_send, x_recv, t_send, t_recv, s_send, s_recv,
    n_send, n_recv, p_send, p_recv, r_send, r_recv, own_sem, oown_sem, load_sem, ready,
):
    me = lax.axis_index("seq")
    col = lax.axis_index("tp")
    core = lax.rem(lax.axis_index("dp"), 2)
    tokens = vq.shape[0]
    hd = vq.shape[1] // VHEAD // n
    rows, width = aq.shape
    pairs = width // 128
    units = up.shape[1]
    step = units // CHUNKS
    f32, bf16 = jnp.float32, jnp.bfloat16
    peers = partners(me, n)
    tp_peers = [lax.rem(col + d, tp) for d in range(1, tp)]

    def remote(src, dst, ss, rs, where):
        copy = pltpu.make_async_remote_copy(
            src_ref=src, dst_ref=dst, send_sem=ss, recv_sem=rs, device_id=where, device_id_type=MESH
        )
        copy.start()
        return copy

    far, over, side = peers
    inner = lax.rem(lax.div(me + 1, 2), 2) == 1
    outer = jnp.logical_not(inner)
    streams = ((vq, qbuf), (vk, kbuf), (vv, vbuf))
    sent = []
    order = ORDER
    first = jnp.where(inner, 1, 0) if OUTER_FIRST else 1
    back = ((first, jnp.where(inner, over, far) if OUTER_FIRST else over), (1 - first, jnp.where(inner, far, over) if OUTER_FIRST else far), (2, side), (3, me))
    units = [(h, i) for h in range(hd) for i in (1, 2, 0)]
    video = [[] for _ in range(hd)]

    def unit(h, i, d):
        src, buf = streams[i]
        cols = pl.ds(pl.multiple_of((peers[d] * hd + h) * VHEAD, VHEAD), VHEAD)
        return pltpu.make_async_remote_copy(
            src_ref=src.at[:, cols], dst_ref=buf.at[h, me], send_sem=v_send.at[h, d, i], recv_sem=v_recv.at[h, d, i],
            device_id={"seq": peers[d]}, device_id_type=MESH,
        )

    for h, i in units:
        video[h] += [unit(h, i, d) for d in order]
    sent += [copy for copies in video for copy in copies]
    marks = [EARLY, EARLY]

    def pump(w):
        ends = [min(marks[c] + PACE[c][w], len(units)) if w < len(PACE[c]) else len(units) for c in range(2)]
        for k, (h, i) in enumerate(units):
            mine = [marks[c] <= k < ends[c] for c in range(2)]

            def go():
                for d in order:
                    unit(h, i, d).start()

            if all(mine):
                go()
            elif any(mine):
                pl.when(core == mine.index(True))(go)
        marks[:] = ends

    def tell(where, k):
        pl.semaphore_signal(ready.at[k], inc=1, device_id=where, device_id_type=MESH)

    barrier = pltpu.get_barrier_semaphore()
    early = units[:EARLY]

    @pl.when(inner)
    def _():
        for p in (far, side):
            pl.semaphore_signal(barrier, inc=1, device_id={"seq": p}, device_id_type=MESH)

    @pl.when(outer)
    def _():
        for t in tp_peers:
            pl.semaphore_signal(barrier, inc=1, device_id={"tp": t}, device_id_type=MESH)

    pl.semaphore_wait(barrier, jnp.where(inner, 1, tp))

    @pl.when(inner)
    def _():
        for h, i in early:
            unit(h, i, 0).start()

    @pl.when(outer)
    def _():
        tell({"seq": side}, 0)
        for t in tp_peers:
            tell({"tp": t}, 3)
        for h, i in early:
            unit(h, i, 2).start()

    loads = []
    stays = ((ck, ckv), (cv, cvv), (cq, cqv), (up, upv), (down, downv), (ai, aiv), (gain, gainv))
    stays += tuple((src, abuf.at[i, me]) for i, src in enumerate((aq, ak, av)))
    for i, (src, dst) in enumerate(stays):
        loads.append(pltpu.make_async_copy(src, dst, load_sem.at[i]))

    for i in (0, 1, 7):
        loads[i].start()

    @pl.when(inner)
    def _():
        pl.semaphore_wait(ready.at[0], 1)
        tell({"seq": far}, 1)
        pl.semaphore_wait(ready.at[1], 1)
        tell({"seq": side}, 2)

    @pl.when(outer)
    def _():
        pl.semaphore_wait(ready.at[2], 1)

    def attend_video(h, copies):
        for copy in owns[h]:
            copy.wait()
        for copy in copies:
            copy.wait_recv()
        k = kbuf[h].reshape(n * tokens, VHEAD)
        v = vbuf[h].reshape(n * tokens, VHEAD)
        cols = pl.ds(pl.multiple_of((me * hd + h) * VHEAD, VHEAD), VHEAD)
        out = []
        for k_, (d, p) in enumerate(back):
            w, _, total = softmax_parts(qbuf[h, p], k, 1.0 / math.sqrt(VHEAD))
            o = jnp.dot(w.astype(bf16), v, preferred_element_type=f32) / total
            obuf[h, p] = o.astype(bf16)
            if k_ < n - 1:
                out.append(remote(obuf.at[h, p], mixed.at[:, cols], o_send.at[h, d], o_recv.at[h, d], {"seq": p}))
        own = pltpu.make_async_copy(obuf.at[h, me], mixed.at[:, cols], oown_sem.at[h])
        own.start()
        return out, own

    outs = []
    heads = list(range(hd))

    def attend_next(count):
        for h in heads[:count]:
            outs.append(attend_video(h, video[h]))
        del heads[:count]

    def spread(src, slots, ss, rs, direct=(False, False)):
        def copy(d):
            return pltpu.make_async_remote_copy(
                src_ref=src, dst_ref=slots.at[me], send_sem=ss.at[d], recv_sem=rs.at[d],
                device_id={"seq": peers[d]}, device_id_type=MESH,
            )

        copies = [copy(2), copy(1)]
        for c in copies:
            c.start()
        if all(direct):
            copy(0).start()
        elif any(direct):
            pl.when(core == direct.index(True))(lambda: copy(0).start())
        sent.extend(copies)
        return copies

    def hand_on(copies, slots, ss, rs, direct=(False, False)):
        copies[1].wait_recv()
        copy = pltpu.make_async_remote_copy(
            src_ref=slots.at[over], dst_ref=slots.at[over], send_sem=ss.at[0], recv_sem=rs.at[0],
            device_id={"seq": side}, device_id_type=MESH,
        )
        if not any(direct):
            copy.start()
        elif not all(direct):
            pl.when(core == direct.index(False))(lambda: copy.start())
        sent.append(copy)
        return [copies[0], copy]

    asked = spread(aq, abuf.at[0], a_send.at[0], a_recv.at[0], DIRECT[0])
    for h, i in early:

        @pl.when(inner)
        def _():
            unit(h, i, 2).start()

        @pl.when(outer)
        def _():
            unit(h, i, 0).start()

        unit(h, i, 1).start()
    owns = []
    for h in range(hd):
        cols = pl.ds(pl.multiple_of((me * hd + h) * VHEAD, VHEAD), VHEAD)
        owns.append([])
        for i, (src, buf) in enumerate(streams):
            copy = pltpu.make_async_copy(src.at[:, cols], buf.at[h, me], own_sem.at[h, i])
            copy.start()
            owns[-1].append(copy)
    for copy in loads[2:7] + loads[8:]:
        copy.start()
    pump(0)
    asked = hand_on(asked, abuf.at[0], a_send.at[0], a_recv.at[0], DIRECT[0])
    pump(1)

    @pl.when(outer)
    def _():
        pl.semaphore_wait(ready.at[3], tp - 1)
        tell({"seq": side}, 4)

    for copy in loads[:2] + loads[5:]:
        copy.wait()
    for copy in asked:
        copy.wait_recv()

    def whole(i):
        return jnp.concatenate([abuf[i, s].astype(f32) for s in range(n)], axis=0).astype(bf16)

    scale = 1.0 / math.sqrt(CHEAD)
    total_rows = n * rows
    q_all = whole(0)
    lane = lax.broadcasted_iota(jnp.int32, (total_rows, 128), 1)
    stats = jnp.ones((total_rows, 128), f32)
    for j in range(pairs):
        at = slice(j * 128, (j + 1) * 128)
        o, peak, total = pair_attend(q_all[:, at], ckv[:, at], cvv[:, at], scale)
        picked = jnp.where(lane < CHEAD, o[:total_rows], o[total_rows:])
        xown[:, :, at] = picked.reshape(n, rows, 128)
        for half in range(2):
            part = slice(half * total_rows, (half + 1) * total_rows)
            stats = jnp.where(lane == 2 * j + half, peak[part], stats)
            stats = jnp.where(lane == 64 + 2 * j + half, total[part], stats)
    tsend[...] = stats.reshape(n, rows, 128)

    def send_part(d, slot, k):
        p = peers[d]
        copies = [
            remote(tsend.at[slot], trecv.at[k], t_send.at[k], t_recv.at[k], {"seq": p}),
            remote(xsend.at[k], xrecv.at[k], x_send.at[k], x_recv.at[k], {"seq": p}),
        ]
        sent.extend(copies)
        return copies

    xsend[0] = xown[far].astype(bf16)
    crossing = send_part(2, far, 0)
    xsend[1] = xown[side].astype(bf16)
    near = send_part(2, side, 1)
    place = lax.broadcasted_iota(jnp.int32, (rows, 128), 1)

    def weigh(stats):
        peak = functools.reduce(jnp.maximum, stats)
        factors = [jnp.exp(t - peak) for t in stats]
        return peak, factors, sum(f * pltpu.roll(t, 64, 1) for f, t in zip(factors, stats))

    def blend(factors, blocks):
        pieces = []
        for j in range(pairs):
            at = slice(j * 128, (j + 1) * 128)
            terms = [
                jnp.where(place < CHEAD, f[:, 2 * j : 2 * j + 1], f[:, 2 * j + 1 : 2 * j + 2]) * b[:, at].astype(f32)
                for f, b in zip(factors, blocks)
            ]
            pieces.append(sum(terms[1:], terms[0]))
        return jnp.concatenate(pieces, axis=1).astype(bf16)

    pump(2)

    for copy in crossing:
        copy.wait_recv()
    peak, factors, total = weigh([tsend[over], trecv[0]])
    xsend[2] = blend(factors, [xown[over], xrecv[0]])
    tsend[over] = jnp.where(place < 64, peak, pltpu.roll(total, 64, 1))
    joined = send_part(1, over, 2)
    audio = [None, None]

    def send_audio():
        for i, src in enumerate((ak, av)):
            audio[i] = spread(src, abuf.at[i + 1], a_send.at[i + 1], a_recv.at[i + 1])

    def pass_audio():
        for i in range(2):
            audio[i] = hand_on(audio[i], abuf.at[i + 1], a_send.at[i + 1], a_recv.at[i + 1])

    pump(3)
    attend_next(TURNS[0])

    for copy in near + joined:
        copy.wait_recv()
    _, factors, total = weigh([tsend[me], trecv[1], trecv[2]])
    seen_bf = blend([f / total for f in factors], [xown[me], xrecv[1], xrecv[2]])
    seen[...] = seen_bf

    mine = pl.ds(pl.multiple_of(col * width, 128), width)
    residual = aiv[:, mine].astype(f32) + seen_bf.astype(f32)
    square = jnp.sum(residual * residual, axis=1, keepdims=True)
    first = square.astype(bf16).astype(f32)
    second = (square - first).astype(bf16).astype(f32)
    third = square - first - second
    split = jnp.where(place == 0, first, jnp.where(place == 1, second, jnp.where(place == 2, third, 0.0)))
    nbuf[me, :, :width] = (residual * gainv[:, mine]).astype(bf16)
    nbuf[me, :, width:] = split.astype(bf16)
    normed = spread(nbuf.at[me], nbuf, n_send, n_recv, DIRECT[1])
    send_audio()
    pump(4)
    attend_next(TURNS[1])
    normed = hand_on(normed, nbuf, n_send, n_recv, DIRECT[1])
    pump(5)
    attend_next(TURNS[2])

    loads[3].wait()
    for copy in normed:
        copy.wait_recv()
    held = jnp.concatenate([nbuf[s].astype(f32) for s in range(n)], axis=0)
    x = held[:, :width].astype(bf16)
    square = jnp.sum(held[:, width:], axis=1, keepdims=True)
    ssbuf[col] = jnp.broadcast_to(square, (total_rows, 128))
    partials = []

    @pl.when(inner)
    def _():
        pl.semaphore_wait(ready.at[4], 1)

    for d, t in enumerate(tp_peers):
        partials.append(remote(ssbuf.at[col], ssbuf.at[col], s_send.at[d], s_recv.at[d], {"tp": t}))
    for c in range(CHUNKS):
        ubuf[c] = jnp.dot(x, upv[:, c * step : (c + 1) * step], preferred_element_type=f32)
        pbuf[col, c] = ubuf[c].astype(bf16)
        for d, t in enumerate(tp_peers):
            partials.append(
                remote(pbuf.at[col, c], pbuf.at[col, c], p_send.at[c, d], p_recv.at[c, d], {"tp": t})
            )
    sent.extend(partials)
    pass_audio()
    pump(6)
    attend_next(TURNS[3])

    loads[4].wait()
    for copy in partials[: tp - 1]:
        copy.wait_recv()
    square = sum(ssbuf[t] for t in range(tp))[:, 0:1]
    factor = lax.rsqrt(square / (width * tp) + 1e-6)
    acc = jnp.zeros((total_rows, width), f32)
    for c in range(CHUNKS):
        for copy in partials[(c + 1) * (tp - 1) : (c + 2) * (tp - 1)]:
            copy.wait_recv()
        up_sum = (ubuf[c] + sum(pbuf[t, c].astype(f32) for t in tp_peers)) * factor
        hidden = jax.nn.gelu(up_sum, approximate=True).astype(bf16)
        acc += jnp.dot(hidden, downv[c * step : (c + 1) * step, :], preferred_element_type=f32)
    racc[...] = acc.reshape(n, rows, width)

    def send_sum(d, k):
        copy = remote(rsend.at[k], rrecv.at[k], r_send.at[k], r_recv.at[k], {"seq": peers[d]})
        sent.append(copy)
        return copy

    rsend[0] = racc[far].astype(bf16)
    crossing = send_sum(2, 0)
    rsend[1] = racc[side].astype(bf16)
    near = send_sum(2, 1)
    pump(7)

    def join_sums():
        crossing.wait_recv()
        rsend[2] = (racc[over] + rrecv[0].astype(f32)).astype(bf16)
        return send_sum(1, 2)

    attend_next(TURNS[4])
    joined = join_sums()
    pump(8)
    attend_next(TURNS[5])

    loads[2].wait()
    for copy in audio[0] + audio[1]:
        copy.wait_recv()
    k_all, v_all = whole(1), whole(2)
    wide = lax.broadcasted_iota(jnp.int32, (tokens, 128), 1)
    for j in range(pairs):
        at = slice(j * 128, (j + 1) * 128)
        o, _, total = pair_attend(cqv[:, at], k_all[:, at], v_all[:, at], scale)
        o = o / total
        heard[:, at] = jnp.where(wide < CHEAD, o[:tokens], o[tokens:]).astype(bf16)

    attend_next(len(heads) - 1)

    near.wait_recv()
    joined.wait_recv()
    mlp[...] = (racc[me] + rrecv[1].astype(f32) + rrecv[2].astype(f32)).astype(bf16)

    attend_next(len(heads))

    for copy in sent:
        copy.wait_send()
    for out, own in outs:
        for copy in out:
            copy.wait()
        own.wait()


def fused(n, tp, args):
    vq, vk, vv, cq, ak, av, aq, ck, cv, ai, gain, up, down = args
    tokens, vwidth = vq.shape
    hd = vwidth // VHEAD // n
    rows, width = aq.shape
    units = up.shape[1]
    bf16, f32 = jnp.bfloat16, jnp.float32
    anywhere = pl.BlockSpec(memory_space=pl.ANY)
    dma = pltpu.SemaphoreType.DMA
    head = pltpu.VMEM((hd, n, tokens, VHEAD), bf16)
    cross = pltpu.VMEM((tokens, width), bf16)
    z, t = max(n - 1, 1), max(tp - 1, 1)
    return pl.pallas_call(
        functools.partial(fused_kernel, n, tp),
        out_shape=(
            pltpu.VMEM((tokens, vwidth), bf16),
            pltpu.VMEM((tokens, width), bf16),
            pltpu.VMEM((rows, width), bf16),
            pltpu.VMEM((rows, width), bf16),
        ),
        in_specs=[anywhere] * 13,
        out_specs=(pl.BlockSpec(memory_space=pltpu.VMEM),) * 4,
        scratch_shapes=[
            head, head, head, head,
            pltpu.VMEM((3, n, rows, width), bf16),
            cross, cross, cross,
            pltpu.VMEM(up.shape, bf16),
            pltpu.VMEM(down.shape, bf16),
            pltpu.VMEM(ai.shape, bf16),
            pltpu.VMEM((1, gain.shape[0]), f32),
            pltpu.VMEM((n, rows, width), f32),
            pltpu.VMEM((3, rows, width), bf16),
            pltpu.VMEM((3, rows, width), bf16),
            pltpu.VMEM((n, rows, 128), f32),
            pltpu.VMEM((3, rows, 128), f32),
            pltpu.VMEM((tp, n * rows, 128), f32),
            pltpu.VMEM((n, rows, width + 128), bf16),
            pltpu.VMEM((tp, CHUNKS, n * rows, units // CHUNKS), bf16),
            pltpu.VMEM((CHUNKS, n * rows, units // CHUNKS), f32),
            pltpu.VMEM((n, rows, width), f32),
            pltpu.VMEM((3, rows, width), bf16),
            pltpu.VMEM((3, rows, width), bf16),
            dma((hd, z, 3)), dma((hd, z, 3)), dma((hd, z)), dma((hd, z)),
            dma((3, z)), dma((3, z)), dma((z,)), dma((z,)), dma((z,)), dma((z,)), dma((t,)), dma((t,)),
            dma((z,)), dma((z,)), dma((CHUNKS, t)), dma((CHUNKS, t)), dma((z,)), dma((z,)),
            dma((hd, 3)), dma((hd,)), dma((10,)), pltpu.SemaphoreType.REGULAR((5,)),
        ],
        compiler_params=pltpu.CompilerParams(collective_id=0, has_side_effects=True),
    )(vq, vk, vv, cq, ak, av, aq, ck, cv, ai, gain.reshape(1, -1), up, down)


def hand_over(*refs):
    count = (len(refs) - 1) // 2
    copies = [pltpu.make_async_copy(refs[i], refs[count + i], refs[-1].at[i]) for i in range(count)]
    for copy in copies:
        copy.start()
    for copy in copies:
        copy.wait()


def deliver(arrays):
    arrays = [pltpu.with_memory_space_constraint(a, pltpu.VMEM) for a in arrays]
    return pl.pallas_call(
        hand_over,
        out_shape=tuple(jax.ShapeDtypeStruct(a.shape, a.dtype) for a in arrays),
        in_specs=[pl.BlockSpec(memory_space=pltpu.VMEM)] * len(arrays),
        out_specs=(pl.BlockSpec(memory_space=pl.ANY),) * len(arrays),
        scratch_shapes=[pltpu.SemaphoreType.DMA((len(arrays),))],
    )(*arrays)


def fits(n, vq, aq, up):
    heads = vq.shape[2] // VHEAD
    return (
        n == 4
        and heads % n == 0
        and vq.shape[1] % 16 == 0
        and aq.shape[1] % 8 == 0
        and aq.shape[2] % 128 == 0
        and aq.shape[2] // CHEAD <= 64
        and up.shape[0] == aq.shape[2]
        and up.shape[1] % (128 * CHUNKS) == 0
    )


def attend_rows(queries, keys_in, values_in, head_count):
    head_size = queries.shape[1] // head_count
    query_heads = queries.reshape(queries.shape[0], head_count, head_size)
    key_heads = keys_in.reshape(keys_in.shape[0], head_count, head_size)
    value_heads = values_in.reshape(values_in.shape[0], head_count, head_size)
    scores = jnp.einsum(
        "qhd,khd->qhk", query_heads, key_heads, preferred_element_type=jnp.float32
    ) / math.sqrt(head_size)
    peak_value = jnp.max(scores, axis=2, keepdims=True)
    weights = jnp.exp(scores - peak_value)
    totals = jnp.sum(weights, axis=2)
    weighted = jnp.einsum(
        "qhk,khd->qhd",
        weights.astype(jnp.bfloat16),
        value_heads,
        preferred_element_type=jnp.float32,
    )
    result = weighted / totals[:, :, None]
    return result.reshape(queries.shape[0], head_count * head_size).astype(jnp.bfloat16)


def attend(queries, keys_in, values_in, head_count):
    row_total = queries.shape[0]
    block_rows = 512 if row_total % 512 == 0 else row_total
    pieces = queries.reshape(row_total // block_rows, block_rows, queries.shape[1])
    result = lax.map(
        lambda row_piece: attend_rows(row_piece, keys_in, values_in, head_count), pieces
    )
    return result.reshape(row_total, queries.shape[1])


def video_self(queries, keys_in, values_in):
    seq_count = lax.axis_size("seq")
    local_heads = queries.shape[1] // VHEAD
    dest_heads = max(local_heads // seq_count, 1)
    blocks = seq_count * dest_heads // local_heads
    groups = local_heads // dest_heads
    group_width = dest_heads * VHEAD
    token_count = queries.shape[0]
    block_tokens = token_count // blocks

    def spread(tensor):
        shaped = tensor.reshape(token_count, groups, group_width).transpose(1, 0, 2)
        shaped = jnp.broadcast_to(shaped[:, None], (groups, blocks, token_count, group_width))
        return shaped.reshape(seq_count, token_count, group_width)

    shaped = queries.reshape(blocks, block_tokens, groups, group_width).transpose(2, 0, 1, 3)
    own_queries = lax.all_to_all(
        shaped.reshape(seq_count, block_tokens, group_width),
        "seq",
        split_axis=0,
        concat_axis=0,
        tiled=True,
    )
    keys_all = lax.all_to_all(spread(keys_in), "seq", split_axis=0, concat_axis=0, tiled=True)
    values_all = lax.all_to_all(spread(values_in), "seq", split_axis=0, concat_axis=0, tiled=True)
    keys_all = keys_all.reshape(-1, group_width)
    values_all = values_all.reshape(-1, group_width)
    own_queries = own_queries.reshape(-1, group_width)
    attended = attend(own_queries, keys_all, values_all, dest_heads)
    returned = lax.all_to_all(
        attended.reshape(seq_count, block_tokens, group_width),
        "seq",
        split_axis=0,
        concat_axis=0,
        tiled=True,
    )
    returned = returned.reshape(groups, blocks, block_tokens, group_width).transpose(1, 2, 0, 3)
    return returned.reshape(token_count, groups * group_width)


def audio_listen(queries, keys_in, values_in, head_count):
    head_size = queries.shape[1] // head_count
    query_heads = queries.reshape(queries.shape[0], head_count, head_size)
    key_heads = keys_in.reshape(keys_in.shape[0], head_count, head_size)
    value_heads = values_in.reshape(values_in.shape[0], head_count, head_size)
    scores = jnp.einsum(
        "qhd,khd->qhk", query_heads, key_heads, preferred_element_type=jnp.float32
    ) / math.sqrt(head_size)
    local_peak = jnp.max(scores, axis=2)
    peak_value = lax.pmax(local_peak, "seq")
    weights = jnp.exp(scores - peak_value[:, :, None])
    totals = jnp.sum(weights, axis=2)
    weighted = jnp.einsum(
        "qhk,khd->qhd",
        weights.astype(jnp.bfloat16),
        value_heads,
        preferred_element_type=jnp.float32,
    )
    totals, weighted = (totals, weighted.reshape(queries.shape[0], head_count * head_size))
    totals, weighted = (
        lax.psum_scatter(totals, "seq", scatter_dimension=0, tiled=True),
        lax.psum_scatter(weighted, "seq", scatter_dimension=0, tiled=True),
    )
    return (weighted / jnp.repeat(totals, head_size, axis=1)).astype(jnp.bfloat16)


def audio_block(audio_rows, audio_seen, norm_gain, up_weight, down_weight):
    features = lax.all_gather(audio_seen, "tp", axis=1, tiled=True)
    residual = audio_rows.astype(jnp.float32) + features.astype(jnp.float32)
    scale_factor = lax.rsqrt(jnp.mean(residual * residual, axis=1, keepdims=True) + 1e-06)
    normed = (residual * scale_factor * norm_gain).astype(jnp.bfloat16)
    slice_width = up_weight.shape[0]
    own_features = lax.dynamic_slice_in_dim(
        normed, lax.axis_index("tp") * slice_width, slice_width, 1
    )
    partial_sum = jnp.dot(
        lax.all_gather(own_features, "seq", axis=0, tiled=True),
        up_weight,
        preferred_element_type=jnp.float32,
    )
    hidden = jax.nn.gelu(lax.psum(partial_sum, "tp")).astype(jnp.bfloat16)
    return lax.psum_scatter(
        jnp.dot(hidden, down_weight, preferred_element_type=jnp.float32),
        "seq",
        scatter_dimension=0,
        tiled=True,
    ).astype(jnp.bfloat16)


def body(
    video_query,
    video_key,
    video_value,
    cross_query,
    audio_key,
    audio_value,
    audio_query,
    cross_key,
    cross_value,
    audio_input,
    norm_gain,
    up_weight,
    down_weight,
):
    if fits(lax.axis_size("seq"), video_query, audio_query, up_weight):
        args = (video_query, video_key, video_value, cross_query, audio_key, audio_value)
        args += (audio_query, cross_key, cross_value, audio_input)
        args = tuple(a[0] for a in args) + (norm_gain, up_weight, down_weight)
        outs = deliver(fused(lax.axis_size("seq"), lax.axis_size("tp"), args))
        return tuple(out[None] for out in outs)
    mixed_list, heard_list, seen_list, output_list = ([], [], [], [])
    cross_heads = cross_query.shape[2] // CHEAD
    mixed_list.append(video_self(video_query[0], video_key[0], video_value[0]))
    gathered_query = lax.all_gather(audio_query[0], "seq", axis=0, tiled=True)
    gathered_key = lax.all_gather(audio_key[0], "seq", axis=0, tiled=True)
    gathered_value = lax.all_gather(audio_value[0], "seq", axis=0, tiled=True)
    heard_list.append(attend(cross_query[0], gathered_key, gathered_value, cross_heads))
    audio_seen = audio_listen(gathered_query, cross_key[0], cross_value[0], cross_heads)
    seen_list.append(audio_seen)
    output_list.append(audio_block(audio_input[0], audio_seen, norm_gain, up_weight, down_weight))
    return (
        jnp.stack(mixed_list),
        jnp.stack(heard_list),
        jnp.stack(seen_list),
        jnp.stack(output_list),
    )


def solution(mesh):
    placed = (
        P(("clips", "dp"), "seq", "tp"),
        P(("clips", "dp"), "seq", "tp"),
        P(("clips", "dp"), "seq", "tp"),
        P(("clips", "dp"), "seq", "tp"),
        P(("clips", "dp"), "seq", "tp"),
        P(("clips", "dp"), "seq", "tp"),
        P(("clips", "dp"), "seq", "tp"),
        P(("clips", "dp"), "seq", "tp"),
        P(("clips", "dp"), "seq", "tp"),
        P(("clips", "dp"), "seq", None),
        P(),
        P("tp", "seq"),
        P("seq", "tp"),
    )
    return jax.shard_map(
        body,
        mesh=mesh,
        in_specs=placed,
        out_specs=(
            P(("clips", "dp"), "seq", "tp"),
            P(("clips", "dp"), "seq", "tp"),
            P(("clips", "dp"), "seq", "tp"),
            P(("clips", "dp"), "seq", "tp"),
        ),
        check_vma=False,
    )
```

```python
import functools
import math

import jax
import jax.numpy as jnp
from jax import lax
from jax.experimental import pallas as pl
from jax.experimental.pallas import tpu as pltpu
from jax.sharding import PartitionSpec as P

VHEAD = 128
CHEAD = 64
MESH = pl.DeviceIdType.MESH
LOG2E = math.log2(math.e)
CHUNKS = 4
EARLY = 3
PACE = ((1, 1, 1, 2, 2, 2, 0, 1), (0, 2, 1, 0, 1, 1, 3, 1))
ORDER = (1, 0, 2)
TURNS = (0, 0, 0, 0, 1, 0)


def dot_t(a, b):
    return lax.dot_general(a, b, (((1,), (1,)), ((), ())), preferred_element_type=jnp.float32)


def softmax_parts(q, k, scale):
    s = dot_t(q, k)
    peak = jnp.max(s, axis=1, keepdims=True)
    p = jnp.exp2((s - peak) * (scale * LOG2E))
    return p, peak * scale, jnp.sum(p, axis=1, keepdims=True)


def pair_attend(q, k, v, scale):
    low = lax.broadcasted_iota(jnp.int32, q.shape, 1) < CHEAD
    zero = jnp.zeros_like(q)
    both = jnp.concatenate([jnp.where(low, q, zero), jnp.where(low, zero, q)], axis=0)
    p, peak, total = softmax_parts(both, k, scale)
    o = jnp.dot(p.astype(jnp.bfloat16), v, preferred_element_type=jnp.float32)
    return o, peak, total


def partners(me, n):
    if n & (n - 1):
        return [lax.rem(me + d, n) for d in range(1, n)]
    found = []
    for flip in range(n - 1, 0, -1):
        place, bit = me * 0, 1
        while bit < n:
            digit = lax.rem(lax.div(me, bit), 2)
            place = place + bit * ((1 - digit) if flip & bit else digit)
            bit *= 2
        found.append(place)
    return found


def fused_kernel(
    n, tp,
    vq, vk, vv, cq, ak, av, aq, ck, cv, ai, gain, up, down,
    mixed, heard, seen, mlp,
    vbuf, obuf, abuf, cqv, ckv, cvv, upv, downv, aiv, gainv, xown, xsend, xrecv, tsend, trecv, ssbuf, nbuf, pbuf, ubuf, racc, rsend, rrecv,
    v_send, v_recv, o_send, o_recv, a_send, a_recv, x_send, x_recv, t_send, t_recv, s_send, s_recv,
    n_send, n_recv, p_send, p_recv, r_send, r_recv, own_sem, oown_sem, load_sem, ready,
):
    me = lax.axis_index("seq")
    col = lax.axis_index("tp")
    core = lax.rem(lax.axis_index("dp"), 2)
    tokens = vq.shape[0]
    hd = vq.shape[1] // VHEAD // n
    rows, width = aq.shape
    pairs = width // 128
    units = up.shape[1]
    step = units // CHUNKS
    f32, bf16 = jnp.float32, jnp.bfloat16
    peers = partners(me, n)
    tp_peers = [lax.rem(col + d, tp) for d in range(1, tp)]

    def remote(src, dst, ss, rs, where):
        copy = pltpu.make_async_remote_copy(
            src_ref=src, dst_ref=dst, send_sem=ss, recv_sem=rs, device_id=where, device_id_type=MESH
        )
        copy.start()
        return copy

    far, over, side = peers
    inner = lax.rem(lax.div(me + 1, 2), 2) == 1
    outer = jnp.logical_not(inner)
    streams = (vq, vk, vv)
    order = ORDER
    end = jnp.where(inner, over, far)
    back = (end, jnp.where(inner, far, over), side, me)
    units = [(h, i) for h in range(hd) for i in (1, 2, 0)]

    def unit(h, i, d):
        cols = pl.ds(pl.multiple_of((peers[d] * hd + h) * VHEAD, VHEAD), VHEAD)
        return pltpu.make_async_remote_copy(
            src_ref=streams[i].at[:, cols], dst_ref=vbuf.at[i, h, me], send_sem=v_send, recv_sem=v_recv.at[h],
            device_id={"seq": peers[d]}, device_id_type=MESH,
        )

    def landed(ref, sem):
        pltpu.make_async_copy(ref, ref, sem).wait()

    marks = [EARLY, EARLY]

    def pump(w):
        ends = [min(marks[c] + PACE[c][w], len(units)) if w < len(PACE[c]) else len(units) for c in range(2)]
        for k, (h, i) in enumerate(units):
            mine = [marks[c] <= k < ends[c] for c in range(2)]

            def go():
                for d in order:
                    unit(h, i, d).start()

            if all(mine):
                go()
            elif any(mine):
                pl.when(core == mine.index(True))(go)
        marks[:] = ends

    def tell(where, k):
        pl.semaphore_signal(ready.at[k], inc=1, device_id=where, device_id_type=MESH)

    barrier = pltpu.get_barrier_semaphore()
    early = units[:EARLY]

    @pl.when(inner)
    def _():
        for p in (far, side):
            pl.semaphore_signal(barrier, inc=1, device_id={"seq": p}, device_id_type=MESH)

    @pl.when(outer)
    def _():
        for t in tp_peers:
            pl.semaphore_signal(barrier, inc=1, device_id={"tp": t}, device_id_type=MESH)

    pl.semaphore_wait(barrier, jnp.where(inner, 1, tp))

    @pl.when(inner)
    def _():
        for h, i in early:
            unit(h, i, 0).start()

    @pl.when(outer)
    def _():
        tell({"seq": side}, 0)
        for t in tp_peers:
            tell({"tp": t}, 3)
        for h, i in early:
            unit(h, i, 2).start()

    loads = []
    stays = ((ck, ckv), (cv, cvv), (cq, cqv), (up, upv), (down, downv), (ai, aiv), (gain, gainv))
    stays += tuple((src, abuf.at[i, me]) for i, src in enumerate((aq, ak, av)))
    for i, (src, dst) in enumerate(stays):
        loads.append(pltpu.make_async_copy(src, dst, load_sem.at[i]))

    for i in (0, 1, 7):
        loads[i].start()

    @pl.when(inner)
    def _():
        pl.semaphore_wait(ready.at[0], 1)
        tell({"seq": far}, 1)
        pl.semaphore_wait(ready.at[1], 1)
        tell({"seq": side}, 2)

    @pl.when(outer)
    def _():
        pl.semaphore_wait(ready.at[2], 1)

    def attend_video(h):
        landed(vbuf.at[:, h, 0], own_sem.at[h])
        landed(vbuf.at[:, h, : n - 1], v_recv.at[h])
        k = vbuf[1, h].reshape(n * tokens, VHEAD)
        v = vbuf[2, h].reshape(n * tokens, VHEAD)
        cols = pl.ds(pl.multiple_of((me * hd + h) * VHEAD, VHEAD), VHEAD)
        for i, p in enumerate(back):
            w, _, total = softmax_parts(vbuf[0, h, p], k, 1.0 / math.sqrt(VHEAD))
            o = jnp.dot(w.astype(bf16), v, preferred_element_type=f32) / total
            obuf[h, p] = o.astype(bf16)
            if i < n - 1:
                remote(obuf.at[h, p], mixed.at[:, cols], o_send, o_recv, {"seq": p})
        pltpu.make_async_copy(obuf.at[h, me], mixed.at[:, cols], oown_sem).start()

    heads = list(range(hd))

    def attend_next(count):
        for h in heads[:count]:
            attend_video(h)
        del heads[:count]

    def spread(src, slots, ss, rs):
        for d, r in ((2, rs[1]), (1, rs[0])):
            remote(src, slots.at[me], ss, r, {"seq": peers[d]})

    def hand_on(slots, ss, rs):
        remote(slots.at[over], slots.at[over], ss, rs[1], {"seq": side})

    a_recvs = [(a_recv.at[0], a_recv.at[1]), (a_recv.at[2], a_recv.at[3])]
    n_recvs = (n_recv.at[0], n_recv.at[1])
    spread(aq, abuf.at[0], a_send, a_recvs[0])
    for h, i in early:

        @pl.when(inner)
        def _():
            unit(h, i, 2).start()

        @pl.when(outer)
        def _():
            unit(h, i, 0).start()

        unit(h, i, 1).start()
    for h in range(hd):
        cols = pl.ds(pl.multiple_of((me * hd + h) * VHEAD, VHEAD), VHEAD)
        for i, src in enumerate(streams):
            pltpu.make_async_copy(src.at[:, cols], vbuf.at[i, h, me], own_sem.at[h]).start()
    for copy in loads[2:7] + loads[8:]:
        copy.start()
    pump(0)
    landed(abuf.at[0, 0], a_recvs[0][0])
    hand_on(abuf.at[0], a_send, a_recvs[0])
    pump(1)

    @pl.when(outer)
    def _():
        pl.semaphore_wait(ready.at[3], tp - 1)
        tell({"seq": side}, 4)

    for copy in loads[:2] + loads[5:]:
        copy.wait()
    landed(abuf.at[0, : n - 2], a_recvs[0][1])

    def whole(i):
        return jnp.concatenate([abuf[i, s].astype(f32) for s in range(n)], axis=0).astype(bf16)

    scale = 1.0 / math.sqrt(CHEAD)
    total_rows = n * rows
    q_all = whole(0)
    lane = lax.broadcasted_iota(jnp.int32, (total_rows, 128), 1)
    stats = jnp.ones((total_rows, 128), f32)
    for j in range(pairs):
        at = slice(j * 128, (j + 1) * 128)
        o, peak, total = pair_attend(q_all[:, at], ckv[:, at], cvv[:, at], scale)
        picked = jnp.where(lane < CHEAD, o[:total_rows], o[total_rows:])
        xown[:, :, at] = picked.reshape(n, rows, 128)
        for half in range(2):
            part = slice(half * total_rows, (half + 1) * total_rows)
            stats = jnp.where(lane == 2 * j + half, peak[part], stats)
            stats = jnp.where(lane == 64 + 2 * j + half, total[part], stats)
    tsend[...] = stats.reshape(n, rows, 128)

    def send_part(d, slot, k):
        r, where = min(k, 1), {"seq": peers[d]}
        remote(tsend.at[slot], trecv.at[k], t_send, t_recv.at[r], where)
        remote(xsend.at[k], xrecv.at[k], x_send, x_recv.at[r], where)

    xsend[0] = xown[far].astype(bf16)
    send_part(2, far, 0)
    xsend[1] = xown[side].astype(bf16)
    send_part(2, side, 1)
    place = lax.broadcasted_iota(jnp.int32, (rows, 128), 1)

    def weigh(stats):
        peak = functools.reduce(jnp.maximum, stats)
        factors = [jnp.exp(t - peak) for t in stats]
        return peak, factors, sum(f * pltpu.roll(t, 64, 1) for f, t in zip(factors, stats))

    def blend(factors, blocks):
        pieces = []
        for j in range(pairs):
            at = slice(j * 128, (j + 1) * 128)
            terms = [
                jnp.where(place < CHEAD, f[:, 2 * j : 2 * j + 1], f[:, 2 * j + 1 : 2 * j + 2]) * b[:, at].astype(f32)
                for f, b in zip(factors, blocks)
            ]
            pieces.append(sum(terms[1:], terms[0]))
        return jnp.concatenate(pieces, axis=1).astype(bf16)

    pump(2)

    landed(trecv.at[0], t_recv.at[0])
    landed(xrecv.at[0], x_recv.at[0])
    peak, factors, total = weigh([tsend[over], trecv[0]])
    xsend[2] = blend(factors, [xown[over], xrecv[0]])
    tsend[over] = jnp.where(place < 64, peak, pltpu.roll(total, 64, 1))
    send_part(1, over, 2)

    pump(3)
    attend_next(TURNS[0])

    landed(trecv.at[1:], t_recv.at[1])
    landed(xrecv.at[1:], x_recv.at[1])
    _, factors, total = weigh([tsend[me], trecv[1], trecv[2]])
    seen_bf = blend([f / total for f in factors], [xown[me], xrecv[1], xrecv[2]])
    seen[...] = seen_bf

    mine = pl.ds(pl.multiple_of(col * width, 128), width)
    residual = aiv[:, mine].astype(f32) + seen_bf.astype(f32)
    square = jnp.sum(residual * residual, axis=1, keepdims=True)
    first = square.astype(bf16).astype(f32)
    second = (square - first).astype(bf16).astype(f32)
    third = square - first - second
    split = jnp.where(place == 0, first, jnp.where(place == 1, second, jnp.where(place == 2, third, 0.0)))
    nbuf[me, :, :width] = (residual * gainv[:, mine]).astype(bf16)
    nbuf[me, :, width:] = split.astype(bf16)
    spread(nbuf.at[me], nbuf, n_send, n_recvs)
    for i, src in enumerate((ak, av)):
        spread(src, abuf.at[i + 1], a_send, a_recvs[1])
    pump(4)
    attend_next(TURNS[1])
    landed(nbuf.at[0], n_recvs[0])
    hand_on(nbuf, n_send, n_recvs)
    pump(5)
    attend_next(TURNS[2])

    loads[3].wait()
    landed(nbuf.at[: n - 2], n_recvs[1])
    held = jnp.concatenate([nbuf[s].astype(f32) for s in range(n)], axis=0)
    x = held[:, :width].astype(bf16)
    square = jnp.sum(held[:, width:], axis=1, keepdims=True)
    ssbuf[col] = jnp.broadcast_to(square, (total_rows, 128))
    partials = []

    @pl.when(inner)
    def _():
        pl.semaphore_wait(ready.at[4], 1)

    for d, t in enumerate(tp_peers):
        partials.append(remote(ssbuf.at[col], ssbuf.at[col], s_send.at[d], s_recv.at[d], {"tp": t}))
    for c in range(CHUNKS):
        ubuf[c] = jnp.dot(x, upv[:, c * step : (c + 1) * step], preferred_element_type=f32)
        pbuf[col, c] = ubuf[c].astype(bf16)
        for d, t in enumerate(tp_peers):
            partials.append(
                remote(pbuf.at[col, c], pbuf.at[col, c], p_send, p_recv.at[c, d], {"tp": t})
            )
    landed(abuf.at[1:, 0], a_recvs[1][0])
    for i in (1, 2):
        hand_on(abuf.at[i], a_send, a_recvs[1])
    pump(6)
    attend_next(TURNS[3])

    loads[4].wait()
    for copy in partials[: tp - 1]:
        copy.wait_recv()
    square = sum(ssbuf[t] for t in range(tp))[:, 0:1]
    factor = lax.rsqrt(square / (width * tp) + 1e-6)
    acc = jnp.zeros((total_rows, width), f32)
    for c in range(CHUNKS):
        for copy in partials[(c + 1) * (tp - 1) : (c + 2) * (tp - 1)]:
            copy.wait_recv()
        up_sum = (ubuf[c] + sum(pbuf[t, c].astype(f32) for t in tp_peers)) * factor
        hidden = jax.nn.gelu(up_sum, approximate=True).astype(bf16)
        acc += jnp.dot(hidden, downv[c * step : (c + 1) * step, :], preferred_element_type=f32)
    racc[...] = acc.reshape(n, rows, width)

    def send_sum(d, k):
        remote(rsend.at[k], rrecv.at[k], r_send, r_recv.at[min(k, 1)], {"seq": peers[d]})

    rsend[0] = racc[far].astype(bf16)
    send_sum(2, 0)
    rsend[1] = racc[side].astype(bf16)
    send_sum(2, 1)
    pump(7)

    attend_next(TURNS[4])
    landed(rrecv.at[0], r_recv.at[0])
    rsend[2] = (racc[over] + rrecv[0].astype(f32)).astype(bf16)
    send_sum(1, 2)
    pump(8)
    attend_next(TURNS[5])

    loads[2].wait()
    landed(abuf.at[1:, : n - 2], a_recvs[1][1])
    k_all, v_all = whole(1), whole(2)
    wide = lax.broadcasted_iota(jnp.int32, (tokens, 128), 1)
    for j in range(pairs):
        at = slice(j * 128, (j + 1) * 128)
        o, _, total = pair_attend(cqv[:, at], k_all[:, at], v_all[:, at], scale)
        o = o / total
        heard[:, at] = jnp.where(wide < CHEAD, o[:tokens], o[tokens:]).astype(bf16)

    attend_next(len(heads) - 1)

    landed(rrecv.at[1:], r_recv.at[1])
    mlp[...] = (racc[me] + rrecv[1].astype(f32) + rrecv[2].astype(f32)).astype(bf16)

    attend_next(len(heads))

    for ref, sem in (
        (vbuf.at[:, :, : n - 1], v_send),
        (abuf.at[:, : n - 1], a_send),
        (xsend, x_send),
        (trecv, t_send),
        (nbuf.at[: n - 1], n_send),
        (rsend, r_send),
    ):
        landed(ref, sem)
    if tp > 1:
        landed(pbuf.at[: tp - 1], p_send)
    for copy in partials[: tp - 1]:
        copy.wait_send()
    landed(mixed.at[:, : hd * VHEAD], oown_sem)
    landed(obuf.at[:, : n - 1], o_send)
    landed(mixed.at[:, : (n - 1) * hd * VHEAD], o_recv)


def fused(n, tp, args):
    vq, vk, vv, cq, ak, av, aq, ck, cv, ai, gain, up, down = args
    tokens, vwidth = vq.shape
    hd = vwidth // VHEAD // n
    rows, width = aq.shape
    units = up.shape[1]
    bf16, f32 = jnp.bfloat16, jnp.float32
    anywhere = pl.BlockSpec(memory_space=pl.ANY)
    dma = pltpu.SemaphoreType.DMA
    head = pltpu.VMEM((hd, n, tokens, VHEAD), bf16)
    cross = pltpu.VMEM((tokens, width), bf16)
    one, t = dma, max(tp - 1, 1)
    return pl.pallas_call(
        functools.partial(fused_kernel, n, tp),
        out_shape=(
            pltpu.VMEM((tokens, vwidth), bf16),
            pltpu.VMEM((tokens, width), bf16),
            pltpu.VMEM((rows, width), bf16),
            pltpu.VMEM((rows, width), bf16),
        ),
        in_specs=[anywhere] * 13,
        out_specs=(pl.BlockSpec(memory_space=pltpu.VMEM),) * 4,
        scratch_shapes=[
            pltpu.VMEM((3, hd, n, tokens, VHEAD), bf16), head,
            pltpu.VMEM((3, n, rows, width), bf16),
            cross, cross, cross,
            pltpu.VMEM(up.shape, bf16),
            pltpu.VMEM(down.shape, bf16),
            pltpu.VMEM(ai.shape, bf16),
            pltpu.VMEM((1, gain.shape[0]), f32),
            pltpu.VMEM((n, rows, width), f32),
            pltpu.VMEM((3, rows, width), bf16),
            pltpu.VMEM((3, rows, width), bf16),
            pltpu.VMEM((n, rows, 128), f32),
            pltpu.VMEM((3, rows, 128), f32),
            pltpu.VMEM((tp, n * rows, 128), f32),
            pltpu.VMEM((n, rows, width + 128), bf16),
            pltpu.VMEM((tp, CHUNKS, n * rows, units // CHUNKS), bf16),
            pltpu.VMEM((CHUNKS, n * rows, units // CHUNKS), f32),
            pltpu.VMEM((n, rows, width), f32),
            pltpu.VMEM((3, rows, width), bf16),
            pltpu.VMEM((3, rows, width), bf16),
            one, dma((hd,)), one, one, one, dma((4,)), one, dma((2,)), one, dma((2,)), dma((t,)), dma((t,)),
            one, dma((2,)), one, dma((CHUNKS, t)), one, dma((2,)),
            dma((hd,)), one, dma((10,)), pltpu.SemaphoreType.REGULAR((5,)),
        ],
        compiler_params=pltpu.CompilerParams(collective_id=0, has_side_effects=True),
    )(vq, vk, vv, cq, ak, av, aq, ck, cv, ai, gain.reshape(1, -1), up, down)


def hand_over(*refs):
    count = (len(refs) - 1) // 2
    copies = [pltpu.make_async_copy(refs[i], refs[count + i], refs[-1].at[i]) for i in range(count)]
    for copy in copies:
        copy.start()
    for copy in copies:
        copy.wait()


def deliver(arrays):
    arrays = [pltpu.with_memory_space_constraint(a, pltpu.VMEM) for a in arrays]
    return pl.pallas_call(
        hand_over,
        out_shape=tuple(jax.ShapeDtypeStruct(a.shape, a.dtype) for a in arrays),
        in_specs=[pl.BlockSpec(memory_space=pltpu.VMEM)] * len(arrays),
        out_specs=(pl.BlockSpec(memory_space=pl.ANY),) * len(arrays),
        scratch_shapes=[pltpu.SemaphoreType.DMA((len(arrays),))],
    )(*arrays)


def fits(n, vq, aq, up):
    heads = vq.shape[2] // VHEAD
    return (
        n == 4
        and heads % n == 0
        and vq.shape[1] % 16 == 0
        and aq.shape[1] % 8 == 0
        and aq.shape[2] % 128 == 0
        and aq.shape[2] // CHEAD <= 64
        and up.shape[0] == aq.shape[2]
        and up.shape[1] % (128 * CHUNKS) == 0
    )


def attend_rows(queries, keys_in, values_in, head_count):
    head_size = queries.shape[1] // head_count
    query_heads = queries.reshape(queries.shape[0], head_count, head_size)
    key_heads = keys_in.reshape(keys_in.shape[0], head_count, head_size)
    value_heads = values_in.reshape(values_in.shape[0], head_count, head_size)
    scores = jnp.einsum(
        "qhd,khd->qhk", query_heads, key_heads, preferred_element_type=jnp.float32
    ) / math.sqrt(head_size)
    peak_value = jnp.max(scores, axis=2, keepdims=True)
    weights = jnp.exp(scores - peak_value)
    totals = jnp.sum(weights, axis=2)
    weighted = jnp.einsum(
        "qhk,khd->qhd",
        weights.astype(jnp.bfloat16),
        value_heads,
        preferred_element_type=jnp.float32,
    )
    result = weighted / totals[:, :, None]
    return result.reshape(queries.shape[0], head_count * head_size).astype(jnp.bfloat16)


def attend(queries, keys_in, values_in, head_count):
    row_total = queries.shape[0]
    block_rows = 512 if row_total % 512 == 0 else row_total
    pieces = queries.reshape(row_total // block_rows, block_rows, queries.shape[1])
    result = lax.map(
        lambda row_piece: attend_rows(row_piece, keys_in, values_in, head_count), pieces
    )
    return result.reshape(row_total, queries.shape[1])


def video_self(queries, keys_in, values_in):
    seq_count = lax.axis_size("seq")
    local_heads = queries.shape[1] // VHEAD
    dest_heads = max(local_heads // seq_count, 1)
    blocks = seq_count * dest_heads // local_heads
    groups = local_heads // dest_heads
    group_width = dest_heads * VHEAD
    token_count = queries.shape[0]
    block_tokens = token_count // blocks

    def spread(tensor):
        shaped = tensor.reshape(token_count, groups, group_width).transpose(1, 0, 2)
        shaped = jnp.broadcast_to(shaped[:, None], (groups, blocks, token_count, group_width))
        return shaped.reshape(seq_count, token_count, group_width)

    shaped = queries.reshape(blocks, block_tokens, groups, group_width).transpose(2, 0, 1, 3)
    own_queries = lax.all_to_all(
        shaped.reshape(seq_count, block_tokens, group_width),
        "seq",
        split_axis=0,
        concat_axis=0,
        tiled=True,
    )
    keys_all = lax.all_to_all(spread(keys_in), "seq", split_axis=0, concat_axis=0, tiled=True)
    values_all = lax.all_to_all(spread(values_in), "seq", split_axis=0, concat_axis=0, tiled=True)
    keys_all = keys_all.reshape(-1, group_width)
    values_all = values_all.reshape(-1, group_width)
    own_queries = own_queries.reshape(-1, group_width)
    attended = attend(own_queries, keys_all, values_all, dest_heads)
    returned = lax.all_to_all(
        attended.reshape(seq_count, block_tokens, group_width),
        "seq",
        split_axis=0,
        concat_axis=0,
        tiled=True,
    )
    returned = returned.reshape(groups, blocks, block_tokens, group_width).transpose(1, 2, 0, 3)
    return returned.reshape(token_count, groups * group_width)


def audio_listen(queries, keys_in, values_in, head_count):
    head_size = queries.shape[1] // head_count
    query_heads = queries.reshape(queries.shape[0], head_count, head_size)
    key_heads = keys_in.reshape(keys_in.shape[0], head_count, head_size)
    value_heads = values_in.reshape(values_in.shape[0], head_count, head_size)
    scores = jnp.einsum(
        "qhd,khd->qhk", query_heads, key_heads, preferred_element_type=jnp.float32
    ) / math.sqrt(head_size)
    local_peak = jnp.max(scores, axis=2)
    peak_value = lax.pmax(local_peak, "seq")
    weights = jnp.exp(scores - peak_value[:, :, None])
    totals = jnp.sum(weights, axis=2)
    weighted = jnp.einsum(
        "qhk,khd->qhd",
        weights.astype(jnp.bfloat16),
        value_heads,
        preferred_element_type=jnp.float32,
    )
    totals, weighted = (totals, weighted.reshape(queries.shape[0], head_count * head_size))
    totals, weighted = (
        lax.psum_scatter(totals, "seq", scatter_dimension=0, tiled=True),
        lax.psum_scatter(weighted, "seq", scatter_dimension=0, tiled=True),
    )
    return (weighted / jnp.repeat(totals, head_size, axis=1)).astype(jnp.bfloat16)


def audio_block(audio_rows, audio_seen, norm_gain, up_weight, down_weight):
    features = lax.all_gather(audio_seen, "tp", axis=1, tiled=True)
    residual = audio_rows.astype(jnp.float32) + features.astype(jnp.float32)
    scale_factor = lax.rsqrt(jnp.mean(residual * residual, axis=1, keepdims=True) + 1e-06)
    normed = (residual * scale_factor * norm_gain).astype(jnp.bfloat16)
    slice_width = up_weight.shape[0]
    own_features = lax.dynamic_slice_in_dim(
        normed, lax.axis_index("tp") * slice_width, slice_width, 1
    )
    partial_sum = jnp.dot(
        lax.all_gather(own_features, "seq", axis=0, tiled=True),
        up_weight,
        preferred_element_type=jnp.float32,
    )
    hidden = jax.nn.gelu(lax.psum(partial_sum, "tp")).astype(jnp.bfloat16)
    return lax.psum_scatter(
        jnp.dot(hidden, down_weight, preferred_element_type=jnp.float32),
        "seq",
        scatter_dimension=0,
        tiled=True,
    ).astype(jnp.bfloat16)


def body(
    video_query,
    video_key,
    video_value,
    cross_query,
    audio_key,
    audio_value,
    audio_query,
    cross_key,
    cross_value,
    audio_input,
    norm_gain,
    up_weight,
    down_weight,
):
    if fits(lax.axis_size("seq"), video_query, audio_query, up_weight):
        args = (video_query, video_key, video_value, cross_query, audio_key, audio_value)
        args += (audio_query, cross_key, cross_value, audio_input)
        args = tuple(a[0] for a in args) + (norm_gain, up_weight, down_weight)
        outs = deliver(fused(lax.axis_size("seq"), lax.axis_size("tp"), args))
        return tuple(out[None] for out in outs)
    mixed_list, heard_list, seen_list, output_list = ([], [], [], [])
    cross_heads = cross_query.shape[2] // CHEAD
    mixed_list.append(video_self(video_query[0], video_key[0], video_value[0]))
    gathered_query = lax.all_gather(audio_query[0], "seq", axis=0, tiled=True)
    gathered_key = lax.all_gather(audio_key[0], "seq", axis=0, tiled=True)
    gathered_value = lax.all_gather(audio_value[0], "seq", axis=0, tiled=True)
    heard_list.append(attend(cross_query[0], gathered_key, gathered_value, cross_heads))
    audio_seen = audio_listen(gathered_query, cross_key[0], cross_value[0], cross_heads)
    seen_list.append(audio_seen)
    output_list.append(audio_block(audio_input[0], audio_seen, norm_gain, up_weight, down_weight))
    return (
        jnp.stack(mixed_list),
        jnp.stack(heard_list),
        jnp.stack(seen_list),
        jnp.stack(output_list),
    )


def solution(mesh):
    placed = (
        P(("clips", "dp"), "seq", "tp"),
        P(("clips", "dp"), "seq", "tp"),
        P(("clips", "dp"), "seq", "tp"),
        P(("clips", "dp"), "seq", "tp"),
        P(("clips", "dp"), "seq", "tp"),
        P(("clips", "dp"), "seq", "tp"),
        P(("clips", "dp"), "seq", "tp"),
        P(("clips", "dp"), "seq", "tp"),
        P(("clips", "dp"), "seq", "tp"),
        P(("clips", "dp"), "seq", None),
        P(),
        P("tp", "seq"),
        P("seq", "tp"),
    )
    return jax.shard_map(
        body,
        mesh=mesh,
        in_specs=placed,
        out_specs=(
            P(("clips", "dp"), "seq", "tp"),
            P(("clips", "dp"), "seq", "tp"),
            P(("clips", "dp"), "seq", "tp"),
            P(("clips", "dp"), "seq", "tp"),
        ),
        check_vma=False,
    )
```

```python
import functools
import math

import jax
import jax.numpy as jnp
from jax import lax
from jax.experimental import pallas as pl
from jax.experimental.pallas import tpu as pltpu
from jax.sharding import PartitionSpec as P

VHEAD = 128
CHEAD = 64
MESH = pl.DeviceIdType.MESH
LOG2E = math.log2(math.e)
CHUNKS = 4
EARLY = 3
PACE = ((1, 1, 1, 2, 2, 2, 0, 1), (0, 2, 1, 0, 1, 1, 3, 1))
ORDER = (1, 0, 2)
LATE = 1
TURNS = (0, 0, 0, 0, 1, 0)


def dot_t(a, b):
    return lax.dot_general(a, b, (((1,), (1,)), ((), ())), preferred_element_type=jnp.float32)


def softmax_parts(q, k, scale):
    s = dot_t(q, k)
    peak = jnp.max(s, axis=1, keepdims=True)
    p = jnp.exp2((s - peak) * (scale * LOG2E))
    return p, peak * scale, jnp.sum(p, axis=1, keepdims=True)


def pair_attend(q, k, v, scale):
    low = lax.broadcasted_iota(jnp.int32, q.shape, 1) < CHEAD
    zero = jnp.zeros_like(q)
    both = jnp.concatenate([jnp.where(low, q, zero), jnp.where(low, zero, q)], axis=0)
    p, peak, total = softmax_parts(both, k, scale)
    o = jnp.dot(p.astype(jnp.bfloat16), v, preferred_element_type=jnp.float32)
    return o, peak, total


def partners(me, n):
    if n & (n - 1):
        return [lax.rem(me + d, n) for d in range(1, n)]
    found = []
    for flip in range(n - 1, 0, -1):
        place, bit = me * 0, 1
        while bit < n:
            digit = lax.rem(lax.div(me, bit), 2)
            place = place + bit * ((1 - digit) if flip & bit else digit)
            bit *= 2
        found.append(place)
    return found


def fused_kernel(
    n, tp,
    vq, vk, vv, cq, ak, av, aq, ck, cv, ai, gain, up, down,
    mixed, heard, seen, mlp,
    vbuf, obuf, abuf, cqv, ckv, cvv, upv, downv, aiv, gainv, xown, xsend, xrecv, tsend, trecv, ssbuf, nbuf, pbuf, ubuf, racc, rsend, rrecv,
    v_send, v_recv, o_send, o_recv, a_send, a_recv, x_send, x_recv, t_send, t_recv, s_send, s_recv,
    n_send, n_recv, p_send, p_recv, r_send, r_recv, own_sem, oown_sem, load_sem, ready,
):
    me = lax.axis_index("seq")
    col = lax.axis_index("tp")
    core = lax.rem(lax.axis_index("dp"), 2)
    tokens = vq.shape[0]
    hd = vq.shape[1] // VHEAD // n
    rows, width = aq.shape
    pairs = width // 128
    units = up.shape[1]
    step = units // CHUNKS
    f32, bf16 = jnp.float32, jnp.bfloat16
    peers = partners(me, n)
    tp_peers = [lax.rem(col + d, tp) for d in range(1, tp)]

    def remote(src, dst, ss, rs, where):
        copy = pltpu.make_async_remote_copy(
            src_ref=src, dst_ref=dst, send_sem=ss, recv_sem=rs, device_id=where, device_id_type=MESH
        )
        copy.start()
        return copy

    far, over, side = peers
    inner = lax.rem(lax.div(me + 1, 2), 2) == 1
    outer = jnp.logical_not(inner)
    streams = (vq, vk, vv)
    order = ORDER
    end = jnp.where(inner, over, far)
    back = (end, jnp.where(inner, far, over), side, me)
    units = [(h, i) for h in range(hd) for i in (1, 2, 0)]

    def unit(h, i, d):
        cols = pl.ds(pl.multiple_of((peers[d] * hd + h) * VHEAD, VHEAD), VHEAD)
        return pltpu.make_async_remote_copy(
            src_ref=streams[i].at[:, cols], dst_ref=vbuf.at[i, h, me], send_sem=v_send, recv_sem=v_recv.at[h],
            device_id={"seq": peers[d]}, device_id_type=MESH,
        )

    def landed(ref, sem):
        pltpu.make_async_copy(ref, ref, sem).wait()

    marks = [EARLY, EARLY]

    def pump(w):
        ends = [min(marks[c] + PACE[c][w], len(units)) if w < len(PACE[c]) else len(units) for c in range(2)]
        for k, (h, i) in enumerate(units):
            mine = [marks[c] <= k < ends[c] for c in range(2)]

            def go():
                for d in order:
                    unit(h, i, d).start()

            if all(mine):
                go()
            elif any(mine):
                pl.when(core == mine.index(True))(go)
        marks[:] = ends

    def tell(where, k):
        pl.semaphore_signal(ready.at[k], inc=1, device_id=where, device_id_type=MESH)

    barrier = pltpu.get_barrier_semaphore()
    early = units[:EARLY]

    @pl.when(inner)
    def _():
        for p in (far, side):
            pl.semaphore_signal(barrier, inc=1, device_id={"seq": p}, device_id_type=MESH)

    @pl.when(outer)
    def _():
        for t in tp_peers:
            pl.semaphore_signal(barrier, inc=1, device_id={"tp": t}, device_id_type=MESH)

    pl.semaphore_wait(barrier, jnp.where(inner, 1, tp))

    @pl.when(inner)
    def _():
        for h, i in early:
            unit(h, i, 0).start()

    @pl.when(outer)
    def _():
        tell({"seq": side}, 0)
        for t in tp_peers:
            tell({"tp": t}, 3)
        for h, i in early:
            unit(h, i, 2).start()

    loads = []
    stays = ((ck, ckv), (cv, cvv), (cq, cqv), (up, upv), (down, downv), (ai, aiv), (gain, gainv))
    stays += tuple((src, abuf.at[i, me]) for i, src in enumerate((aq, ak, av)))
    for i, (src, dst) in enumerate(stays):
        loads.append(pltpu.make_async_copy(src, dst, load_sem.at[i]))

    for i in (0, 1, 7):
        loads[i].start()

    @pl.when(inner)
    def _():
        pl.semaphore_wait(ready.at[0], 1)
        tell({"seq": far}, 1)
        pl.semaphore_wait(ready.at[1], 1)
        tell({"seq": side}, 2)

    @pl.when(outer)
    def _():
        pl.semaphore_wait(ready.at[2], 1)

    kept = []

    def give(h, p, cols):
        remote(obuf.at[h, p], mixed.at[:, cols], o_send, o_recv, {"seq": p})

    def attend_video(h):
        landed(vbuf.at[:, h, 0], own_sem.at[h])
        landed(vbuf.at[:, h, : n - 1], v_recv.at[h])
        k = vbuf[1, h].reshape(n * tokens, VHEAD)
        v = vbuf[2, h].reshape(n * tokens, VHEAD)
        cols = pl.ds(pl.multiple_of((me * hd + h) * VHEAD, VHEAD), VHEAD)
        for i, p in enumerate(back):
            w, _, total = softmax_parts(vbuf[0, h, p], k, 1.0 / math.sqrt(VHEAD))
            o = jnp.dot(w.astype(bf16), v, preferred_element_type=f32) / total
            obuf[h, p] = o.astype(bf16)
            if i == 1 and LATE <= h < hd - 1:
                kept.append((h, p, cols))
            elif i < n - 1:
                give(h, p, cols)
            if i == 0 and h == hd - 1:
                for later in kept:
                    give(*later)
        pltpu.make_async_copy(obuf.at[h, me], mixed.at[:, cols], oown_sem).start()

    heads = list(range(hd))

    def attend_next(count):
        for h in heads[:count]:
            attend_video(h)
        del heads[:count]

    def spread(src, slots, ss, rs):
        for d, r in ((2, rs[1]), (1, rs[0])):
            remote(src, slots.at[me], ss, r, {"seq": peers[d]})

    def hand_on(slots, ss, rs):
        remote(slots.at[over], slots.at[over], ss, rs[1], {"seq": side})

    a_recvs = [(a_recv.at[0], a_recv.at[1]), (a_recv.at[2], a_recv.at[3])]
    n_recvs = (n_recv.at[0], n_recv.at[1])
    spread(aq, abuf.at[0], a_send, a_recvs[0])
    for h, i in early:

        @pl.when(inner)
        def _():
            unit(h, i, 2).start()

        @pl.when(outer)
        def _():
            unit(h, i, 0).start()

        unit(h, i, 1).start()
    for h in range(hd):
        cols = pl.ds(pl.multiple_of((me * hd + h) * VHEAD, VHEAD), VHEAD)
        for i, src in enumerate(streams):
            pltpu.make_async_copy(src.at[:, cols], vbuf.at[i, h, me], own_sem.at[h]).start()
    for copy in loads[2:7] + loads[8:]:
        copy.start()
    pump(0)
    landed(abuf.at[0, 0], a_recvs[0][0])
    hand_on(abuf.at[0], a_send, a_recvs[0])
    pump(1)

    @pl.when(outer)
    def _():
        pl.semaphore_wait(ready.at[3], tp - 1)
        tell({"seq": side}, 4)

    for copy in loads[:2] + loads[5:]:
        copy.wait()
    landed(abuf.at[0, : n - 2], a_recvs[0][1])

    def whole(i):
        return jnp.concatenate([abuf[i, s].astype(f32) for s in range(n)], axis=0).astype(bf16)

    scale = 1.0 / math.sqrt(CHEAD)
    total_rows = n * rows
    q_all = whole(0)
    lane = lax.broadcasted_iota(jnp.int32, (total_rows, 128), 1)
    stats = jnp.ones((total_rows, 128), f32)
    for j in range(pairs):
        at = slice(j * 128, (j + 1) * 128)
        o, peak, total = pair_attend(q_all[:, at], ckv[:, at], cvv[:, at], scale)
        picked = jnp.where(lane < CHEAD, o[:total_rows], o[total_rows:])
        xown[:, :, at] = picked.reshape(n, rows, 128)
        for half in range(2):
            part = slice(half * total_rows, (half + 1) * total_rows)
            stats = jnp.where(lane == 2 * j + half, peak[part], stats)
            stats = jnp.where(lane == 64 + 2 * j + half, total[part], stats)
    tsend[...] = stats.reshape(n, rows, 128)

    def send_part(d, slot, k):
        r, where = min(k, 1), {"seq": peers[d]}
        remote(tsend.at[slot], trecv.at[k], t_send, t_recv.at[r], where)
        remote(xsend.at[k], xrecv.at[k], x_send, x_recv.at[r], where)

    xsend[0] = xown[far].astype(bf16)
    send_part(2, far, 0)
    xsend[1] = xown[side].astype(bf16)
    send_part(2, side, 1)
    place = lax.broadcasted_iota(jnp.int32, (rows, 128), 1)

    def weigh(stats):
        peak = functools.reduce(jnp.maximum, stats)
        factors = [jnp.exp(t - peak) for t in stats]
        return peak, factors, sum(f * pltpu.roll(t, 64, 1) for f, t in zip(factors, stats))

    def blend(factors, blocks):
        pieces = []
        for j in range(pairs):
            at = slice(j * 128, (j + 1) * 128)
            terms = [
                jnp.where(place < CHEAD, f[:, 2 * j : 2 * j + 1], f[:, 2 * j + 1 : 2 * j + 2]) * b[:, at].astype(f32)
                for f, b in zip(factors, blocks)
            ]
            pieces.append(sum(terms[1:], terms[0]))
        return jnp.concatenate(pieces, axis=1).astype(bf16)

    pump(2)

    landed(trecv.at[0], t_recv.at[0])
    landed(xrecv.at[0], x_recv.at[0])
    peak, factors, total = weigh([tsend[over], trecv[0]])
    xsend[2] = blend(factors, [xown[over], xrecv[0]])
    tsend[over] = jnp.where(place < 64, peak, pltpu.roll(total, 64, 1))
    send_part(1, over, 2)

    pump(3)
    attend_next(TURNS[0])

    landed(trecv.at[1:], t_recv.at[1])
    landed(xrecv.at[1:], x_recv.at[1])
    _, factors, total = weigh([tsend[me], trecv[1], trecv[2]])
    seen_bf = blend([f / total for f in factors], [xown[me], xrecv[1], xrecv[2]])
    seen[...] = seen_bf

    mine = pl.ds(pl.multiple_of(col * width, 128), width)
    residual = aiv[:, mine].astype(f32) + seen_bf.astype(f32)
    square = jnp.sum(residual * residual, axis=1, keepdims=True)
    first = square.astype(bf16).astype(f32)
    second = (square - first).astype(bf16).astype(f32)
    third = square - first - second
    split = jnp.where(place == 0, first, jnp.where(place == 1, second, jnp.where(place == 2, third, 0.0)))
    nbuf[me, :, :width] = (residual * gainv[:, mine]).astype(bf16)
    nbuf[me, :, width:] = split.astype(bf16)
    spread(nbuf.at[me], nbuf, n_send, n_recvs)
    for i, src in enumerate((ak, av)):
        spread(src, abuf.at[i + 1], a_send, a_recvs[1])
    pump(4)
    attend_next(TURNS[1])
    landed(nbuf.at[0], n_recvs[0])
    hand_on(nbuf, n_send, n_recvs)
    pump(5)
    attend_next(TURNS[2])

    loads[3].wait()
    landed(nbuf.at[: n - 2], n_recvs[1])
    held = jnp.concatenate([nbuf[s].astype(f32) for s in range(n)], axis=0)
    x = held[:, :width].astype(bf16)
    square = jnp.sum(held[:, width:], axis=1, keepdims=True)
    ssbuf[col] = jnp.broadcast_to(square, (total_rows, 128))
    partials = []

    @pl.when(inner)
    def _():
        pl.semaphore_wait(ready.at[4], 1)

    for d, t in enumerate(tp_peers):
        partials.append(remote(ssbuf.at[col], ssbuf.at[col], s_send.at[d], s_recv.at[d], {"tp": t}))
    for c in range(CHUNKS):
        ubuf[c] = jnp.dot(x, upv[:, c * step : (c + 1) * step], preferred_element_type=f32)
        pbuf[col, c] = ubuf[c].astype(bf16)
        for d, t in enumerate(tp_peers):
            partials.append(
                remote(pbuf.at[col, c], pbuf.at[col, c], p_send, p_recv.at[c, d], {"tp": t})
            )
    landed(abuf.at[1:, 0], a_recvs[1][0])
    for i in (1, 2):
        hand_on(abuf.at[i], a_send, a_recvs[1])
    pump(6)
    attend_next(TURNS[3])

    loads[4].wait()
    for copy in partials[: tp - 1]:
        copy.wait_recv()
    square = sum(ssbuf[t] for t in range(tp))[:, 0:1]
    factor = lax.rsqrt(square / (width * tp) + 1e-6)
    acc = jnp.zeros((total_rows, width), f32)
    for c in range(CHUNKS):
        for copy in partials[(c + 1) * (tp - 1) : (c + 2) * (tp - 1)]:
            copy.wait_recv()
        up_sum = (ubuf[c] + sum(pbuf[t, c].astype(f32) for t in tp_peers)) * factor
        hidden = jax.nn.gelu(up_sum, approximate=True).astype(bf16)
        acc += jnp.dot(hidden, downv[c * step : (c + 1) * step, :], preferred_element_type=f32)
    racc[...] = acc.reshape(n, rows, width)

    def send_sum(d, k):
        remote(rsend.at[k], rrecv.at[k], r_send, r_recv.at[min(k, 1)], {"seq": peers[d]})

    rsend[0] = racc[far].astype(bf16)
    send_sum(2, 0)
    rsend[1] = racc[side].astype(bf16)
    send_sum(2, 1)
    pump(7)

    attend_next(TURNS[4])
    landed(rrecv.at[0], r_recv.at[0])
    rsend[2] = (racc[over] + rrecv[0].astype(f32)).astype(bf16)
    send_sum(1, 2)
    pump(8)
    attend_next(TURNS[5])

    loads[2].wait()
    landed(abuf.at[1:, : n - 2], a_recvs[1][1])
    k_all, v_all = whole(1), whole(2)
    wide = lax.broadcasted_iota(jnp.int32, (tokens, 128), 1)
    for j in range(pairs):
        at = slice(j * 128, (j + 1) * 128)
        o, _, total = pair_attend(cqv[:, at], k_all[:, at], v_all[:, at], scale)
        o = o / total
        heard[:, at] = jnp.where(wide < CHEAD, o[:tokens], o[tokens:]).astype(bf16)

    attend_next(len(heads) - 1)

    landed(rrecv.at[1:], r_recv.at[1])
    mlp[...] = (racc[me] + rrecv[1].astype(f32) + rrecv[2].astype(f32)).astype(bf16)

    attend_next(len(heads))

    for ref, sem in (
        (vbuf.at[:, :, : n - 1], v_send),
        (abuf.at[:, : n - 1], a_send),
        (xsend, x_send),
        (trecv, t_send),
        (nbuf.at[: n - 1], n_send),
        (rsend, r_send),
    ):
        landed(ref, sem)
    if tp > 1:
        landed(pbuf.at[: tp - 1], p_send)
    for copy in partials[: tp - 1]:
        copy.wait_send()
    landed(mixed.at[:, : hd * VHEAD], oown_sem)
    landed(obuf.at[:, : n - 1], o_send)
    landed(mixed.at[:, : (n - 1) * hd * VHEAD], o_recv)


def fused(n, tp, args):
    vq, vk, vv, cq, ak, av, aq, ck, cv, ai, gain, up, down = args
    tokens, vwidth = vq.shape
    hd = vwidth // VHEAD // n
    rows, width = aq.shape
    units = up.shape[1]
    bf16, f32 = jnp.bfloat16, jnp.float32
    anywhere = pl.BlockSpec(memory_space=pl.ANY)
    dma = pltpu.SemaphoreType.DMA
    head = pltpu.VMEM((hd, n, tokens, VHEAD), bf16)
    cross = pltpu.VMEM((tokens, width), bf16)
    one, t = dma, max(tp - 1, 1)
    return pl.pallas_call(
        functools.partial(fused_kernel, n, tp),
        out_shape=(
            pltpu.VMEM((tokens, vwidth), bf16),
            pltpu.VMEM((tokens, width), bf16),
            pltpu.VMEM((rows, width), bf16),
            pltpu.VMEM((rows, width), bf16),
        ),
        in_specs=[anywhere] * 13,
        out_specs=(pl.BlockSpec(memory_space=pltpu.VMEM),) * 4,
        scratch_shapes=[
            pltpu.VMEM((3, hd, n, tokens, VHEAD), bf16), head,
            pltpu.VMEM((3, n, rows, width), bf16),
            cross, cross, cross,
            pltpu.VMEM(up.shape, bf16),
            pltpu.VMEM(down.shape, bf16),
            pltpu.VMEM(ai.shape, bf16),
            pltpu.VMEM((1, gain.shape[0]), f32),
            pltpu.VMEM((n, rows, width), f32),
            pltpu.VMEM((3, rows, width), bf16),
            pltpu.VMEM((3, rows, width), bf16),
            pltpu.VMEM((n, rows, 128), f32),
            pltpu.VMEM((3, rows, 128), f32),
            pltpu.VMEM((tp, n * rows, 128), f32),
            pltpu.VMEM((n, rows, width + 128), bf16),
            pltpu.VMEM((tp, CHUNKS, n * rows, units // CHUNKS), bf16),
            pltpu.VMEM((CHUNKS, n * rows, units // CHUNKS), f32),
            pltpu.VMEM((n, rows, width), f32),
            pltpu.VMEM((3, rows, width), bf16),
            pltpu.VMEM((3, rows, width), bf16),
            one, dma((hd,)), one, one, one, dma((4,)), one, dma((2,)), one, dma((2,)), dma((t,)), dma((t,)),
            one, dma((2,)), one, dma((CHUNKS, t)), one, dma((2,)),
            dma((hd,)), one, dma((10,)), pltpu.SemaphoreType.REGULAR((5,)),
        ],
        compiler_params=pltpu.CompilerParams(collective_id=0, has_side_effects=True),
    )(vq, vk, vv, cq, ak, av, aq, ck, cv, ai, gain.reshape(1, -1), up, down)


def hand_over(*refs):
    count = (len(refs) - 1) // 2
    copies = [pltpu.make_async_copy(refs[i], refs[count + i], refs[-1].at[i]) for i in range(count)]
    for copy in copies:
        copy.start()
    for copy in copies:
        copy.wait()


def deliver(arrays):
    arrays = [pltpu.with_memory_space_constraint(a, pltpu.VMEM) for a in arrays]
    return pl.pallas_call(
        hand_over,
        out_shape=tuple(jax.ShapeDtypeStruct(a.shape, a.dtype) for a in arrays),
        in_specs=[pl.BlockSpec(memory_space=pltpu.VMEM)] * len(arrays),
        out_specs=(pl.BlockSpec(memory_space=pl.ANY),) * len(arrays),
        scratch_shapes=[pltpu.SemaphoreType.DMA((len(arrays),))],
    )(*arrays)


def fits(n, vq, aq, up):
    heads = vq.shape[2] // VHEAD
    return (
        n == 4
        and heads % n == 0
        and vq.shape[1] % 16 == 0
        and aq.shape[1] % 8 == 0
        and aq.shape[2] % 128 == 0
        and aq.shape[2] // CHEAD <= 64
        and up.shape[0] == aq.shape[2]
        and up.shape[1] % (128 * CHUNKS) == 0
    )


def attend_rows(queries, keys_in, values_in, head_count):
    head_size = queries.shape[1] // head_count
    query_heads = queries.reshape(queries.shape[0], head_count, head_size)
    key_heads = keys_in.reshape(keys_in.shape[0], head_count, head_size)
    value_heads = values_in.reshape(values_in.shape[0], head_count, head_size)
    scores = jnp.einsum(
        "qhd,khd->qhk", query_heads, key_heads, preferred_element_type=jnp.float32
    ) / math.sqrt(head_size)
    peak_value = jnp.max(scores, axis=2, keepdims=True)
    weights = jnp.exp(scores - peak_value)
    totals = jnp.sum(weights, axis=2)
    weighted = jnp.einsum(
        "qhk,khd->qhd",
        weights.astype(jnp.bfloat16),
        value_heads,
        preferred_element_type=jnp.float32,
    )
    result = weighted / totals[:, :, None]
    return result.reshape(queries.shape[0], head_count * head_size).astype(jnp.bfloat16)


def attend(queries, keys_in, values_in, head_count):
    row_total = queries.shape[0]
    block_rows = 512 if row_total % 512 == 0 else row_total
    pieces = queries.reshape(row_total // block_rows, block_rows, queries.shape[1])
    result = lax.map(
        lambda row_piece: attend_rows(row_piece, keys_in, values_in, head_count), pieces
    )
    return result.reshape(row_total, queries.shape[1])


def video_self(queries, keys_in, values_in):
    seq_count = lax.axis_size("seq")
    local_heads = queries.shape[1] // VHEAD
    dest_heads = max(local_heads // seq_count, 1)
    blocks = seq_count * dest_heads // local_heads
    groups = local_heads // dest_heads
    group_width = dest_heads * VHEAD
    token_count = queries.shape[0]
    block_tokens = token_count // blocks

    def spread(tensor):
        shaped = tensor.reshape(token_count, groups, group_width).transpose(1, 0, 2)
        shaped = jnp.broadcast_to(shaped[:, None], (groups, blocks, token_count, group_width))
        return shaped.reshape(seq_count, token_count, group_width)

    shaped = queries.reshape(blocks, block_tokens, groups, group_width).transpose(2, 0, 1, 3)
    own_queries = lax.all_to_all(
        shaped.reshape(seq_count, block_tokens, group_width),
        "seq",
        split_axis=0,
        concat_axis=0,
        tiled=True,
    )
    keys_all = lax.all_to_all(spread(keys_in), "seq", split_axis=0, concat_axis=0, tiled=True)
    values_all = lax.all_to_all(spread(values_in), "seq", split_axis=0, concat_axis=0, tiled=True)
    keys_all = keys_all.reshape(-1, group_width)
    values_all = values_all.reshape(-1, group_width)
    own_queries = own_queries.reshape(-1, group_width)
    attended = attend(own_queries, keys_all, values_all, dest_heads)
    returned = lax.all_to_all(
        attended.reshape(seq_count, block_tokens, group_width),
        "seq",
        split_axis=0,
        concat_axis=0,
        tiled=True,
    )
    returned = returned.reshape(groups, blocks, block_tokens, group_width).transpose(1, 2, 0, 3)
    return returned.reshape(token_count, groups * group_width)


def audio_listen(queries, keys_in, values_in, head_count):
    head_size = queries.shape[1] // head_count
    query_heads = queries.reshape(queries.shape[0], head_count, head_size)
    key_heads = keys_in.reshape(keys_in.shape[0], head_count, head_size)
    value_heads = values_in.reshape(values_in.shape[0], head_count, head_size)
    scores = jnp.einsum(
        "qhd,khd->qhk", query_heads, key_heads, preferred_element_type=jnp.float32
    ) / math.sqrt(head_size)
    local_peak = jnp.max(scores, axis=2)
    peak_value = lax.pmax(local_peak, "seq")
    weights = jnp.exp(scores - peak_value[:, :, None])
    totals = jnp.sum(weights, axis=2)
    weighted = jnp.einsum(
        "qhk,khd->qhd",
        weights.astype(jnp.bfloat16),
        value_heads,
        preferred_element_type=jnp.float32,
    )
    totals, weighted = (totals, weighted.reshape(queries.shape[0], head_count * head_size))
    totals, weighted = (
        lax.psum_scatter(totals, "seq", scatter_dimension=0, tiled=True),
        lax.psum_scatter(weighted, "seq", scatter_dimension=0, tiled=True),
    )
    return (weighted / jnp.repeat(totals, head_size, axis=1)).astype(jnp.bfloat16)


def audio_block(audio_rows, audio_seen, norm_gain, up_weight, down_weight):
    features = lax.all_gather(audio_seen, "tp", axis=1, tiled=True)
    residual = audio_rows.astype(jnp.float32) + features.astype(jnp.float32)
    scale_factor = lax.rsqrt(jnp.mean(residual * residual, axis=1, keepdims=True) + 1e-06)
    normed = (residual * scale_factor * norm_gain).astype(jnp.bfloat16)
    slice_width = up_weight.shape[0]
    own_features = lax.dynamic_slice_in_dim(
        normed, lax.axis_index("tp") * slice_width, slice_width, 1
    )
    partial_sum = jnp.dot(
        lax.all_gather(own_features, "seq", axis=0, tiled=True),
        up_weight,
        preferred_element_type=jnp.float32,
    )
    hidden = jax.nn.gelu(lax.psum(partial_sum, "tp")).astype(jnp.bfloat16)
    return lax.psum_scatter(
        jnp.dot(hidden, down_weight, preferred_element_type=jnp.float32),
        "seq",
        scatter_dimension=0,
        tiled=True,
    ).astype(jnp.bfloat16)


def body(
    video_query,
    video_key,
    video_value,
    cross_query,
    audio_key,
    audio_value,
    audio_query,
    cross_key,
    cross_value,
    audio_input,
    norm_gain,
    up_weight,
    down_weight,
):
    if fits(lax.axis_size("seq"), video_query, audio_query, up_weight):
        args = (video_query, video_key, video_value, cross_query, audio_key, audio_value)
        args += (audio_query, cross_key, cross_value, audio_input)
        args = tuple(a[0] for a in args) + (norm_gain, up_weight, down_weight)
        outs = deliver(fused(lax.axis_size("seq"), lax.axis_size("tp"), args))
        return tuple(out[None] for out in outs)
    mixed_list, heard_list, seen_list, output_list = ([], [], [], [])
    cross_heads = cross_query.shape[2] // CHEAD
    mixed_list.append(video_self(video_query[0], video_key[0], video_value[0]))
    gathered_query = lax.all_gather(audio_query[0], "seq", axis=0, tiled=True)
    gathered_key = lax.all_gather(audio_key[0], "seq", axis=0, tiled=True)
    gathered_value = lax.all_gather(audio_value[0], "seq", axis=0, tiled=True)
    heard_list.append(attend(cross_query[0], gathered_key, gathered_value, cross_heads))
    audio_seen = audio_listen(gathered_query, cross_key[0], cross_value[0], cross_heads)
    seen_list.append(audio_seen)
    output_list.append(audio_block(audio_input[0], audio_seen, norm_gain, up_weight, down_weight))
    return (
        jnp.stack(mixed_list),
        jnp.stack(heard_list),
        jnp.stack(seen_list),
        jnp.stack(output_list),
    )


def solution(mesh):
    placed = (
        P(("clips", "dp"), "seq", "tp"),
        P(("clips", "dp"), "seq", "tp"),
        P(("clips", "dp"), "seq", "tp"),
        P(("clips", "dp"), "seq", "tp"),
        P(("clips", "dp"), "seq", "tp"),
        P(("clips", "dp"), "seq", "tp"),
        P(("clips", "dp"), "seq", "tp"),
        P(("clips", "dp"), "seq", "tp"),
        P(("clips", "dp"), "seq", "tp"),
        P(("clips", "dp"), "seq", None),
        P(),
        P("tp", "seq"),
        P("seq", "tp"),
    )
    return jax.shard_map(
        body,
        mesh=mesh,
        in_specs=placed,
        out_specs=(
            P(("clips", "dp"), "seq", "tp"),
            P(("clips", "dp"), "seq", "tp"),
            P(("clips", "dp"), "seq", "tp"),
            P(("clips", "dp"), "seq", "tp"),
        ),
        check_vma=False,
    )
```

```python
import functools
import math

import jax
import jax.numpy as jnp
from jax import lax
from jax.experimental import pallas as pl
from jax.experimental.pallas import tpu as pltpu
from jax.sharding import PartitionSpec as P

VHEAD = 128
CHEAD = 64
MESH = pl.DeviceIdType.MESH
LOG2E = math.log2(math.e)
CHUNKS = 4
EARLY = 3
PACE = ((1, 1, 1, 2, 2, 2, 0, 1), (0, 2, 1, 0, 1, 1, 3, 1))
ORDER = (2, 0, 1)
LATE = 1
RIGHT = True
TURNS = (0, 0, 0, 0, 1, 0)


def dot_t(a, b):
    return lax.dot_general(a, b, (((1,), (1,)), ((), ())), preferred_element_type=jnp.float32)


def softmax_parts(q, k, scale):
    s = dot_t(q, k)
    peak = jnp.max(s, axis=1, keepdims=True)
    p = jnp.exp2((s - peak) * (scale * LOG2E))
    return p, peak * scale, jnp.sum(p, axis=1, keepdims=True)


def pair_attend(q, k, v, scale):
    low = lax.broadcasted_iota(jnp.int32, q.shape, 1) < CHEAD
    zero = jnp.zeros_like(q)
    both = jnp.concatenate([jnp.where(low, q, zero), jnp.where(low, zero, q)], axis=0)
    p, peak, total = softmax_parts(both, k, scale)
    o = jnp.dot(p.astype(jnp.bfloat16), v, preferred_element_type=jnp.float32)
    return o, peak, total


def partners(me, n):
    if n & (n - 1):
        return [lax.rem(me + d, n) for d in range(1, n)]
    found = []
    for flip in range(n - 1, 0, -1):
        place, bit = me * 0, 1
        while bit < n:
            digit = lax.rem(lax.div(me, bit), 2)
            place = place + bit * ((1 - digit) if flip & bit else digit)
            bit *= 2
        found.append(place)
    return found


def fused_kernel(
    n, tp,
    vq, vk, vv, cq, ak, av, aq, ck, cv, ai, gain, up, down,
    mixed, heard, seen, mlp,
    vbuf, obuf, abuf, cqv, ckv, cvv, upv, downv, aiv, gainv, xown, xsend, xrecv, tsend, trecv, ssbuf, nbuf, pbuf, ubuf, racc, rsend, rrecv,
    v_send, v_recv, o_send, o_recv, a_send, a_recv, x_send, x_recv, t_send, t_recv, s_send, s_recv,
    n_send, n_recv, p_send, p_recv, r_send, r_recv, own_sem, oown_sem, load_sem, ready,
):
    me = lax.axis_index("seq")
    col = lax.axis_index("tp")
    core = lax.rem(lax.axis_index("dp"), 2)
    tokens = vq.shape[0]
    hd = vq.shape[1] // VHEAD // n
    rows, width = aq.shape
    pairs = width // 128
    units = up.shape[1]
    step = units // CHUNKS
    f32, bf16 = jnp.float32, jnp.bfloat16
    peers = partners(me, n)
    tp_peers = [lax.rem(col + d, tp) for d in range(1, tp)]

    def remote(src, dst, ss, rs, where):
        copy = pltpu.make_async_remote_copy(
            src_ref=src, dst_ref=dst, send_sem=ss, recv_sem=rs, device_id=where, device_id_type=MESH
        )
        copy.start()
        return copy

    far, over, side = peers
    inner = lax.rem(lax.div(me + 1, 2), 2) == 1
    outer = jnp.logical_not(inner)
    streams = (vq, vk, vv)
    order = ORDER
    cross = inner
    if RIGHT:
        cross = jnp.logical_xor(inner, me < n // 2)
    back = (jnp.where(cross, over, far), jnp.where(cross, far, over), side, me)
    units = [(h, i) for h in range(hd) for i in (1, 2, 0)]

    def unit(h, i, d):
        cols = pl.ds(pl.multiple_of((peers[d] * hd + h) * VHEAD, VHEAD), VHEAD)
        return pltpu.make_async_remote_copy(
            src_ref=streams[i].at[:, cols], dst_ref=vbuf.at[i, h, me], send_sem=v_send, recv_sem=v_recv.at[h],
            device_id={"seq": peers[d]}, device_id_type=MESH,
        )

    def landed(ref, sem):
        pltpu.make_async_copy(ref, ref, sem).wait()

    marks = [EARLY, EARLY]

    def pump(w):
        ends = [min(marks[c] + PACE[c][w], len(units)) if w < len(PACE[c]) else len(units) for c in range(2)]
        for k, (h, i) in enumerate(units):
            mine = [marks[c] <= k < ends[c] for c in range(2)]

            def go():
                for d in order:
                    unit(h, i, d).start()

            if all(mine):
                go()
            elif any(mine):
                pl.when(core == mine.index(True))(go)
        marks[:] = ends

    def tell(where, k):
        pl.semaphore_signal(ready.at[k], inc=1, device_id=where, device_id_type=MESH)

    hub = me == n // 2 - 1
    barrier = pltpu.get_barrier_semaphore()
    early = units[:EARLY]

    @pl.when(inner)
    def _():
        for p in (far, side):
            pl.semaphore_signal(barrier, inc=1, device_id={"seq": p}, device_id_type=MESH)

    @pl.when(hub)
    def _():
        for t in tp_peers:
            pl.semaphore_signal(barrier, inc=1, device_id={"tp": t}, device_id_type=MESH)

    pl.semaphore_wait(barrier, jnp.where(hub, tp, 1))

    @pl.when(inner)
    def _():
        for h, i in early:
            unit(h, i, 0).start()

    @pl.when(outer)
    def _():
        tell({"seq": side}, 0)
        for h, i in early:
            unit(h, i, 2).start()

    loads = []
    stays = ((ck, ckv), (cv, cvv), (cq, cqv), (up, upv), (down, downv), (ai, aiv), (gain, gainv))
    stays += tuple((src, abuf.at[i, me]) for i, src in enumerate((aq, ak, av)))
    for i, (src, dst) in enumerate(stays):
        loads.append(pltpu.make_async_copy(src, dst, load_sem.at[i]))

    for i in (0, 1, 7):
        loads[i].start()

    @pl.when(inner)
    def _():
        pl.semaphore_wait(ready.at[0], 1)
        tell({"seq": far}, 1)
        pl.semaphore_wait(ready.at[1], 1)
        tell({"seq": side}, 2)

    @pl.when(hub)
    def _():
        for t in tp_peers:
            tell({"tp": t}, 3)

    @pl.when(outer)
    def _():
        pl.semaphore_wait(ready.at[2], 1)

    kept = []

    def give(h, p, cols):
        remote(obuf.at[h, p], mixed.at[:, cols], o_send, o_recv, {"seq": p})

    def attend_video(h):
        if h == 0:
            landed(vbuf.at[:, :, 0], own_sem)
        landed(vbuf.at[:, h, : n - 1], v_recv.at[h])
        k = vbuf[1, h].reshape(n * tokens, VHEAD)
        v = vbuf[2, h].reshape(n * tokens, VHEAD)
        cols = pl.ds(pl.multiple_of((me * hd + h) * VHEAD, VHEAD), VHEAD)
        for i, p in enumerate(back):
            w, _, total = softmax_parts(vbuf[0, h, p], k, 1.0 / math.sqrt(VHEAD))
            o = jnp.dot(w.astype(bf16), v, preferred_element_type=f32) / total
            obuf[h, p] = o.astype(bf16)
            if i == 1 and LATE <= h < hd - 1:
                kept.append((h, p, cols))
            elif i < n - 1:
                give(h, p, cols)
            if i == 0 and h == hd - 1:
                for later in kept:
                    give(*later)
        pltpu.make_async_copy(obuf.at[h, me], mixed.at[:, cols], oown_sem).start()

    heads = list(range(hd))

    def attend_next(count):
        for h in heads[:count]:
            attend_video(h)
        del heads[:count]

    def spread(src, slots, ss, rs):
        for d, r in ((2, rs[1]), (1, rs[0])):
            remote(src, slots.at[me], ss, r, {"seq": peers[d]})

    def hand_on(slots, ss, rs):
        remote(slots.at[over], slots.at[over], ss, rs[1], {"seq": side})

    a_recvs = [(a_recv.at[0], a_recv.at[1]), (a_recv.at[2], a_recv.at[3])]
    n_recvs = (n_recv.at[0], n_recv.at[1])
    spread(aq, abuf.at[0], a_send, a_recvs[0])
    for h, i in early:

        @pl.when(inner)
        def _():
            unit(h, i, 2).start()

        @pl.when(outer)
        def _():
            unit(h, i, 0).start()

        unit(h, i, 1).start()
    for h in range(hd):
        cols = pl.ds(pl.multiple_of((me * hd + h) * VHEAD, VHEAD), VHEAD)
        for i, src in enumerate(streams):
            pltpu.make_async_copy(src.at[:, cols], vbuf.at[i, h, me], own_sem).start()
    for copy in loads[2:7] + loads[8:]:
        copy.start()
    pump(0)
    landed(abuf.at[0, 0], a_recvs[0][0])
    hand_on(abuf.at[0], a_send, a_recvs[0])
    pump(1)

    @pl.when(hub)
    def _():
        pl.semaphore_wait(ready.at[3], tp - 1)
        for p in peers:
            tell({"seq": p}, 4)

    for copy in loads[:2] + loads[5:]:
        copy.wait()
    landed(abuf.at[0, : n - 2], a_recvs[0][1])

    def whole(i):
        return jnp.concatenate([abuf[i, s].astype(f32) for s in range(n)], axis=0).astype(bf16)

    scale = 1.0 / math.sqrt(CHEAD)
    total_rows = n * rows
    q_all = whole(0)
    lane = lax.broadcasted_iota(jnp.int32, (total_rows, 128), 1)
    stats = jnp.ones((total_rows, 128), f32)
    for j in range(pairs):
        at = slice(j * 128, (j + 1) * 128)
        o, peak, total = pair_attend(q_all[:, at], ckv[:, at], cvv[:, at], scale)
        picked = jnp.where(lane < CHEAD, o[:total_rows], o[total_rows:])
        xown[:, :, at] = picked.reshape(n, rows, 128)
        for half in range(2):
            part = slice(half * total_rows, (half + 1) * total_rows)
            stats = jnp.where(lane == 2 * j + half, peak[part], stats)
            stats = jnp.where(lane == 64 + 2 * j + half, total[part], stats)
    tsend[...] = stats.reshape(n, rows, 128)

    def send_part(d, slot, k):
        r, where = min(k, 1), {"seq": peers[d]}
        remote(tsend.at[slot], trecv.at[k], t_send, t_recv.at[r], where)
        remote(xsend.at[k], xrecv.at[k], x_send, x_recv.at[r], where)

    xsend[0] = xown[far].astype(bf16)
    send_part(2, far, 0)
    xsend[1] = xown[side].astype(bf16)
    send_part(2, side, 1)
    place = lax.broadcasted_iota(jnp.int32, (rows, 128), 1)

    def weigh(stats):
        peak = functools.reduce(jnp.maximum, stats)
        factors = [jnp.exp(t - peak) for t in stats]
        return peak, factors, sum(f * pltpu.roll(t, 64, 1) for f, t in zip(factors, stats))

    def blend(factors, blocks):
        pieces = []
        for j in range(pairs):
            at = slice(j * 128, (j + 1) * 128)
            terms = [
                jnp.where(place < CHEAD, f[:, 2 * j : 2 * j + 1], f[:, 2 * j + 1 : 2 * j + 2]) * b[:, at].astype(f32)
                for f, b in zip(factors, blocks)
            ]
            pieces.append(sum(terms[1:], terms[0]))
        return jnp.concatenate(pieces, axis=1).astype(bf16)

    pump(2)

    landed(trecv.at[0], t_recv.at[0])
    landed(xrecv.at[0], x_recv.at[0])
    peak, factors, total = weigh([tsend[over], trecv[0]])
    xsend[2] = blend(factors, [xown[over], xrecv[0]])
    tsend[over] = jnp.where(place < 64, peak, pltpu.roll(total, 64, 1))
    send_part(1, over, 2)

    pump(3)
    attend_next(TURNS[0])

    landed(trecv.at[1:], t_recv.at[1])
    landed(xrecv.at[1:], x_recv.at[1])
    _, factors, total = weigh([tsend[me], trecv[1], trecv[2]])
    seen_bf = blend([f / total for f in factors], [xown[me], xrecv[1], xrecv[2]])
    seen[...] = seen_bf

    mine = pl.ds(pl.multiple_of(col * width, 128), width)
    residual = aiv[:, mine].astype(f32) + seen_bf.astype(f32)
    square = jnp.sum(residual * residual, axis=1, keepdims=True)
    first = square.astype(bf16).astype(f32)
    second = (square - first).astype(bf16).astype(f32)
    third = square - first - second
    split = jnp.where(place == 0, first, jnp.where(place == 1, second, jnp.where(place == 2, third, 0.0)))
    nbuf[me, :, :width] = (residual * gainv[:, mine]).astype(bf16)
    nbuf[me, :, width:] = split.astype(bf16)
    spread(nbuf.at[me], nbuf, n_send, n_recvs)
    for i, src in enumerate((ak, av)):
        spread(src, abuf.at[i + 1], a_send, a_recvs[1])
    pump(4)
    attend_next(TURNS[1])
    landed(nbuf.at[0], n_recvs[0])
    hand_on(nbuf, n_send, n_recvs)
    pump(5)
    attend_next(TURNS[2])

    loads[3].wait()
    landed(nbuf.at[: n - 2], n_recvs[1])
    held = jnp.concatenate([nbuf[s].astype(f32) for s in range(n)], axis=0)
    x = held[:, :width].astype(bf16)
    square = jnp.sum(held[:, width:], axis=1, keepdims=True)
    ssbuf[col] = jnp.broadcast_to(square, (total_rows, 128))
    partials = []

    @pl.when(jnp.logical_not(hub))
    def _():
        pl.semaphore_wait(ready.at[4], 1)

    for d, t in enumerate(tp_peers):
        partials.append(remote(ssbuf.at[col], ssbuf.at[col], s_send.at[d], s_recv.at[d], {"tp": t}))
    for c in range(CHUNKS):
        ubuf[c] = jnp.dot(x, upv[:, c * step : (c + 1) * step], preferred_element_type=f32)
        pbuf[col, c] = ubuf[c].astype(bf16)
        for d, t in enumerate(tp_peers):
            partials.append(
                remote(pbuf.at[col, c], pbuf.at[col, c], p_send, p_recv.at[c, d], {"tp": t})
            )
    landed(abuf.at[1:, 0], a_recvs[1][0])
    for i in (1, 2):
        hand_on(abuf.at[i], a_send, a_recvs[1])
    pump(6)
    attend_next(TURNS[3])

    loads[4].wait()
    for copy in partials[: tp - 1]:
        copy.wait_recv()
    square = sum(ssbuf[t] for t in range(tp))[:, 0:1]
    factor = lax.rsqrt(square / (width * tp) + 1e-6)
    acc = jnp.zeros((total_rows, width), f32)
    for c in range(CHUNKS):
        for copy in partials[(c + 1) * (tp - 1) : (c + 2) * (tp - 1)]:
            copy.wait_recv()
        up_sum = (ubuf[c] + sum(pbuf[t, c].astype(f32) for t in tp_peers)) * factor
        hidden = jax.nn.gelu(up_sum, approximate=True).astype(bf16)
        acc += jnp.dot(hidden, downv[c * step : (c + 1) * step, :], preferred_element_type=f32)
    racc[...] = acc.reshape(n, rows, width)

    def send_sum(d, k):
        remote(rsend.at[k], rrecv.at[k], r_send, r_recv.at[min(k, 1)], {"seq": peers[d]})

    rsend[0] = racc[far].astype(bf16)
    send_sum(2, 0)
    rsend[1] = racc[side].astype(bf16)
    send_sum(2, 1)
    pump(7)

    attend_next(TURNS[4])
    landed(rrecv.at[0], r_recv.at[0])
    rsend[2] = (racc[over] + rrecv[0].astype(f32)).astype(bf16)
    send_sum(1, 2)
    pump(8)
    attend_next(TURNS[5])

    loads[2].wait()
    landed(abuf.at[1:, : n - 2], a_recvs[1][1])
    k_all, v_all = whole(1), whole(2)
    wide = lax.broadcasted_iota(jnp.int32, (tokens, 128), 1)
    for j in range(pairs):
        at = slice(j * 128, (j + 1) * 128)
        o, _, total = pair_attend(cqv[:, at], k_all[:, at], v_all[:, at], scale)
        o = o / total
        heard[:, at] = jnp.where(wide < CHEAD, o[:tokens], o[tokens:]).astype(bf16)

    attend_next(len(heads) - 1)

    landed(rrecv.at[1:], r_recv.at[1])
    mlp[...] = (racc[me] + rrecv[1].astype(f32) + rrecv[2].astype(f32)).astype(bf16)

    attend_next(len(heads))

    for ref, sem in (
        (vbuf.at[:, :, : n - 1], v_send),
        (abuf.at[:, : n - 1], a_send),
        (xsend, x_send),
        (trecv, t_send),
        (nbuf.at[: n - 1], n_send),
        (rsend, r_send),
    ):
        landed(ref, sem)
    if tp > 1:
        landed(pbuf.at[: tp - 1], p_send)
    for copy in partials[: tp - 1]:
        copy.wait_send()
    landed(mixed.at[:, : hd * VHEAD], oown_sem)
    landed(obuf.at[:, : n - 1], o_send)
    landed(mixed.at[:, : (n - 1) * hd * VHEAD], o_recv)


def fused(n, tp, args):
    vq, vk, vv, cq, ak, av, aq, ck, cv, ai, gain, up, down = args
    tokens, vwidth = vq.shape
    hd = vwidth // VHEAD // n
    rows, width = aq.shape
    units = up.shape[1]
    bf16, f32 = jnp.bfloat16, jnp.float32
    anywhere = pl.BlockSpec(memory_space=pl.ANY)
    dma = pltpu.SemaphoreType.DMA
    head = pltpu.VMEM((hd, n, tokens, VHEAD), bf16)
    cross = pltpu.VMEM((tokens, width), bf16)
    one, t = dma, max(tp - 1, 1)
    return pl.pallas_call(
        functools.partial(fused_kernel, n, tp),
        out_shape=(
            pltpu.VMEM((tokens, vwidth), bf16),
            pltpu.VMEM((tokens, width), bf16),
            pltpu.VMEM((rows, width), bf16),
            pltpu.VMEM((rows, width), bf16),
        ),
        in_specs=[anywhere] * 13,
        out_specs=(pl.BlockSpec(memory_space=pltpu.VMEM),) * 4,
        scratch_shapes=[
            pltpu.VMEM((3, hd, n, tokens, VHEAD), bf16), head,
            pltpu.VMEM((3, n, rows, width), bf16),
            cross, cross, cross,
            pltpu.VMEM(up.shape, bf16),
            pltpu.VMEM(down.shape, bf16),
            pltpu.VMEM(ai.shape, bf16),
            pltpu.VMEM((1, gain.shape[0]), f32),
            pltpu.VMEM((n, rows, width), f32),
            pltpu.VMEM((3, rows, width), bf16),
            pltpu.VMEM((3, rows, width), bf16),
            pltpu.VMEM((n, rows, 128), f32),
            pltpu.VMEM((3, rows, 128), f32),
            pltpu.VMEM((tp, n * rows, 128), f32),
            pltpu.VMEM((n, rows, width + 128), bf16),
            pltpu.VMEM((tp, CHUNKS, n * rows, units // CHUNKS), bf16),
            pltpu.VMEM((CHUNKS, n * rows, units // CHUNKS), f32),
            pltpu.VMEM((n, rows, width), f32),
            pltpu.VMEM((3, rows, width), bf16),
            pltpu.VMEM((3, rows, width), bf16),
            one, dma((hd,)), one, one, one, dma((4,)), one, dma((2,)), one, dma((2,)), dma((t,)), dma((t,)),
            one, dma((2,)), one, dma((CHUNKS, t)), one, dma((2,)),
            one, one, dma((10,)), pltpu.SemaphoreType.REGULAR((5,)),
        ],
        compiler_params=pltpu.CompilerParams(collective_id=0, has_side_effects=True),
    )(vq, vk, vv, cq, ak, av, aq, ck, cv, ai, gain.reshape(1, -1), up, down)


def hand_over(*refs):
    count = (len(refs) - 1) // 2
    copies = [pltpu.make_async_copy(refs[i], refs[count + i], refs[-1].at[i]) for i in range(count)]
    for copy in copies:
        copy.start()
    for copy in copies:
        copy.wait()


def deliver(arrays):
    arrays = [pltpu.with_memory_space_constraint(a, pltpu.VMEM) for a in arrays]
    return pl.pallas_call(
        hand_over,
        out_shape=tuple(jax.ShapeDtypeStruct(a.shape, a.dtype) for a in arrays),
        in_specs=[pl.BlockSpec(memory_space=pltpu.VMEM)] * len(arrays),
        out_specs=(pl.BlockSpec(memory_space=pl.ANY),) * len(arrays),
        scratch_shapes=[pltpu.SemaphoreType.DMA((len(arrays),))],
    )(*arrays)


def fits(n, vq, aq, up):
    heads = vq.shape[2] // VHEAD
    return (
        n == 4
        and heads % n == 0
        and vq.shape[1] % 16 == 0
        and aq.shape[1] % 8 == 0
        and aq.shape[2] % 128 == 0
        and aq.shape[2] // CHEAD <= 64
        and up.shape[0] == aq.shape[2]
        and up.shape[1] % (128 * CHUNKS) == 0
    )


def attend_rows(queries, keys_in, values_in, head_count):
    head_size = queries.shape[1] // head_count
    query_heads = queries.reshape(queries.shape[0], head_count, head_size)
    key_heads = keys_in.reshape(keys_in.shape[0], head_count, head_size)
    value_heads = values_in.reshape(values_in.shape[0], head_count, head_size)
    scores = jnp.einsum(
        "qhd,khd->qhk", query_heads, key_heads, preferred_element_type=jnp.float32
    ) / math.sqrt(head_size)
    peak_value = jnp.max(scores, axis=2, keepdims=True)
    weights = jnp.exp(scores - peak_value)
    totals = jnp.sum(weights, axis=2)
    weighted = jnp.einsum(
        "qhk,khd->qhd",
        weights.astype(jnp.bfloat16),
        value_heads,
        preferred_element_type=jnp.float32,
    )
    result = weighted / totals[:, :, None]
    return result.reshape(queries.shape[0], head_count * head_size).astype(jnp.bfloat16)


def attend(queries, keys_in, values_in, head_count):
    row_total = queries.shape[0]
    block_rows = 512 if row_total % 512 == 0 else row_total
    pieces = queries.reshape(row_total // block_rows, block_rows, queries.shape[1])
    result = lax.map(
        lambda row_piece: attend_rows(row_piece, keys_in, values_in, head_count), pieces
    )
    return result.reshape(row_total, queries.shape[1])


def video_self(queries, keys_in, values_in):
    seq_count = lax.axis_size("seq")
    local_heads = queries.shape[1] // VHEAD
    dest_heads = max(local_heads // seq_count, 1)
    blocks = seq_count * dest_heads // local_heads
    groups = local_heads // dest_heads
    group_width = dest_heads * VHEAD
    token_count = queries.shape[0]
    block_tokens = token_count // blocks

    def spread(tensor):
        shaped = tensor.reshape(token_count, groups, group_width).transpose(1, 0, 2)
        shaped = jnp.broadcast_to(shaped[:, None], (groups, blocks, token_count, group_width))
        return shaped.reshape(seq_count, token_count, group_width)

    shaped = queries.reshape(blocks, block_tokens, groups, group_width).transpose(2, 0, 1, 3)
    own_queries = lax.all_to_all(
        shaped.reshape(seq_count, block_tokens, group_width),
        "seq",
        split_axis=0,
        concat_axis=0,
        tiled=True,
    )
    keys_all = lax.all_to_all(spread(keys_in), "seq", split_axis=0, concat_axis=0, tiled=True)
    values_all = lax.all_to_all(spread(values_in), "seq", split_axis=0, concat_axis=0, tiled=True)
    keys_all = keys_all.reshape(-1, group_width)
    values_all = values_all.reshape(-1, group_width)
    own_queries = own_queries.reshape(-1, group_width)
    attended = attend(own_queries, keys_all, values_all, dest_heads)
    returned = lax.all_to_all(
        attended.reshape(seq_count, block_tokens, group_width),
        "seq",
        split_axis=0,
        concat_axis=0,
        tiled=True,
    )
    returned = returned.reshape(groups, blocks, block_tokens, group_width).transpose(1, 2, 0, 3)
    return returned.reshape(token_count, groups * group_width)


def audio_listen(queries, keys_in, values_in, head_count):
    head_size = queries.shape[1] // head_count
    query_heads = queries.reshape(queries.shape[0], head_count, head_size)
    key_heads = keys_in.reshape(keys_in.shape[0], head_count, head_size)
    value_heads = values_in.reshape(values_in.shape[0], head_count, head_size)
    scores = jnp.einsum(
        "qhd,khd->qhk", query_heads, key_heads, preferred_element_type=jnp.float32
    ) / math.sqrt(head_size)
    local_peak = jnp.max(scores, axis=2)
    peak_value = lax.pmax(local_peak, "seq")
    weights = jnp.exp(scores - peak_value[:, :, None])
    totals = jnp.sum(weights, axis=2)
    weighted = jnp.einsum(
        "qhk,khd->qhd",
        weights.astype(jnp.bfloat16),
        value_heads,
        preferred_element_type=jnp.float32,
    )
    totals, weighted = (totals, weighted.reshape(queries.shape[0], head_count * head_size))
    totals, weighted = (
        lax.psum_scatter(totals, "seq", scatter_dimension=0, tiled=True),
        lax.psum_scatter(weighted, "seq", scatter_dimension=0, tiled=True),
    )
    return (weighted / jnp.repeat(totals, head_size, axis=1)).astype(jnp.bfloat16)


def audio_block(audio_rows, audio_seen, norm_gain, up_weight, down_weight):
    features = lax.all_gather(audio_seen, "tp", axis=1, tiled=True)
    residual = audio_rows.astype(jnp.float32) + features.astype(jnp.float32)
    scale_factor = lax.rsqrt(jnp.mean(residual * residual, axis=1, keepdims=True) + 1e-06)
    normed = (residual * scale_factor * norm_gain).astype(jnp.bfloat16)
    slice_width = up_weight.shape[0]
    own_features = lax.dynamic_slice_in_dim(
        normed, lax.axis_index("tp") * slice_width, slice_width, 1
    )
    partial_sum = jnp.dot(
        lax.all_gather(own_features, "seq", axis=0, tiled=True),
        up_weight,
        preferred_element_type=jnp.float32,
    )
    hidden = jax.nn.gelu(lax.psum(partial_sum, "tp")).astype(jnp.bfloat16)
    return lax.psum_scatter(
        jnp.dot(hidden, down_weight, preferred_element_type=jnp.float32),
        "seq",
        scatter_dimension=0,
        tiled=True,
    ).astype(jnp.bfloat16)


def body(
    video_query,
    video_key,
    video_value,
    cross_query,
    audio_key,
    audio_value,
    audio_query,
    cross_key,
    cross_value,
    audio_input,
    norm_gain,
    up_weight,
    down_weight,
):
    if fits(lax.axis_size("seq"), video_query, audio_query, up_weight):
        args = (video_query, video_key, video_value, cross_query, audio_key, audio_value)
        args += (audio_query, cross_key, cross_value, audio_input)
        args = tuple(a[0] for a in args) + (norm_gain, up_weight, down_weight)
        outs = deliver(fused(lax.axis_size("seq"), lax.axis_size("tp"), args))
        return tuple(out[None] for out in outs)
    mixed_list, heard_list, seen_list, output_list = ([], [], [], [])
    cross_heads = cross_query.shape[2] // CHEAD
    mixed_list.append(video_self(video_query[0], video_key[0], video_value[0]))
    gathered_query = lax.all_gather(audio_query[0], "seq", axis=0, tiled=True)
    gathered_key = lax.all_gather(audio_key[0], "seq", axis=0, tiled=True)
    gathered_value = lax.all_gather(audio_value[0], "seq", axis=0, tiled=True)
    heard_list.append(attend(cross_query[0], gathered_key, gathered_value, cross_heads))
    audio_seen = audio_listen(gathered_query, cross_key[0], cross_value[0], cross_heads)
    seen_list.append(audio_seen)
    output_list.append(audio_block(audio_input[0], audio_seen, norm_gain, up_weight, down_weight))
    return (
        jnp.stack(mixed_list),
        jnp.stack(heard_list),
        jnp.stack(seen_list),
        jnp.stack(output_list),
    )


def solution(mesh):
    placed = (
        P(("clips", "dp"), "seq", "tp"),
        P(("clips", "dp"), "seq", "tp"),
        P(("clips", "dp"), "seq", "tp"),
        P(("clips", "dp"), "seq", "tp"),
        P(("clips", "dp"), "seq", "tp"),
        P(("clips", "dp"), "seq", "tp"),
        P(("clips", "dp"), "seq", "tp"),
        P(("clips", "dp"), "seq", "tp"),
        P(("clips", "dp"), "seq", "tp"),
        P(("clips", "dp"), "seq", None),
        P(),
        P("tp", "seq"),
        P("seq", "tp"),
    )
    return jax.shard_map(
        body,
        mesh=mesh,
        in_specs=placed,
        out_specs=(
            P(("clips", "dp"), "seq", "tp"),
            P(("clips", "dp"), "seq", "tp"),
            P(("clips", "dp"), "seq", "tp"),
            P(("clips", "dp"), "seq", "tp"),
        ),
        check_vma=False,
    )
```

```python
import functools
import math

import jax
import jax.numpy as jnp
from jax import lax
from jax.experimental import pallas as pl
from jax.experimental.pallas import tpu as pltpu
from jax.sharding import PartitionSpec as P

VHEAD = 128
CHEAD = 64
MESH = pl.DeviceIdType.MESH
LOG2E = math.log2(math.e)
CHUNKS = 4
EARLY = 3
PACE = ((1, 1, 1, 2, 1, 2, 1, 0), (0, 2, 1, 0, 1, 1, 2, 2))
ORDER = (2, 0, 1)
LATE = 1
RIGHT = True
TURNS = (0, 0, 0, 0, 1, 0)


def dot_t(a, b):
    return lax.dot_general(a, b, (((1,), (1,)), ((), ())), preferred_element_type=jnp.float32)


def softmax_parts(q, k, scale):
    s = dot_t(q, k)
    peak = jnp.max(s, axis=1, keepdims=True)
    p = jnp.exp2((s - peak) * (scale * LOG2E))
    return p, peak * scale, jnp.sum(p, axis=1, keepdims=True)


def pair_attend(q, k, v, scale):
    low = lax.broadcasted_iota(jnp.int32, q.shape, 1) < CHEAD
    zero = jnp.zeros_like(q)
    both = jnp.concatenate([jnp.where(low, q, zero), jnp.where(low, zero, q)], axis=0)
    p, peak, total = softmax_parts(both, k, scale)
    o = jnp.dot(p.astype(jnp.bfloat16), v, preferred_element_type=jnp.float32)
    return o, peak, total


def partners(me, n):
    if n & (n - 1):
        return [lax.rem(me + d, n) for d in range(1, n)]
    found = []
    for flip in range(n - 1, 0, -1):
        place, bit = me * 0, 1
        while bit < n:
            digit = lax.rem(lax.div(me, bit), 2)
            place = place + bit * ((1 - digit) if flip & bit else digit)
            bit *= 2
        found.append(place)
    return found


def fused_kernel(
    n, tp,
    vq, vk, vv, cq, ak, av, aq, ck, cv, ai, gain, up, down,
    mixed, heard, seen, mlp,
    vbuf, obuf, abuf, cqv, ckv, cvv, upv, downv, aiv, gainv, xown, xsend, xrecv, tsend, trecv, ssbuf, nbuf, pbuf, ubuf, racc, rsend, rrecv,
    v_send, v_recv, o_send, o_recv, a_send, a_recv, x_send, x_recv, t_send, t_recv, s_send, s_recv,
    n_send, n_recv, p_send, p_recv, r_send, r_recv, own_sem, load_sem, ready,
):
    me = lax.axis_index("seq")
    col = lax.axis_index("tp")
    core = lax.rem(lax.axis_index("dp"), 2)
    tokens = vq.shape[0]
    hd = vq.shape[1] // VHEAD // n
    rows, width = aq.shape
    pairs = width // 128
    units = up.shape[1]
    step = units // CHUNKS
    f32, bf16 = jnp.float32, jnp.bfloat16
    peers = partners(me, n)
    tp_peers = [lax.rem(col + d, tp) for d in range(1, tp)]

    def remote(src, dst, ss, rs, where):
        copy = pltpu.make_async_remote_copy(
            src_ref=src, dst_ref=dst, send_sem=ss, recv_sem=rs, device_id=where, device_id_type=MESH
        )
        copy.start()
        return copy

    far, over, side = peers
    inner = lax.rem(lax.div(me + 1, 2), 2) == 1
    outer = jnp.logical_not(inner)
    streams = (vq, vk, vv)
    order = ORDER
    cross = inner
    if RIGHT:
        cross = jnp.logical_xor(inner, me < n // 2)
    back = (jnp.where(cross, over, far), jnp.where(cross, far, over), side, me)
    units = [(h, i) for h in range(hd) for i in (1, 2, 0)]

    def unit(h, i, d):
        cols = pl.ds(pl.multiple_of((peers[d] * hd + h) * VHEAD, VHEAD), VHEAD)
        return pltpu.make_async_remote_copy(
            src_ref=streams[i].at[:, cols], dst_ref=vbuf.at[i, h, me], send_sem=v_send, recv_sem=v_recv.at[h],
            device_id={"seq": peers[d]}, device_id_type=MESH,
        )

    def landed(ref, sem):
        pltpu.make_async_copy(ref, ref, sem).wait()

    marks = [EARLY, EARLY]

    def pump(w):
        ends = [min(marks[c] + PACE[c][w], len(units)) if w < len(PACE[c]) else len(units) for c in range(2)]
        for k, (h, i) in enumerate(units):
            mine = [marks[c] <= k < ends[c] for c in range(2)]

            def go():
                for d in order:
                    unit(h, i, d).start()

            if all(mine):
                go()
            elif any(mine):
                pl.when(core == mine.index(True))(go)
        marks[:] = ends

    def tell(where, k):
        pl.semaphore_signal(ready.at[k], inc=1, device_id=where, device_id_type=MESH)

    hub = me == n // 2 - 1
    barrier = pltpu.get_barrier_semaphore()
    early = units[:EARLY]

    @pl.when(inner)
    def _():
        for p in (far, side):
            pl.semaphore_signal(barrier, inc=1, device_id={"seq": p}, device_id_type=MESH)

    @pl.when(hub)
    def _():
        for t in tp_peers:
            pl.semaphore_signal(barrier, inc=1, device_id={"tp": t}, device_id_type=MESH)

    pl.semaphore_wait(barrier, jnp.where(hub, tp, 1))

    @pl.when(inner)
    def _():
        for h, i in early:
            unit(h, i, 0).start()

    @pl.when(outer)
    def _():
        tell({"seq": side}, 0)
        for h, i in early:
            unit(h, i, 2).start()

    loads = []
    stays = ((ck, ckv), (cv, cvv), (cq, cqv), (up, upv), (down, downv), (ai, aiv), (gain, gainv))
    stays += tuple((src, abuf.at[i, me]) for i, src in enumerate((aq, ak, av)))
    for i, (src, dst) in enumerate(stays):
        loads.append(pltpu.make_async_copy(src, dst, load_sem.at[i]))

    for i in (0, 1, 7):
        loads[i].start()

    @pl.when(inner)
    def _():
        pl.semaphore_wait(ready.at[0], 1)
        tell({"seq": far}, 1)
        pl.semaphore_wait(ready.at[1], 1)
        tell({"seq": side}, 2)

    @pl.when(hub)
    def _():
        for t in tp_peers:
            tell({"tp": t}, 3)

    @pl.when(outer)
    def _():
        pl.semaphore_wait(ready.at[2], 1)

    kept = []

    def give(h, p, cols):
        remote(obuf.at[h, p], mixed.at[:, cols], o_send, o_recv, {"seq": p})

    def attend_video(h):
        if h == 0:
            landed(vbuf.at[:, :, 0], own_sem)
        landed(vbuf.at[:, h, : n - 1], v_recv.at[h])
        k = vbuf[1, h].reshape(n * tokens, VHEAD)
        v = vbuf[2, h].reshape(n * tokens, VHEAD)
        cols = pl.ds(pl.multiple_of((me * hd + h) * VHEAD, VHEAD), VHEAD)
        for i, p in enumerate(back):
            w, _, total = softmax_parts(vbuf[0, h, p], k, 1.0 / math.sqrt(VHEAD))
            o = jnp.dot(w.astype(bf16), v, preferred_element_type=f32) / total
            if i < n - 1:
                obuf[h, p] = o.astype(bf16)
            else:
                mixed[:, cols] = o.astype(bf16)
            if i == 1 and LATE <= h < hd - 1:
                kept.append((h, p, cols))
            elif i < n - 1:
                give(h, p, cols)
            if i == 0 and h == hd - 1:
                for later in kept:
                    give(*later)

    heads = list(range(hd))

    def attend_next(count):
        for h in heads[:count]:
            attend_video(h)
        del heads[:count]

    def spread(src, slots, ss, rs):
        for d, r in ((2, rs[1]), (1, rs[0])):
            remote(src, slots.at[me], ss, r, {"seq": peers[d]})

    def hand_on(slots, ss, rs):
        remote(slots.at[over], slots.at[over], ss, rs[1], {"seq": side})

    a_recvs = [(a_recv.at[0], a_recv.at[1]), (a_recv.at[2], a_recv.at[3])]
    n_recvs = (n_recv.at[0], n_recv.at[1])
    spread(aq, abuf.at[0], a_send, a_recvs[0])
    for h, i in early:

        @pl.when(inner)
        def _():
            unit(h, i, 2).start()

        @pl.when(outer)
        def _():
            unit(h, i, 0).start()

        unit(h, i, 1).start()
    for h in range(hd):
        cols = pl.ds(pl.multiple_of((me * hd + h) * VHEAD, VHEAD), VHEAD)
        for i, src in enumerate(streams):
            pltpu.make_async_copy(src.at[:, cols], vbuf.at[i, h, me], own_sem).start()
    for copy in loads[2:7] + loads[8:]:
        copy.start()
    pump(0)
    landed(abuf.at[0, 0], a_recvs[0][0])
    hand_on(abuf.at[0], a_send, a_recvs[0])
    pump(1)

    @pl.when(hub)
    def _():
        pl.semaphore_wait(ready.at[3], tp - 1)
        for p in peers:
            tell({"seq": p}, 4)

    for copy in loads[:2] + loads[5:]:
        copy.wait()
    landed(abuf.at[0, : n - 2], a_recvs[0][1])

    def whole(i):
        return jnp.concatenate([abuf[i, s].astype(f32) for s in range(n)], axis=0).astype(bf16)

    scale = 1.0 / math.sqrt(CHEAD)
    total_rows = n * rows
    q_all = whole(0)
    lane = lax.broadcasted_iota(jnp.int32, (total_rows, 128), 1)
    stats = jnp.ones((total_rows, 128), f32)
    for j in range(pairs):
        at = slice(j * 128, (j + 1) * 128)
        o, peak, total = pair_attend(q_all[:, at], ckv[:, at], cvv[:, at], scale)
        picked = jnp.where(lane < CHEAD, o[:total_rows], o[total_rows:])
        xown[:, :, at] = picked.reshape(n, rows, 128)
        for half in range(2):
            part = slice(half * total_rows, (half + 1) * total_rows)
            stats = jnp.where(lane == 2 * j + half, peak[part], stats)
            stats = jnp.where(lane == 64 + 2 * j + half, total[part], stats)
    tsend[...] = stats.reshape(n, rows, 128)

    def send_part(d, slot, k):
        r, where = min(k, 1), {"seq": peers[d]}
        remote(tsend.at[slot], trecv.at[k], t_send, t_recv.at[r], where)
        remote(xsend.at[k], xrecv.at[k], x_send, x_recv.at[r], where)

    xsend[0] = xown[far].astype(bf16)
    send_part(2, far, 0)
    xsend[1] = xown[side].astype(bf16)
    send_part(2, side, 1)
    place = lax.broadcasted_iota(jnp.int32, (rows, 128), 1)

    def weigh(stats):
        peak = functools.reduce(jnp.maximum, stats)
        factors = [jnp.exp(t - peak) for t in stats]
        return peak, factors, sum(f * pltpu.roll(t, 64, 1) for f, t in zip(factors, stats))

    def blend(factors, blocks):
        pieces = []
        for j in range(pairs):
            at = slice(j * 128, (j + 1) * 128)
            terms = [
                jnp.where(place < CHEAD, f[:, 2 * j : 2 * j + 1], f[:, 2 * j + 1 : 2 * j + 2]) * b[:, at].astype(f32)
                for f, b in zip(factors, blocks)
            ]
            pieces.append(sum(terms[1:], terms[0]))
        return jnp.concatenate(pieces, axis=1).astype(bf16)

    pump(2)

    landed(trecv.at[0], t_recv.at[0])
    landed(xrecv.at[0], x_recv.at[0])
    peak, factors, total = weigh([tsend[over], trecv[0]])
    xsend[2] = blend(factors, [xown[over], xrecv[0]])
    tsend[over] = jnp.where(place < 64, peak, pltpu.roll(total, 64, 1))
    send_part(1, over, 2)

    pump(3)
    attend_next(TURNS[0])

    landed(trecv.at[1:], t_recv.at[1])
    landed(xrecv.at[1:], x_recv.at[1])
    _, factors, total = weigh([tsend[me], trecv[1], trecv[2]])
    seen_bf = blend([f / total for f in factors], [xown[me], xrecv[1], xrecv[2]])
    seen[...] = seen_bf

    mine = pl.ds(pl.multiple_of(col * width, 128), width)
    residual = aiv[:, mine].astype(f32) + seen_bf.astype(f32)
    square = jnp.sum(residual * residual, axis=1, keepdims=True)
    first = square.astype(bf16).astype(f32)
    second = (square - first).astype(bf16).astype(f32)
    third = square - first - second
    split = jnp.where(place == 0, first, jnp.where(place == 1, second, jnp.where(place == 2, third, 0.0)))
    nbuf[me, :, :width] = (residual * gainv[:, mine]).astype(bf16)
    nbuf[me, :, width:] = split.astype(bf16)
    spread(nbuf.at[me], nbuf, n_send, n_recvs)
    for i, src in enumerate((ak, av)):
        spread(src, abuf.at[i + 1], a_send, a_recvs[1])
    pump(4)
    attend_next(TURNS[1])
    landed(nbuf.at[0], n_recvs[0])
    hand_on(nbuf, n_send, n_recvs)
    pump(5)
    attend_next(TURNS[2])

    loads[3].wait()
    landed(nbuf.at[: n - 2], n_recvs[1])
    held = jnp.concatenate([nbuf[s].astype(f32) for s in range(n)], axis=0)
    x = held[:, :width].astype(bf16)
    square = jnp.sum(held[:, width:], axis=1, keepdims=True)
    ssbuf[col] = jnp.broadcast_to(square, (total_rows, 128))
    partials = []

    @pl.when(jnp.logical_not(hub))
    def _():
        pl.semaphore_wait(ready.at[4], 1)

    for d, t in enumerate(tp_peers):
        partials.append(remote(ssbuf.at[col], ssbuf.at[col], s_send.at[d], s_recv.at[d], {"tp": t}))
    for c in range(CHUNKS):
        ubuf[c] = jnp.dot(x, upv[:, c * step : (c + 1) * step], preferred_element_type=f32)
        pbuf[col, c] = ubuf[c].astype(bf16)
        for d, t in enumerate(tp_peers):
            partials.append(
                remote(pbuf.at[col, c], pbuf.at[col, c], p_send, p_recv.at[c, d], {"tp": t})
            )
    landed(abuf.at[1:, 0], a_recvs[1][0])
    for i in (1, 2):
        hand_on(abuf.at[i], a_send, a_recvs[1])
    pump(6)
    attend_next(TURNS[3])

    loads[4].wait()
    for copy in partials[: tp - 1]:
        copy.wait_recv()
    square = sum(ssbuf[t] for t in range(tp))[:, 0:1]
    factor = lax.rsqrt(square / (width * tp) + 1e-6)
    acc = jnp.zeros((total_rows, width), f32)
    for c in range(CHUNKS):
        for copy in partials[(c + 1) * (tp - 1) : (c + 2) * (tp - 1)]:
            copy.wait_recv()
        up_sum = (ubuf[c] + sum(pbuf[t, c].astype(f32) for t in tp_peers)) * factor
        hidden = jax.nn.gelu(up_sum, approximate=True).astype(bf16)
        acc += jnp.dot(hidden, downv[c * step : (c + 1) * step, :], preferred_element_type=f32)
    racc[...] = acc.reshape(n, rows, width)

    def send_sum(d, k):
        remote(rsend.at[k], rrecv.at[k], r_send, r_recv.at[min(k, 1)], {"seq": peers[d]})

    rsend[0] = racc[far].astype(bf16)
    send_sum(2, 0)
    rsend[1] = racc[side].astype(bf16)
    send_sum(2, 1)
    pump(7)

    attend_next(TURNS[4])
    landed(rrecv.at[0], r_recv.at[0])
    rsend[2] = (racc[over] + rrecv[0].astype(f32)).astype(bf16)
    send_sum(1, 2)
    pump(8)
    attend_next(TURNS[5])

    loads[2].wait()
    landed(abuf.at[1:, : n - 2], a_recvs[1][1])
    k_all, v_all = whole(1), whole(2)
    wide = lax.broadcasted_iota(jnp.int32, (tokens, 128), 1)
    for j in range(pairs):
        at = slice(j * 128, (j + 1) * 128)
        o, _, total = pair_attend(cqv[:, at], k_all[:, at], v_all[:, at], scale)
        o = o / total
        heard[:, at] = jnp.where(wide < CHEAD, o[:tokens], o[tokens:]).astype(bf16)

    attend_next(len(heads) - 1)

    landed(rrecv.at[1:], r_recv.at[1])
    mlp[...] = (racc[me] + rrecv[1].astype(f32) + rrecv[2].astype(f32)).astype(bf16)

    attend_next(len(heads))

    for ref, sem in (
        (vbuf.at[:, :, : n - 1], v_send),
        (abuf.at[:, : n - 1], a_send),
        (xsend, x_send),
        (trecv, t_send),
        (nbuf.at[: n - 1], n_send),
        (rsend, r_send),
    ):
        landed(ref, sem)
    if tp > 1:
        landed(pbuf.at[: tp - 1], p_send)
    for copy in partials[: tp - 1]:
        copy.wait_send()
    landed(obuf.at[:, : n - 1], o_send)
    landed(mixed.at[:, : (n - 1) * hd * VHEAD], o_recv)


def fused(n, tp, args):
    vq, vk, vv, cq, ak, av, aq, ck, cv, ai, gain, up, down = args
    tokens, vwidth = vq.shape
    hd = vwidth // VHEAD // n
    rows, width = aq.shape
    units = up.shape[1]
    bf16, f32 = jnp.bfloat16, jnp.float32
    anywhere = pl.BlockSpec(memory_space=pl.ANY)
    dma = pltpu.SemaphoreType.DMA
    head = pltpu.VMEM((hd, n, tokens, VHEAD), bf16)
    cross = pltpu.VMEM((tokens, width), bf16)
    one, t = dma, max(tp - 1, 1)
    return pl.pallas_call(
        functools.partial(fused_kernel, n, tp),
        out_shape=(
            pltpu.VMEM((tokens, vwidth), bf16),
            pltpu.VMEM((tokens, width), bf16),
            pltpu.VMEM((rows, width), bf16),
            pltpu.VMEM((rows, width), bf16),
        ),
        in_specs=[anywhere] * 13,
        out_specs=(pl.BlockSpec(memory_space=pltpu.VMEM),) * 4,
        scratch_shapes=[
            pltpu.VMEM((3, hd, n, tokens, VHEAD), bf16), head,
            pltpu.VMEM((3, n, rows, width), bf16),
            cross, cross, cross,
            pltpu.VMEM(up.shape, bf16),
            pltpu.VMEM(down.shape, bf16),
            pltpu.VMEM(ai.shape, bf16),
            pltpu.VMEM((1, gain.shape[0]), f32),
            pltpu.VMEM((n, rows, width), f32),
            pltpu.VMEM((3, rows, width), bf16),
            pltpu.VMEM((3, rows, width), bf16),
            pltpu.VMEM((n, rows, 128), f32),
            pltpu.VMEM((3, rows, 128), f32),
            pltpu.VMEM((tp, n * rows, 128), f32),
            pltpu.VMEM((n, rows, width + 128), bf16),
            pltpu.VMEM((tp, CHUNKS, n * rows, units // CHUNKS), bf16),
            pltpu.VMEM((CHUNKS, n * rows, units // CHUNKS), f32),
            pltpu.VMEM((n, rows, width), f32),
            pltpu.VMEM((3, rows, width), bf16),
            pltpu.VMEM((3, rows, width), bf16),
            one, dma((hd,)), one, one, one, dma((4,)), one, dma((2,)), one, dma((2,)), dma((t,)), dma((t,)),
            one, dma((2,)), one, dma((CHUNKS, t)), one, dma((2,)),
            one, dma((10,)), pltpu.SemaphoreType.REGULAR((5,)),
        ],
        compiler_params=pltpu.CompilerParams(collective_id=0, has_side_effects=True),
    )(vq, vk, vv, cq, ak, av, aq, ck, cv, ai, gain.reshape(1, -1), up, down)


def hand_over(*refs):
    count = (len(refs) - 1) // 2
    copies = [pltpu.make_async_copy(refs[i], refs[count + i], refs[-1].at[i]) for i in range(count)]
    for copy in copies:
        copy.start()
    for copy in copies:
        copy.wait()


def deliver(arrays):
    arrays = [pltpu.with_memory_space_constraint(a, pltpu.VMEM) for a in arrays]
    return pl.pallas_call(
        hand_over,
        out_shape=tuple(jax.ShapeDtypeStruct(a.shape, a.dtype) for a in arrays),
        in_specs=[pl.BlockSpec(memory_space=pltpu.VMEM)] * len(arrays),
        out_specs=(pl.BlockSpec(memory_space=pl.ANY),) * len(arrays),
        scratch_shapes=[pltpu.SemaphoreType.DMA((len(arrays),))],
    )(*arrays)


def fits(n, vq, aq, up):
    heads = vq.shape[2] // VHEAD
    return (
        n == 4
        and heads % n == 0
        and vq.shape[1] % 16 == 0
        and aq.shape[1] % 8 == 0
        and aq.shape[2] % 128 == 0
        and aq.shape[2] // CHEAD <= 64
        and up.shape[0] == aq.shape[2]
        and up.shape[1] % (128 * CHUNKS) == 0
    )


def attend_rows(queries, keys_in, values_in, head_count):
    head_size = queries.shape[1] // head_count
    query_heads = queries.reshape(queries.shape[0], head_count, head_size)
    key_heads = keys_in.reshape(keys_in.shape[0], head_count, head_size)
    value_heads = values_in.reshape(values_in.shape[0], head_count, head_size)
    scores = jnp.einsum(
        "qhd,khd->qhk", query_heads, key_heads, preferred_element_type=jnp.float32
    ) / math.sqrt(head_size)
    peak_value = jnp.max(scores, axis=2, keepdims=True)
    weights = jnp.exp(scores - peak_value)
    totals = jnp.sum(weights, axis=2)
    weighted = jnp.einsum(
        "qhk,khd->qhd",
        weights.astype(jnp.bfloat16),
        value_heads,
        preferred_element_type=jnp.float32,
    )
    result = weighted / totals[:, :, None]
    return result.reshape(queries.shape[0], head_count * head_size).astype(jnp.bfloat16)


def attend(queries, keys_in, values_in, head_count):
    row_total = queries.shape[0]
    block_rows = 512 if row_total % 512 == 0 else row_total
    pieces = queries.reshape(row_total // block_rows, block_rows, queries.shape[1])
    result = lax.map(
        lambda row_piece: attend_rows(row_piece, keys_in, values_in, head_count), pieces
    )
    return result.reshape(row_total, queries.shape[1])


def video_self(queries, keys_in, values_in):
    seq_count = lax.axis_size("seq")
    local_heads = queries.shape[1] // VHEAD
    dest_heads = max(local_heads // seq_count, 1)
    blocks = seq_count * dest_heads // local_heads
    groups = local_heads // dest_heads
    group_width = dest_heads * VHEAD
    token_count = queries.shape[0]
    block_tokens = token_count // blocks

    def spread(tensor):
        shaped = tensor.reshape(token_count, groups, group_width).transpose(1, 0, 2)
        shaped = jnp.broadcast_to(shaped[:, None], (groups, blocks, token_count, group_width))
        return shaped.reshape(seq_count, token_count, group_width)

    shaped = queries.reshape(blocks, block_tokens, groups, group_width).transpose(2, 0, 1, 3)
    own_queries = lax.all_to_all(
        shaped.reshape(seq_count, block_tokens, group_width),
        "seq",
        split_axis=0,
        concat_axis=0,
        tiled=True,
    )
    keys_all = lax.all_to_all(spread(keys_in), "seq", split_axis=0, concat_axis=0, tiled=True)
    values_all = lax.all_to_all(spread(values_in), "seq", split_axis=0, concat_axis=0, tiled=True)
    keys_all = keys_all.reshape(-1, group_width)
    values_all = values_all.reshape(-1, group_width)
    own_queries = own_queries.reshape(-1, group_width)
    attended = attend(own_queries, keys_all, values_all, dest_heads)
    returned = lax.all_to_all(
        attended.reshape(seq_count, block_tokens, group_width),
        "seq",
        split_axis=0,
        concat_axis=0,
        tiled=True,
    )
    returned = returned.reshape(groups, blocks, block_tokens, group_width).transpose(1, 2, 0, 3)
    return returned.reshape(token_count, groups * group_width)


def audio_listen(queries, keys_in, values_in, head_count):
    head_size = queries.shape[1] // head_count
    query_heads = queries.reshape(queries.shape[0], head_count, head_size)
    key_heads = keys_in.reshape(keys_in.shape[0], head_count, head_size)
    value_heads = values_in.reshape(values_in.shape[0], head_count, head_size)
    scores = jnp.einsum(
        "qhd,khd->qhk", query_heads, key_heads, preferred_element_type=jnp.float32
    ) / math.sqrt(head_size)
    local_peak = jnp.max(scores, axis=2)
    peak_value = lax.pmax(local_peak, "seq")
    weights = jnp.exp(scores - peak_value[:, :, None])
    totals = jnp.sum(weights, axis=2)
    weighted = jnp.einsum(
        "qhk,khd->qhd",
        weights.astype(jnp.bfloat16),
        value_heads,
        preferred_element_type=jnp.float32,
    )
    totals, weighted = (totals, weighted.reshape(queries.shape[0], head_count * head_size))
    totals, weighted = (
        lax.psum_scatter(totals, "seq", scatter_dimension=0, tiled=True),
        lax.psum_scatter(weighted, "seq", scatter_dimension=0, tiled=True),
    )
    return (weighted / jnp.repeat(totals, head_size, axis=1)).astype(jnp.bfloat16)


def audio_block(audio_rows, audio_seen, norm_gain, up_weight, down_weight):
    features = lax.all_gather(audio_seen, "tp", axis=1, tiled=True)
    residual = audio_rows.astype(jnp.float32) + features.astype(jnp.float32)
    scale_factor = lax.rsqrt(jnp.mean(residual * residual, axis=1, keepdims=True) + 1e-06)
    normed = (residual * scale_factor * norm_gain).astype(jnp.bfloat16)
    slice_width = up_weight.shape[0]
    own_features = lax.dynamic_slice_in_dim(
        normed, lax.axis_index("tp") * slice_width, slice_width, 1
    )
    partial_sum = jnp.dot(
        lax.all_gather(own_features, "seq", axis=0, tiled=True),
        up_weight,
        preferred_element_type=jnp.float32,
    )
    hidden = jax.nn.gelu(lax.psum(partial_sum, "tp")).astype(jnp.bfloat16)
    return lax.psum_scatter(
        jnp.dot(hidden, down_weight, preferred_element_type=jnp.float32),
        "seq",
        scatter_dimension=0,
        tiled=True,
    ).astype(jnp.bfloat16)


def body(
    video_query,
    video_key,
    video_value,
    cross_query,
    audio_key,
    audio_value,
    audio_query,
    cross_key,
    cross_value,
    audio_input,
    norm_gain,
    up_weight,
    down_weight,
):
    if fits(lax.axis_size("seq"), video_query, audio_query, up_weight):
        args = (video_query, video_key, video_value, cross_query, audio_key, audio_value)
        args += (audio_query, cross_key, cross_value, audio_input)
        args = tuple(a[0] for a in args) + (norm_gain, up_weight, down_weight)
        outs = deliver(fused(lax.axis_size("seq"), lax.axis_size("tp"), args))
        return tuple(out[None] for out in outs)
    mixed_list, heard_list, seen_list, output_list = ([], [], [], [])
    cross_heads = cross_query.shape[2] // CHEAD
    mixed_list.append(video_self(video_query[0], video_key[0], video_value[0]))
    gathered_query = lax.all_gather(audio_query[0], "seq", axis=0, tiled=True)
    gathered_key = lax.all_gather(audio_key[0], "seq", axis=0, tiled=True)
    gathered_value = lax.all_gather(audio_value[0], "seq", axis=0, tiled=True)
    heard_list.append(attend(cross_query[0], gathered_key, gathered_value, cross_heads))
    audio_seen = audio_listen(gathered_query, cross_key[0], cross_value[0], cross_heads)
    seen_list.append(audio_seen)
    output_list.append(audio_block(audio_input[0], audio_seen, norm_gain, up_weight, down_weight))
    return (
        jnp.stack(mixed_list),
        jnp.stack(heard_list),
        jnp.stack(seen_list),
        jnp.stack(output_list),
    )


def solution(mesh):
    placed = (
        P(("clips", "dp"), "seq", "tp"),
        P(("clips", "dp"), "seq", "tp"),
        P(("clips", "dp"), "seq", "tp"),
        P(("clips", "dp"), "seq", "tp"),
        P(("clips", "dp"), "seq", "tp"),
        P(("clips", "dp"), "seq", "tp"),
        P(("clips", "dp"), "seq", "tp"),
        P(("clips", "dp"), "seq", "tp"),
        P(("clips", "dp"), "seq", "tp"),
        P(("clips", "dp"), "seq", None),
        P(),
        P("tp", "seq"),
        P("seq", "tp"),
    )
    return jax.shard_map(
        body,
        mesh=mesh,
        in_specs=placed,
        out_specs=(
            P(("clips", "dp"), "seq", "tp"),
            P(("clips", "dp"), "seq", "tp"),
            P(("clips", "dp"), "seq", "tp"),
            P(("clips", "dp"), "seq", "tp"),
        ),
        check_vma=False,
    )
```

```python
import functools
import math

import jax
import jax.numpy as jnp
from jax import lax
from jax.experimental import pallas as pl
from jax.experimental.pallas import tpu as pltpu
from jax.sharding import PartitionSpec as P

VHEAD = 128
CHEAD = 64
MESH = pl.DeviceIdType.MESH
LOG2E = math.log2(math.e)
CHUNKS = 4
EARLY = 3
PACE = ((1, 1, 1, 2, 1, 2, 1, 0), (0, 2, 1, 0, 1, 1, 2, 2))
ORDER = (2, 0, 1)
LATE = 1
RIGHT = True
TURNS = (0, 0, 0, 0, 1, 0)


def dot_t(a, b):
    return lax.dot_general(a, b, (((1,), (1,)), ((), ())), preferred_element_type=jnp.float32)


def softmax_parts(q, k, scale):
    s = dot_t(q, k)
    peak = jnp.max(s, axis=1, keepdims=True)
    p = jnp.exp2((s - peak) * (scale * LOG2E))
    return p, peak * scale, jnp.sum(p, axis=1, keepdims=True)


def pair_attend(q, k, v, scale):
    low = lax.broadcasted_iota(jnp.int32, q.shape, 1) < CHEAD
    zero = jnp.zeros_like(q)
    both = jnp.concatenate([jnp.where(low, q, zero), jnp.where(low, zero, q)], axis=0)
    p, peak, total = softmax_parts(both, k, scale)
    o = jnp.dot(p.astype(jnp.bfloat16), v, preferred_element_type=jnp.float32)
    return o, peak, total


def partners(me, n):
    if n & (n - 1):
        return [lax.rem(me + d, n) for d in range(1, n)]
    found = []
    for flip in range(n - 1, 0, -1):
        place, bit = me * 0, 1
        while bit < n:
            digit = lax.rem(lax.div(me, bit), 2)
            place = place + bit * ((1 - digit) if flip & bit else digit)
            bit *= 2
        found.append(place)
    return found


def fused_kernel(
    n, tp,
    vq, vk, vv, cq, ak, av, aq, ck, cv, ai, gain, up, down,
    mixed, heard, seen, mlp,
    vbuf, obuf, abuf, cqv, ckv, cvv, upv, downv, aiv, gainv, xown, xsend, xrecv, tsend, trecv, ssbuf, nbuf, pbuf, ubuf, racc, rsend, rrecv,
    v_send, v_recv, o_send, o_recv, a_send, a_recv, x_send, x_recv, t_send, t_recv, s_send, s_recv,
    n_send, n_recv, p_send, p_recv, r_send, r_recv, own_sem, load_sem, ready,
):
    me = lax.axis_index("seq")
    col = lax.axis_index("tp")
    core = lax.rem(lax.axis_index("dp"), 2)
    tokens = vq.shape[0]
    hd = vq.shape[1] // VHEAD // n
    rows, width = aq.shape
    pairs = width // 128
    units = up.shape[1]
    step = units // CHUNKS
    f32, bf16 = jnp.float32, jnp.bfloat16
    peers = partners(me, n)
    tp_peers = [lax.rem(col + d, tp) for d in range(1, tp)]

    def remote(src, dst, ss, rs, where):
        copy = pltpu.make_async_remote_copy(
            src_ref=src, dst_ref=dst, send_sem=ss, recv_sem=rs, device_id=where, device_id_type=MESH
        )
        copy.start()
        return copy

    far, over, side = peers
    inner = lax.rem(lax.div(me + 1, 2), 2) == 1
    outer = jnp.logical_not(inner)
    streams = (vq, vk, vv)
    order = ORDER
    cross = inner
    if RIGHT:
        cross = jnp.logical_xor(inner, me < n // 2)
    back = (jnp.where(cross, over, far), jnp.where(cross, far, over), side, me)
    units = [(h, i) for h in range(hd) for i in (1, 2, 0)]

    def unit(h, i, d):
        cols = pl.ds(pl.multiple_of((peers[d] * hd + h) * VHEAD, VHEAD), VHEAD)
        return pltpu.make_async_remote_copy(
            src_ref=streams[i].at[:, cols], dst_ref=vbuf.at[i, h, me], send_sem=v_send, recv_sem=v_recv.at[h],
            device_id={"seq": peers[d]}, device_id_type=MESH,
        )

    def landed(ref, sem):
        pltpu.make_async_copy(ref, ref, sem).wait()

    marks = [EARLY, EARLY]

    def pump(w):
        ends = [min(marks[c] + PACE[c][w], len(units)) if w < len(PACE[c]) else len(units) for c in range(2)]
        for k, (h, i) in enumerate(units):
            mine = [marks[c] <= k < ends[c] for c in range(2)]

            def go():
                for d in order:
                    unit(h, i, d).start()

            if all(mine):
                go()
            elif any(mine):
                pl.when(core == mine.index(True))(go)
        marks[:] = ends

    def tell(where, k):
        pl.semaphore_signal(ready.at[k], inc=1, device_id=where, device_id_type=MESH)

    hub = me == n // 2 - 1
    barrier = pltpu.get_barrier_semaphore()
    early = units[:EARLY]

    @pl.when(inner)
    def _():
        for p in (far, side):
            pl.semaphore_signal(barrier, inc=1, device_id={"seq": p}, device_id_type=MESH)

    @pl.when(hub)
    def _():
        for t in tp_peers:
            pl.semaphore_signal(barrier, inc=1, device_id={"tp": t}, device_id_type=MESH)

    pl.semaphore_wait(barrier, jnp.where(hub, tp, 1))

    @pl.when(inner)
    def _():
        for h, i in early:
            unit(h, i, 0).start()

    @pl.when(outer)
    def _():
        tell({"seq": side}, 0)
        for h, i in early:
            unit(h, i, 2).start()

    loads = []
    stays = ((ck, ckv), (cv, cvv), (cq, cqv), (up, upv), (down, downv), (ai, aiv), (gain, gainv))
    stays += tuple((src, abuf.at[i, me]) for i, src in enumerate((aq, ak, av)))
    for i, (src, dst) in enumerate(stays):
        loads.append(pltpu.make_async_copy(src, dst, load_sem.at[i]))

    for i in (0, 1, 7):
        loads[i].start()

    @pl.when(inner)
    def _():
        pl.semaphore_wait(ready.at[0], 1)
        tell({"seq": far}, 1)
        pl.semaphore_wait(ready.at[1], 1)
        tell({"seq": side}, 2)

    @pl.when(hub)
    def _():
        for t in tp_peers:
            tell({"tp": t}, 3)

    @pl.when(outer)
    def _():
        pl.semaphore_wait(ready.at[2], 1)

    kept = []

    def give(h, p, cols):
        remote(obuf.at[h, p], mixed.at[:, cols], o_send, o_recv, {"seq": p})

    def attend_video(h):
        if h == 0:
            landed(vbuf.at[:, :, 0], own_sem)
        landed(vbuf.at[:, h, : n - 1], v_recv.at[h])
        k = vbuf[1, h].reshape(n * tokens, VHEAD)
        v = vbuf[2, h].reshape(n * tokens, VHEAD)
        cols = pl.ds(pl.multiple_of((me * hd + h) * VHEAD, VHEAD), VHEAD)
        for i, p in enumerate(back):
            w, _, total = softmax_parts(vbuf[0, h, p], k, 1.0 / math.sqrt(VHEAD))
            o = jnp.dot(w.astype(bf16), v, preferred_element_type=f32) / total
            if i < n - 1:
                obuf[h, p] = o.astype(bf16)
            else:
                mixed[:, cols] = o.astype(bf16)
            if i == 1 and LATE <= h < hd - 1:
                kept.append((h, p, cols))
            elif i < n - 1:
                give(h, p, cols)
            if i == 0 and h == hd - 1:
                for later in kept:
                    give(*later)

    heads = list(range(hd))

    def attend_next(count):
        for h in heads[:count]:
            attend_video(h)
        del heads[:count]

    def spread(src, slots, ss, rs):
        for d, r in ((1, rs[0]), (2, rs[1])):
            remote(src, slots.at[me], ss, r, {"seq": peers[d]})

    def hand_on(slots, ss, rs):
        remote(slots.at[over], slots.at[over], ss, rs[1], {"seq": side})

    a_recvs = [(a_recv.at[0], a_recv.at[1]), (a_recv.at[2], a_recv.at[3])]
    n_recvs = (n_recv.at[0], n_recv.at[1])
    spread(aq, abuf.at[0], a_send, a_recvs[0])
    for h, i in early:

        @pl.when(inner)
        def _():
            unit(h, i, 2).start()

        @pl.when(outer)
        def _():
            unit(h, i, 0).start()

        unit(h, i, 1).start()
    for h in range(hd):
        cols = pl.ds(pl.multiple_of((me * hd + h) * VHEAD, VHEAD), VHEAD)
        for i, src in enumerate(streams):
            pltpu.make_async_copy(src.at[:, cols], vbuf.at[i, h, me], own_sem).start()
    for copy in loads[2:7] + loads[8:]:
        copy.start()
    pump(0)
    landed(abuf.at[0, 0], a_recvs[0][0])
    hand_on(abuf.at[0], a_send, a_recvs[0])
    pump(1)

    @pl.when(hub)
    def _():
        pl.semaphore_wait(ready.at[3], tp - 1)
        for p in peers:
            tell({"seq": p}, 4)

    for copy in loads[:2] + loads[5:]:
        copy.wait()
    landed(abuf.at[0, : n - 2], a_recvs[0][1])

    def whole(i):
        return jnp.concatenate([abuf[i, s].astype(f32) for s in range(n)], axis=0).astype(bf16)

    scale = 1.0 / math.sqrt(CHEAD)
    total_rows = n * rows
    q_all = whole(0)
    lane = lax.broadcasted_iota(jnp.int32, (total_rows, 128), 1)
    stats = jnp.ones((total_rows, 128), f32)
    for j in range(pairs):
        at = slice(j * 128, (j + 1) * 128)
        o, peak, total = pair_attend(q_all[:, at], ckv[:, at], cvv[:, at], scale)
        picked = jnp.where(lane < CHEAD, o[:total_rows], o[total_rows:])
        xown[:, :, at] = picked.reshape(n, rows, 128)
        for half in range(2):
            part = slice(half * total_rows, (half + 1) * total_rows)
            stats = jnp.where(lane == 2 * j + half, peak[part], stats)
            stats = jnp.where(lane == 64 + 2 * j + half, total[part], stats)
    tsend[...] = stats.reshape(n, rows, 128)

    def send_part(d, slot, k):
        r, where = min(k, 1), {"seq": peers[d]}
        remote(tsend.at[slot], trecv.at[k], t_send, t_recv.at[r], where)
        remote(xsend.at[k], xrecv.at[k], x_send, x_recv.at[r], where)

    xsend[0] = xown[far].astype(bf16)
    send_part(2, far, 0)
    xsend[1] = xown[side].astype(bf16)
    send_part(2, side, 1)
    place = lax.broadcasted_iota(jnp.int32, (rows, 128), 1)

    def weigh(stats):
        peak = functools.reduce(jnp.maximum, stats)
        factors = [jnp.exp(t - peak) for t in stats]
        return peak, factors, sum(f * pltpu.roll(t, 64, 1) for f, t in zip(factors, stats))

    def blend(factors, blocks):
        pieces = []
        for j in range(pairs):
            at = slice(j * 128, (j + 1) * 128)
            terms = [
                jnp.where(place < CHEAD, f[:, 2 * j : 2 * j + 1], f[:, 2 * j + 1 : 2 * j + 2]) * b[:, at].astype(f32)
                for f, b in zip(factors, blocks)
            ]
            pieces.append(sum(terms[1:], terms[0]))
        return jnp.concatenate(pieces, axis=1).astype(bf16)

    pump(2)

    landed(trecv.at[0], t_recv.at[0])
    landed(xrecv.at[0], x_recv.at[0])
    peak, factors, total = weigh([tsend[over], trecv[0]])
    xsend[2] = blend(factors, [xown[over], xrecv[0]])
    tsend[over] = jnp.where(place < 64, peak, pltpu.roll(total, 64, 1))
    send_part(1, over, 2)

    pump(3)
    attend_next(TURNS[0])

    landed(trecv.at[1:], t_recv.at[1])
    landed(xrecv.at[1:], x_recv.at[1])
    _, factors, total = weigh([tsend[me], trecv[1], trecv[2]])
    seen_bf = blend([f / total for f in factors], [xown[me], xrecv[1], xrecv[2]])
    seen[...] = seen_bf

    mine = pl.ds(pl.multiple_of(col * width, 128), width)
    residual = aiv[:, mine].astype(f32) + seen_bf.astype(f32)
    square = jnp.sum(residual * residual, axis=1, keepdims=True)
    first = square.astype(bf16).astype(f32)
    second = (square - first).astype(bf16).astype(f32)
    third = square - first - second
    split = jnp.where(place == 0, first, jnp.where(place == 1, second, jnp.where(place == 2, third, 0.0)))
    nbuf[me, :, :width] = (residual * gainv[:, mine]).astype(bf16)
    nbuf[me, :, width:] = split.astype(bf16)
    spread(nbuf.at[me], nbuf, n_send, n_recvs)
    for i, src in enumerate((ak, av)):
        spread(src, abuf.at[i + 1], a_send, a_recvs[1])
    pump(4)
    attend_next(TURNS[1])
    landed(nbuf.at[0], n_recvs[0])
    hand_on(nbuf, n_send, n_recvs)
    pump(5)
    attend_next(TURNS[2])

    loads[3].wait()
    landed(nbuf.at[: n - 2], n_recvs[1])
    held = jnp.concatenate([nbuf[s].astype(f32) for s in range(n)], axis=0)
    x = held[:, :width].astype(bf16)
    square = jnp.sum(held[:, width:], axis=1, keepdims=True)
    ssbuf[col] = jnp.broadcast_to(square, (total_rows, 128))
    partials = []

    @pl.when(jnp.logical_not(hub))
    def _():
        pl.semaphore_wait(ready.at[4], 1)

    for d, t in enumerate(tp_peers):
        partials.append(remote(ssbuf.at[col], ssbuf.at[col], s_send.at[d], s_recv.at[d], {"tp": t}))
    for c in range(CHUNKS):
        ubuf[c] = jnp.dot(x, upv[:, c * step : (c + 1) * step], preferred_element_type=f32)
        pbuf[col, c] = ubuf[c].astype(bf16)
        for d, t in enumerate(tp_peers):
            partials.append(
                remote(pbuf.at[col, c], pbuf.at[col, c], p_send, p_recv.at[c, d], {"tp": t})
            )
    landed(abuf.at[1:, 0], a_recvs[1][0])
    for i in (1, 2):
        hand_on(abuf.at[i], a_send, a_recvs[1])
    pump(6)
    attend_next(TURNS[3])

    loads[4].wait()
    for copy in partials[: tp - 1]:
        copy.wait_recv()
    square = sum(ssbuf[t] for t in range(tp))[:, 0:1]
    factor = lax.rsqrt(square / (width * tp) + 1e-6)
    acc = jnp.zeros((total_rows, width), f32)
    for c in range(CHUNKS):
        for copy in partials[(c + 1) * (tp - 1) : (c + 2) * (tp - 1)]:
            copy.wait_recv()
        up_sum = (ubuf[c] + sum(pbuf[t, c].astype(f32) for t in tp_peers)) * factor
        hidden = jax.nn.gelu(up_sum, approximate=True).astype(bf16)
        acc += jnp.dot(hidden, downv[c * step : (c + 1) * step, :], preferred_element_type=f32)
    racc[...] = acc.reshape(n, rows, width)

    def send_sum(d, k):
        remote(rsend.at[k], rrecv.at[k], r_send, r_recv.at[min(k, 1)], {"seq": peers[d]})

    rsend[0] = racc[far].astype(bf16)
    send_sum(2, 0)
    rsend[1] = racc[side].astype(bf16)
    send_sum(2, 1)
    pump(7)

    attend_next(TURNS[4])
    landed(rrecv.at[0], r_recv.at[0])
    rsend[2] = (racc[over] + rrecv[0].astype(f32)).astype(bf16)
    send_sum(1, 2)
    pump(8)
    attend_next(TURNS[5])

    loads[2].wait()
    landed(abuf.at[1:, : n - 2], a_recvs[1][1])
    k_all, v_all = whole(1), whole(2)
    wide = lax.broadcasted_iota(jnp.int32, (tokens, 128), 1)
    for j in range(pairs):
        at = slice(j * 128, (j + 1) * 128)
        o, _, total = pair_attend(cqv[:, at], k_all[:, at], v_all[:, at], scale)
        o = o / total
        heard[:, at] = jnp.where(wide < CHEAD, o[:tokens], o[tokens:]).astype(bf16)

    attend_next(len(heads) - 1)

    landed(rrecv.at[1:], r_recv.at[1])
    mlp[...] = (racc[me] + rrecv[1].astype(f32) + rrecv[2].astype(f32)).astype(bf16)

    attend_next(len(heads))

    for ref, sem in (
        (vbuf.at[:, :, : n - 1], v_send),
        (abuf.at[:, : n - 1], a_send),
        (xsend, x_send),
        (trecv, t_send),
        (nbuf.at[: n - 1], n_send),
        (rsend, r_send),
    ):
        landed(ref, sem)
    if tp > 1:
        landed(pbuf.at[: tp - 1], p_send)
    for copy in partials[: tp - 1]:
        copy.wait_send()
    landed(obuf.at[:, : n - 1], o_send)
    landed(mixed.at[:, : (n - 1) * hd * VHEAD], o_recv)


def fused(n, tp, args):
    vq, vk, vv, cq, ak, av, aq, ck, cv, ai, gain, up, down = args
    tokens, vwidth = vq.shape
    hd = vwidth // VHEAD // n
    rows, width = aq.shape
    units = up.shape[1]
    bf16, f32 = jnp.bfloat16, jnp.float32
    anywhere = pl.BlockSpec(memory_space=pl.ANY)
    dma = pltpu.SemaphoreType.DMA
    head = pltpu.VMEM((hd, n, tokens, VHEAD), bf16)
    cross = pltpu.VMEM((tokens, width), bf16)
    one, t = dma, max(tp - 1, 1)
    return pl.pallas_call(
        functools.partial(fused_kernel, n, tp),
        out_shape=(
            pltpu.VMEM((tokens, vwidth), bf16),
            pltpu.VMEM((tokens, width), bf16),
            pltpu.VMEM((rows, width), bf16),
            pltpu.VMEM((rows, width), bf16),
        ),
        in_specs=[anywhere] * 13,
        out_specs=(pl.BlockSpec(memory_space=pltpu.VMEM),) * 4,
        scratch_shapes=[
            pltpu.VMEM((3, hd, n, tokens, VHEAD), bf16), head,
            pltpu.VMEM((3, n, rows, width), bf16),
            cross, cross, cross,
            pltpu.VMEM(up.shape, bf16),
            pltpu.VMEM(down.shape, bf16),
            pltpu.VMEM(ai.shape, bf16),
            pltpu.VMEM((1, gain.shape[0]), f32),
            pltpu.VMEM((n, rows, width), f32),
            pltpu.VMEM((3, rows, width), bf16),
            pltpu.VMEM((3, rows, width), bf16),
            pltpu.VMEM((n, rows, 128), f32),
            pltpu.VMEM((3, rows, 128), f32),
            pltpu.VMEM((tp, n * rows, 128), f32),
            pltpu.VMEM((n, rows, width + 128), bf16),
            pltpu.VMEM((tp, CHUNKS, n * rows, units // CHUNKS), bf16),
            pltpu.VMEM((CHUNKS, n * rows, units // CHUNKS), f32),
            pltpu.VMEM((n, rows, width), f32),
            pltpu.VMEM((3, rows, width), bf16),
            pltpu.VMEM((3, rows, width), bf16),
            one, dma((hd,)), one, one, one, dma((4,)), one, dma((2,)), one, dma((2,)), dma((t,)), dma((t,)),
            one, dma((2,)), one, dma((CHUNKS, t)), one, dma((2,)),
            one, dma((10,)), pltpu.SemaphoreType.REGULAR((5,)),
        ],
        compiler_params=pltpu.CompilerParams(collective_id=0, has_side_effects=True),
    )(vq, vk, vv, cq, ak, av, aq, ck, cv, ai, gain.reshape(1, -1), up, down)


def hand_over(*refs):
    count = (len(refs) - 1) // 2
    copies = [pltpu.make_async_copy(refs[i], refs[count + i], refs[-1].at[i]) for i in range(count)]
    for copy in copies:
        copy.start()
    for copy in copies:
        copy.wait()


def deliver(arrays):
    arrays = [pltpu.with_memory_space_constraint(a, pltpu.VMEM) for a in arrays]
    return pl.pallas_call(
        hand_over,
        out_shape=tuple(jax.ShapeDtypeStruct(a.shape, a.dtype) for a in arrays),
        in_specs=[pl.BlockSpec(memory_space=pltpu.VMEM)] * len(arrays),
        out_specs=(pl.BlockSpec(memory_space=pl.ANY),) * len(arrays),
        scratch_shapes=[pltpu.SemaphoreType.DMA((len(arrays),))],
    )(*arrays)


def fits(n, vq, aq, up):
    heads = vq.shape[2] // VHEAD
    return (
        n == 4
        and heads % n == 0
        and vq.shape[1] % 16 == 0
        and aq.shape[1] % 8 == 0
        and aq.shape[2] % 128 == 0
        and aq.shape[2] // CHEAD <= 64
        and up.shape[0] == aq.shape[2]
        and up.shape[1] % (128 * CHUNKS) == 0
    )


def attend_rows(queries, keys_in, values_in, head_count):
    head_size = queries.shape[1] // head_count
    query_heads = queries.reshape(queries.shape[0], head_count, head_size)
    key_heads = keys_in.reshape(keys_in.shape[0], head_count, head_size)
    value_heads = values_in.reshape(values_in.shape[0], head_count, head_size)
    scores = jnp.einsum(
        "qhd,khd->qhk", query_heads, key_heads, preferred_element_type=jnp.float32
    ) / math.sqrt(head_size)
    peak_value = jnp.max(scores, axis=2, keepdims=True)
    weights = jnp.exp(scores - peak_value)
    totals = jnp.sum(weights, axis=2)
    weighted = jnp.einsum(
        "qhk,khd->qhd",
        weights.astype(jnp.bfloat16),
        value_heads,
        preferred_element_type=jnp.float32,
    )
    result = weighted / totals[:, :, None]
    return result.reshape(queries.shape[0], head_count * head_size).astype(jnp.bfloat16)


def attend(queries, keys_in, values_in, head_count):
    row_total = queries.shape[0]
    block_rows = 512 if row_total % 512 == 0 else row_total
    pieces = queries.reshape(row_total // block_rows, block_rows, queries.shape[1])
    result = lax.map(
        lambda row_piece: attend_rows(row_piece, keys_in, values_in, head_count), pieces
    )
    return result.reshape(row_total, queries.shape[1])


def video_self(queries, keys_in, values_in):
    seq_count = lax.axis_size("seq")
    local_heads = queries.shape[1] // VHEAD
    dest_heads = max(local_heads // seq_count, 1)
    blocks = seq_count * dest_heads // local_heads
    groups = local_heads // dest_heads
    group_width = dest_heads * VHEAD
    token_count = queries.shape[0]
    block_tokens = token_count // blocks

    def spread(tensor):
        shaped = tensor.reshape(token_count, groups, group_width).transpose(1, 0, 2)
        shaped = jnp.broadcast_to(shaped[:, None], (groups, blocks, token_count, group_width))
        return shaped.reshape(seq_count, token_count, group_width)

    shaped = queries.reshape(blocks, block_tokens, groups, group_width).transpose(2, 0, 1, 3)
    own_queries = lax.all_to_all(
        shaped.reshape(seq_count, block_tokens, group_width),
        "seq",
        split_axis=0,
        concat_axis=0,
        tiled=True,
    )
    keys_all = lax.all_to_all(spread(keys_in), "seq", split_axis=0, concat_axis=0, tiled=True)
    values_all = lax.all_to_all(spread(values_in), "seq", split_axis=0, concat_axis=0, tiled=True)
    keys_all = keys_all.reshape(-1, group_width)
    values_all = values_all.reshape(-1, group_width)
    own_queries = own_queries.reshape(-1, group_width)
    attended = attend(own_queries, keys_all, values_all, dest_heads)
    returned = lax.all_to_all(
        attended.reshape(seq_count, block_tokens, group_width),
        "seq",
        split_axis=0,
        concat_axis=0,
        tiled=True,
    )
    returned = returned.reshape(groups, blocks, block_tokens, group_width).transpose(1, 2, 0, 3)
    return returned.reshape(token_count, groups * group_width)


def audio_listen(queries, keys_in, values_in, head_count):
    head_size = queries.shape[1] // head_count
    query_heads = queries.reshape(queries.shape[0], head_count, head_size)
    key_heads = keys_in.reshape(keys_in.shape[0], head_count, head_size)
    value_heads = values_in.reshape(values_in.shape[0], head_count, head_size)
    scores = jnp.einsum(
        "qhd,khd->qhk", query_heads, key_heads, preferred_element_type=jnp.float32
    ) / math.sqrt(head_size)
    local_peak = jnp.max(scores, axis=2)
    peak_value = lax.pmax(local_peak, "seq")
    weights = jnp.exp(scores - peak_value[:, :, None])
    totals = jnp.sum(weights, axis=2)
    weighted = jnp.einsum(
        "qhk,khd->qhd",
        weights.astype(jnp.bfloat16),
        value_heads,
        preferred_element_type=jnp.float32,
    )
    totals, weighted = (totals, weighted.reshape(queries.shape[0], head_count * head_size))
    totals, weighted = (
        lax.psum_scatter(totals, "seq", scatter_dimension=0, tiled=True),
        lax.psum_scatter(weighted, "seq", scatter_dimension=0, tiled=True),
    )
    return (weighted / jnp.repeat(totals, head_size, axis=1)).astype(jnp.bfloat16)


def audio_block(audio_rows, audio_seen, norm_gain, up_weight, down_weight):
    features = lax.all_gather(audio_seen, "tp", axis=1, tiled=True)
    residual = audio_rows.astype(jnp.float32) + features.astype(jnp.float32)
    scale_factor = lax.rsqrt(jnp.mean(residual * residual, axis=1, keepdims=True) + 1e-06)
    normed = (residual * scale_factor * norm_gain).astype(jnp.bfloat16)
    slice_width = up_weight.shape[0]
    own_features = lax.dynamic_slice_in_dim(
        normed, lax.axis_index("tp") * slice_width, slice_width, 1
    )
    partial_sum = jnp.dot(
        lax.all_gather(own_features, "seq", axis=0, tiled=True),
        up_weight,
        preferred_element_type=jnp.float32,
    )
    hidden = jax.nn.gelu(lax.psum(partial_sum, "tp")).astype(jnp.bfloat16)
    return lax.psum_scatter(
        jnp.dot(hidden, down_weight, preferred_element_type=jnp.float32),
        "seq",
        scatter_dimension=0,
        tiled=True,
    ).astype(jnp.bfloat16)


def body(
    video_query,
    video_key,
    video_value,
    cross_query,
    audio_key,
    audio_value,
    audio_query,
    cross_key,
    cross_value,
    audio_input,
    norm_gain,
    up_weight,
    down_weight,
):
    if fits(lax.axis_size("seq"), video_query, audio_query, up_weight):
        args = (video_query, video_key, video_value, cross_query, audio_key, audio_value)
        args += (audio_query, cross_key, cross_value, audio_input)
        args = tuple(a[0] for a in args) + (norm_gain, up_weight, down_weight)
        outs = deliver(fused(lax.axis_size("seq"), lax.axis_size("tp"), args))
        return tuple(out[None] for out in outs)
    mixed_list, heard_list, seen_list, output_list = ([], [], [], [])
    cross_heads = cross_query.shape[2] // CHEAD
    mixed_list.append(video_self(video_query[0], video_key[0], video_value[0]))
    gathered_query = lax.all_gather(audio_query[0], "seq", axis=0, tiled=True)
    gathered_key = lax.all_gather(audio_key[0], "seq", axis=0, tiled=True)
    gathered_value = lax.all_gather(audio_value[0], "seq", axis=0, tiled=True)
    heard_list.append(attend(cross_query[0], gathered_key, gathered_value, cross_heads))
    audio_seen = audio_listen(gathered_query, cross_key[0], cross_value[0], cross_heads)
    seen_list.append(audio_seen)
    output_list.append(audio_block(audio_input[0], audio_seen, norm_gain, up_weight, down_weight))
    return (
        jnp.stack(mixed_list),
        jnp.stack(heard_list),
        jnp.stack(seen_list),
        jnp.stack(output_list),
    )


def solution(mesh):
    placed = (
        P(("clips", "dp"), "seq", "tp"),
        P(("clips", "dp"), "seq", "tp"),
        P(("clips", "dp"), "seq", "tp"),
        P(("clips", "dp"), "seq", "tp"),
        P(("clips", "dp"), "seq", "tp"),
        P(("clips", "dp"), "seq", "tp"),
        P(("clips", "dp"), "seq", "tp"),
        P(("clips", "dp"), "seq", "tp"),
        P(("clips", "dp"), "seq", "tp"),
        P(("clips", "dp"), "seq", None),
        P(),
        P("tp", "seq"),
        P("seq", "tp"),
    )
    return jax.shard_map(
        body,
        mesh=mesh,
        in_specs=placed,
        out_specs=(
            P(("clips", "dp"), "seq", "tp"),
            P(("clips", "dp"), "seq", "tp"),
            P(("clips", "dp"), "seq", "tp"),
            P(("clips", "dp"), "seq", "tp"),
        ),
        check_vma=False,
    )
```
